32 devices in a mesh: groups: 2 (over y), seq: 16 (over z, x, core).
Axes of the slice: x: 2, y: 2, z: 4, core: 2. Of those that a mesh axis runs over, the one named last changes fastest.
Arguments:
- readings: bfloat16 [32, 2048, 1024], P('groups', 'seq'), parts along dimension 0, may hold values from -6 to 6
- block_graph: int32 [32, 16], P('groups'), parts along dimension 0, may hold values 0 or 1
- cluster_of: int32 [32], P('groups'), parts along dimension 0, may hold values from 0 to 15, each once
- mix_weight: float32 [16, 16], replicated, may hold values from -2.4 to 2.4
- boundaries: int32 [4096], P(('groups', 'seq')), parts along dimension 0, may hold values 0 or 1
- w_channels: bfloat16 [1024, 512], replicated, may hold values from -0.1875 to 0.1875
- w_state: bfloat16 [1024, 128], replicated, may hold values from -0.01953125 to 0.01953125
- w_step: bfloat16 [1024, 8], replicated, may hold values from -0.1875 to 0.1875
- step_bias: float32 [8], replicated, may hold values from -1 to 1
- channel_fading_exponent: float32 [8], replicated
- skip_gain: float32 [8], replicated, may hold values from 0.5 to 1.5
- norm_gain: float32 [512], replicated, may hold values from 0.5 to 1.5
- w_out: bfloat16 [512, 1024], replicated, may hold values from -0.25 to 0.25
- cotangent: bfloat16 [32, 2048, 1024], P('groups', 'seq'), parts along dimension 0, may hold values from -0.032958984 to 0.032958984
Outputs:
- grad_out: float32 [1024, 1024], P('groups'), parts along dimension 0
- grad_read: float32 [2048, 64], P('groups'), parts along dimension 0
- grad_gain: float32 [1024], P('groups'), parts along dimension 0
The draws below stay inside these ranges and needn't reach their ends.
There are 2 independent parts, one for each index of `groups`. The reference program is written for one: setup_inputs(seed, part) draws one part's arguments, and reference() takes and returns one part's arrays. A program takes and returns all parts, laid end to end along the dimension named above; an argument that names none is the same for every part. Nothing has to cross between parts.
Inputs may be any that keep to these rules, and one draw needn't show every extreme that they name: `cluster_of`: each cluster holds exactly one sensor.
All inputs are finite; a program needn't handle non-finite values. No bound on the sum of `boundaries` on one device may be relied on, other than what follows from the above.
Results may differ from the reference program's by a relative error of at most 0.0079.
Values may be sent and summed in bfloat16 or wider, within the bound.
No kernel may reach another device: no remote copies, remote signals or barrier semaphores. Data moves between devices by JAX's collectives and lax.ppermute only.
A program may use at most 128 MiB of HBM per device.

```python
import math
import jax
import jax.numpy as jnp
from jax import lax

D = 1024
H = 8
HEAD_DIMENSION = 64
N = 64
S = 16
T_DEV = 128
E = 512
LENGTH = 2048
N_SEQ = 16


def draw_channel_fading_exponent(key, part):
    key_pick, key_fast, key_slow = jax.random.split(key, 3)
    fast_share = 0.5
    picked = jax.random.uniform(key_pick, (H,), jnp.float32) < fast_share
    fast_rate = jnp.exp(jax.random.uniform(key_fast, (H,), jnp.float32, math.log(1.0 / (8.0 * T_DEV)), math.log(4.0 / T_DEV)))
    slow_rate = jnp.exp(jax.random.uniform(key_slow, (H,), jnp.float32, math.log(0.25), math.log(1.2))) / LENGTH
    return jnp.log(jnp.where(picked, fast_rate, slow_rate)).astype(jnp.float32)


def with_ends(values, stream_key, smallest, high):
    place = [jax.random.randint(jax.random.fold_in(stream_key, axis), (), 0, length) for axis, length in enumerate(values.shape)]
    longest = values.shape.index(max(values.shape))
    next_to = place[:longest] + [(place[longest] + 1) % values.shape[longest]] + place[longest + 1:]
    return values.at[tuple(place)].set(smallest).at[tuple(next_to)].set(high)


def block_scale(stream_key, dims, shards, smallest, high):
    gain, own = 1.0, jax.random.fold_in(stream_key, 6)
    for position, shards_of in shards:
        heights = jnp.exp(jax.random.uniform(jax.random.fold_in(own, position), (shards_of,), jnp.float32, smallest / len(shards), high / len(shards)))
        gain = gain * jnp.repeat(heights, dims[position] // shards_of).reshape([-1 if axis == position else 1 for axis in range(len(dims))])
    return gain


def gaussian(key, dims, deviation, reach, shards=(), kind=jnp.bfloat16):
    gain = block_scale(key, dims, shards, -0.22, 0.18) if shards else 1.0
    array = jax.random.normal(key, dims, jnp.float32) * deviation * gain
    return jnp.minimum(jnp.maximum(array, -reach), reach).astype(kind)


def setup_inputs(seed: int = 0, part: int = 0) -> dict:
    key_list = jax.random.split(jax.random.key(seed), 15)
    part_splits = jax.random.split(jax.random.fold_in(key_list[14], part), 15)
    readings = gaussian(part_splits[0], (S, LENGTH, D), 1.0, 6.0, ((1, 16),))
    block_graph = with_ends((jax.random.randint(part_splits[1], (S, S), 0, 4) < 1).astype(jnp.int32), jax.random.fold_in(part_splits[1], 1), 0, 1)
    cluster_of = jax.random.permutation(part_splits[2], S).astype(jnp.int32)
    mix_weight = gaussian(key_list[3], (S, S), 0.4, 2.4, (), jnp.float32)
    boundaries = with_ends((jax.random.randint(part_splits[4], (LENGTH,), 0, LENGTH) < 3).astype(jnp.int32), jax.random.fold_in(part_splits[4], 1), 0, 1)
    w_channels = gaussian(key_list[5], (D, E), D ** -0.5, 0.1875)
    w_state = gaussian(key_list[6], (D, 2 * N), (100 * D) ** -0.5, 0.01953125)
    w_step = gaussian(key_list[7], (D, H), D ** -0.5, 0.1875)
    step_bias = jnp.clip(jax.random.uniform(key_list[8], (H,), jnp.float32, -1.0, 1.0), -1.0, 1.0)
    channel_fading_exponent = draw_channel_fading_exponent(jax.random.fold_in(key_list[14], 71), part)
    skip_gain = jnp.clip(jax.random.uniform(key_list[10], (H,), jnp.float32, 0.5, 1.5), 0.5, 1.5)
    norm_gain = jnp.clip(jax.random.uniform(key_list[11], (E,), jnp.float32, 0.5, 1.5), 0.5, 1.5)
    w_out = gaussian(key_list[12], (E, D), E ** -0.5, 0.25)
    cotangent = gaussian(part_splits[13], (S, LENGTH, D), (1.0 / (S * LENGTH) ** 0.5), 0.032958984, ((1, 16),))
    return {"readings": readings, "block_graph": block_graph, "cluster_of": cluster_of, "mix_weight": mix_weight, "boundaries": boundaries, "w_channels": w_channels, "w_state": w_state, "w_step": w_step, "step_bias": step_bias, "channel_fading_exponent": channel_fading_exponent, "skip_gain": skip_gain, "norm_gain": norm_gain, "w_out": w_out, "cotangent": cotangent}


HIGHEST_PREC = lax.Precision.HIGHEST
surviving_pulse_multiplier = math.log(0.7)

def mix_block(block_data, coupling):
    sensors = block_data.shape[0]
    flat_data = block_data.reshape(sensors, -1)
    spread_factor = jnp.dot(coupling, flat_data, preferred_element_type=jnp.float32)
    mixed_data = (flat_data.astype(jnp.float32) + spread_factor).astype(jnp.bfloat16)
    return mixed_data.reshape(-1, block_data.shape[2])

def mapped_matrix_lines(mixed_rows, w_channels, w_state, w_step, step_bias):
    channels = jnp.dot(mixed_rows, w_channels, preferred_element_type=jnp.float32).astype(jnp.bfloat16)
    state_maps = jnp.dot(mixed_rows, w_state, preferred_element_type=jnp.float32).astype(jnp.bfloat16)
    step_raw = (jnp.dot(mixed_rows, w_step, preferred_element_type=jnp.float32) + step_bias).astype(jnp.bfloat16)
    return (channels, state_maps, step_raw)

def decay_terms(step_raw, interval_start_markers, channel_fading_exponent):
    increment_size_per_tick = jax.nn.softplus(step_raw.astype(jnp.float32))
    natural_fading_exponent = -jnp.exp(channel_fading_exponent) * increment_size_per_tick + surviving_pulse_multiplier * interval_start_markers
    return (increment_size_per_tick, natural_fading_exponent)

def block_decays(natural_fading_exponent):
    cumulative = jnp.cumsum(natural_fading_exponent, axis=1)
    span = natural_fading_exponent.shape[1]
    later = jnp.arange(span)[:, None] >= jnp.arange(span)[None, :]
    lower = later[None, :, :, None]
    gap = cumulative[:, :, None, :] - cumulative[:, None, :, :]
    decays = jnp.where(lower, jnp.exp(jnp.where(lower, gap, 0.0)), 0.0)
    return (cumulative, decays)

def block_summary(scaled_in, writes, cumulative):
    tail = jnp.exp(cumulative[:, -1:, :] - cumulative)
    local_state = jnp.einsum('bsh,bshp,bsn->bhpn', tail, scaled_in, writes.astype(jnp.float32), precision=HIGHEST_PREC)
    return (jnp.exp(cumulative[:, -1, :]), local_state)

def block_output(channels, scaled_in, writes, reads, cumulative, decays, state_in, skip_gain):
    read_f = reads.astype(jnp.float32)
    write_f = writes.astype(jnp.float32)
    scores = jnp.einsum('btn,bsn->bts', read_f, write_f, precision=HIGHEST_PREC)
    within = jnp.einsum('bts,btsh,bshp->bthp', scores, decays, scaled_in, precision=HIGHEST_PREC)
    carried = jnp.einsum('btn,bhpn->bthp', read_f, state_in, precision=HIGHEST_PREC) * jnp.exp(cumulative)[..., None]
    return within + carried + skip_gain[:, None] * channels.astype(jnp.float32)

def block_read_grad(ssd_grad, scaled_in, writes, cumulative, decays, state_in):
    carried = jnp.einsum('bthp,bhpn->btn', ssd_grad * jnp.exp(cumulative)[..., None], state_in, precision=HIGHEST_PREC)
    pair_sums = jnp.einsum('bthp,bshp,btsh->bts', ssd_grad, scaled_in, decays, precision=HIGHEST_PREC)
    within = jnp.einsum('bts,bsn->btn', pair_sums, writes.astype(jnp.float32), precision=HIGHEST_PREC)
    return (carried + within).astype(jnp.bfloat16)

def norm_forward(ssd_out, gain_vec):
    inv_rms = lax.rsqrt(lax.optimization_barrier(jnp.mean(ssd_out * ssd_out, axis=-1, keepdims=True)) + 1e-05)
    normed = ssd_out * inv_rms
    return (normed, inv_rms, (normed * gain_vec).astype(jnp.bfloat16))

def norm_backward(normed_grad, normed, inv_rms, gain_vec):
    scaled_grad = normed_grad * gain_vec
    return inv_rms * (scaled_grad - normed * lax.optimization_barrier(jnp.mean(scaled_grad * normed, axis=-1, keepdims=True)))

def reference(readings, block_graph, cluster_of, mix_weight, boundaries, w_channels, w_state, w_step, step_bias, channel_fading_exponent, skip_gain, norm_gain, w_out, cotangent):
    linked = block_graph[cluster_of][:, cluster_of].astype(jnp.float32)
    coupling = (linked * mix_weight).astype(jnp.bfloat16)
    rows_now = S * T_DEV

    def advance(carry_now, block_index):
        state_now, grad_out, grad_read, grad_gain = carry_now
        offset = block_index * T_DEV
        block_data = lax.dynamic_slice_in_dim(readings, offset, T_DEV, 1)
        cot_rows = lax.dynamic_slice_in_dim(cotangent, offset, T_DEV, 1).reshape(rows_now, D)
        interval_start_markers = lax.dynamic_slice_in_dim(boundaries, offset, T_DEV, 0).astype(jnp.float32)[None, :, None]
        mixed_rows = mix_block(block_data, coupling)
        channels, state_maps, step_raw = mapped_matrix_lines(mixed_rows, w_channels, w_state, w_step, step_bias)
        chan_four = channels.reshape(S, T_DEV, H, HEAD_DIMENSION)
        writes = state_maps[:, :N].reshape(S, T_DEV, N)
        reads = state_maps[:, N:].reshape(S, T_DEV, N)
        increment_size_per_tick, natural_fading_exponent = decay_terms(step_raw.reshape(S, T_DEV, H), interval_start_markers, channel_fading_exponent)
        cumulative, decays = block_decays(natural_fading_exponent)
        scaled_in = chan_four.astype(jnp.float32) * increment_size_per_tick[..., None]
        running_sums, local_state = block_summary(scaled_in, writes, cumulative)
        ssd_out = block_output(chan_four, scaled_in, writes, reads, cumulative, decays, state_now, skip_gain).reshape(rows_now, E)
        normed, inv_rms, normed_out = norm_forward(ssd_out, norm_gain)
        grad_out = grad_out + lax.dot_general(normed_out, cot_rows, (((0,), (0,)), ((), ())), preferred_element_type=jnp.float32)
        normed_grad = lax.dot_general(cot_rows, w_out, (((1,), (1,)), ((), ())), preferred_element_type=jnp.float32)
        grad_gain = grad_gain + lax.optimization_barrier(jnp.sum(normed * normed_grad, axis=0))
        ssd_grad = norm_backward(normed_grad, normed, inv_rms, norm_gain).reshape(S, T_DEV, H, HEAD_DIMENSION)
        read_grad = block_read_grad(ssd_grad, scaled_in, writes, cumulative, decays, state_now).reshape(rows_now, N)
        grad_read = grad_read + lax.dot_general(mixed_rows, read_grad, (((0,), (0,)), ((), ())), preferred_element_type=jnp.float32)
        state_next = running_sums[..., None, None] * state_now + local_state
        return ((state_next, grad_out, grad_read, grad_gain), None)
    start_carry = (jnp.zeros((S, H, HEAD_DIMENSION, N), jnp.float32), jnp.zeros((E, D), jnp.float32), jnp.zeros((D, N), jnp.float32), jnp.zeros((E,), jnp.float32))
    final_carry, unused = lax.scan(advance, start_carry, jnp.arange(N_SEQ, dtype=jnp.int32))
    return (final_carry[1], final_carry[2], final_carry[3])
```

```python
import functools
import math

import jax
import jax.numpy as jnp
from jax import lax
from jax.experimental import pallas as pl
from jax.experimental.pallas import tpu as pltpu
from jax.sharding import PartitionSpec as P

f32 = jnp.float32
bf16 = jnp.bfloat16
LOG2E = math.log2(math.e)
LOG_PULSE = math.log(0.7)
NT = (((1,), (1,)), ((), ()))
TN = (((0,), (0,)), ((), ()))


def dot(a, b, dims=(((1,), (0,)), ((), ()))):
    return lax.dot_general(a, b, dims, preferred_element_type=f32)


def split(x, terms):
    parts = []
    for _ in range(terms):
        part = x.astype(bf16)
        parts.append(part)
        x = x - part.astype(f32)
    return parts


def iota(shape, axis):
    return lax.broadcasted_iota(jnp.int32, shape, axis)


def spread_matrix(rows, heads, channels):
    size = channels // heads
    return (iota((rows, channels), 0) % heads == iota((rows, channels), 1) // size).astype(bf16)


def spread(values, sensor, heads, spread2):
    lane = iota(values.shape, 1)
    own = jnp.where(lane // heads == sensor, values, 0.0)
    return dot(jnp.concatenate(split(own, 2), axis=1), spread2)


def front_kernel(
    half_ref, readings, kmix, w_channels, w_state, w_step, bias, rate, marks,
    mixed_ref, channels_ref, maps_ref, step_ref, cum_ref, cum_t_ref, keep_ref, send_ref, tail_ref,
    wms, spread2, state_sc, log_sc, *, heads,
):
    i = pl.program_id(0)
    sensors, chunk, width = readings.shape
    rows = sensors * chunk
    maps = w_state.shape[1]
    nstate = maps // 2
    channels = w_channels.shape[1]
    lanes = sensors * heads

    @pl.when(i == 0)
    def _():
        wms[...] = jnp.zeros_like(wms)
        wms[:, 0:maps] = w_state[...]
        wms[:, maps : maps + heads] = w_step[...]
        spread2[...] = spread_matrix(spread2.shape[0], heads, channels)

    x = readings[...].reshape(rows, width)
    mixed = (x.astype(f32) + dot(kmix[...], x)).astype(bf16)
    mixed_ref[...] = mixed.reshape(sensors, chunk, width)
    here = pl.ds(pl.multiple_of(i * chunk, chunk), chunk)
    channels_ref[:, here, :] = dot(mixed, w_channels[...]).astype(bf16).reshape(sensors, chunk, channels)
    small = dot(mixed, wms[...])
    maps_ref[:, here, :] = small[:, 0:maps].astype(bf16).reshape(sensors, chunk, maps)
    steps = small[:, maps:].reshape(sensors, chunk, lanes)
    packed = steps[0]
    for s in range(1, sensors):
        packed = packed + pltpu.roll(steps[s], heads * s, 1)
    raw = (packed + bias[...]).astype(bf16).astype(f32)
    step = jnp.maximum(raw, 0.0) + jnp.log1p(jnp.exp(-jnp.abs(raw)))
    step_ref[here, :] = step
    log_sc[here, :] = (rate[...] * step + LOG_PULSE * marks[...]) * LOG2E

    @pl.when(i == pl.num_programs(0) - 1)
    def _():
        span = log_sc.shape[0]
        lower = (iota((span, span), 0) >= iota((span, span), 1)).astype(bf16)
        cum = sum(dot(lower, part) for part in split(log_sc[...], 3))
        cum_ref[...] = cum
        cum_t_ref[...] = cum.T
        last = cum[span - 1 : span, :]
        weight = jnp.exp2(last - cum) * step_ref[...]

        def one(s, carry):
            scale = spread(weight, s, heads, spread2[...])
            scaled = (channels_ref[s].astype(f32) * scale).astype(bf16)
            state = dot(maps_ref[s], scaled, TN)
            state_sc[s] = state[0:nstate]
            return carry

        lax.fori_loop(0, sensors, one, 0)
        own = jnp.where(iota((sensors, lanes), 1) // heads == iota((sensors, lanes), 0), last, 0.0)
        tail = sum(dot(part, spread2[0:lanes, :]) for part in split(own, 3))
        tail_ref[...] = tail
        half = sensors // 2
        mine = half_ref[0] * half
        other = half - mine
        keep_ref[...] = state_sc[pl.ds(mine, half)].reshape(half * nstate, channels)
        send_ref[0 : half * nstate, :] = state_sc[pl.ds(other, half)].reshape(half * nstate, channels)
        send_ref[half * nstate :, :] = tail


def pair_blocks(x, size):
    lane = iota(x.shape, 1)
    zero = jnp.zeros_like(x)
    return jnp.concatenate([jnp.where(lane < size, x, zero), jnp.where(lane >= size, x, zero)], axis=0)


def within_kernel(
    channels, maps, step, cum, cum_t, cot, w_out, skip,
    part_ref, scaled_ref, decay_ref, grad_ref, spread2, *, heads,
):
    i = pl.program_id(0)
    group, span, width = channels.shape
    nstate = maps.shape[2] // 2
    size = width // heads

    @pl.when(i == 0)
    def _():
        spread2[...] = spread_matrix(spread2.shape[0], heads, width)

    grad = dot(cot[...].reshape(group * span, cot.shape[2]), w_out[...], NT)
    grad_ref[...] = grad.reshape(group, span, width)
    causal = iota((span, span), 0) >= iota((span, span), 1)
    for k in range(group):
        s = i * group + k
        chan = channels[k].astype(f32)
        scaled = (chan * spread(step[...], s, heads, spread2[...])).astype(bf16)
        scaled_ref[k] = scaled
        both = maps[k]
        scores = dot(both[:, nstate:], both[:, 0:nstate], NT)
        row = cum_t[k * heads : (k + 1) * heads, :]
        col = row.T
        for pair in range(heads // 2):
            weighted = []
            for h in (2 * pair, 2 * pair + 1):
                gap = jnp.broadcast_to(col[:, h : h + 1], (span, span)) - row[h : h + 1, :]
                decay = jnp.exp2(jnp.where(causal, gap, -jnp.inf))
                decay_ref[k, h] = decay.astype(bf16)
                weighted.append((scores * decay).astype(bf16))
            lanes = slice(2 * pair * size, 2 * (pair + 1) * size)
            out = dot(jnp.concatenate(weighted, axis=1), pair_blocks(scaled[:, lanes], size))
            part_ref[k, :, lanes] = out + skip[:, lanes] * chan[:, lanes]


def back_kernel(
    half_ref, state, maps, scaled, decay, part, grad, cum, cot, mixed, gain,
    keep_ref, send_ref, spread2, total, gain_sc, *, heads,
):
    i = pl.program_id(0)
    group, span, width = part.shape
    nstate = maps.shape[2] // 2
    size = width // heads

    @pl.when(i == 0)
    def _():
        spread2[...] = spread_matrix(spread2.shape[0], heads, width)
        total[...] = jnp.zeros_like(total)
        gain_sc[...] = jnp.zeros_like(gain_sc)

    fade = jnp.exp2(cum[...])
    outs = []
    reads = []
    for k in range(group):
        s = i * group + k
        both = maps[k]
        fade_s = spread(fade, s, heads, spread2[...])
        out = part[k] + dot(both[:, nstate:], state[k]) * fade_s
        inv = lax.rsqrt(jnp.mean(out * out, axis=-1, keepdims=True) + 1e-05)
        normed = out * inv
        outs.append((normed * gain[...]).astype(bf16))
        g = grad[k]
        by_gain = normed * g
        gain_sc[...] += jnp.sum(by_gain.reshape(span // 8, 8, width), axis=0)
        mean = jnp.mean(by_gain * gain[...], axis=-1, keepdims=True)
        back = inv * (g * gain[...] - normed * mean)
        back16 = back.astype(bf16)
        carried = dot((back * fade_s).astype(bf16), state[k], NT)
        pairs = jnp.zeros((span, span), f32)
        for pair in range(heads // 2):
            lanes = slice(2 * pair * size, 2 * (pair + 1) * size)
            both_heads = dot(back16[:, lanes], pair_blocks(scaled[k][:, lanes], size), NT)
            pairs = pairs + both_heads[:, 0:span] * decay[k, 2 * pair].astype(f32)
            pairs = pairs + both_heads[:, span:] * decay[k, 2 * pair + 1].astype(f32)
        inner = dot(pairs.astype(bf16), both[:, 0:nstate])
        reads.append((carried + inner).astype(bf16))
    rows = group * span
    normed_out = jnp.concatenate(outs, axis=0)
    read_grad = jnp.concatenate(reads, axis=0)
    total[0:width, :] += dot(normed_out, cot[...].reshape(rows, cot.shape[2]), TN)
    total[width : width + nstate, :] += dot(read_grad, mixed[...].reshape(rows, mixed.shape[2]), TN)

    @pl.when(i == pl.num_programs(0) - 1)
    def _():
        total[width + nstate : width + nstate + 1, 0:width] = jnp.sum(gain_sc[...], axis=0, keepdims=True)
        half = keep_ref.shape[0]
        mine = pl.multiple_of(half_ref[0] * half, 8)
        other = pl.multiple_of(half - half_ref[0] * half, 8)
        keep_ref[...] = total[pl.ds(mine, half), :]
        send_ref[...] = total[pl.ds(other, half), :]


def whole(shape):
    return pl.BlockSpec(shape, lambda *_: (0,) * len(shape), pipeline_mode=pl.Buffered(1))


def swap(x, distance, count):
    return lax.ppermute(x, "seq", [(i, i ^ distance) for i in range(count)])


def narrow(x):
    return lax.reduce_precision(x, 8, 7)


def pick(bit, when_one, when_zero):
    return jnp.where(bit == 1, when_one, when_zero)


def fading(tail, start, states):
    sensors, nstate, width = states.shape
    own = lax.dynamic_slice_in_dim(tail, start, sensors, 0)
    return jnp.exp2(own)[:, None, :]


def exchange(keep, send, tail, me, count, shards):
    sensors, width = tail.shape
    levels = count.bit_length() - 1
    size = sensors // 2
    nstate = keep.shape[0] // size
    own = keep.reshape(size, nstate, width)
    start = (me & 1) * size
    saved = []
    for level in range(shards):
        bit = (me >> level) & 1
        came = swap(send, 1 << level, count)
        rows = size * nstate
        other = came[0:rows].astype(f32).reshape(size, nstate, width)
        if came.dtype == f32:
            other_tail = came[rows:]
        else:
            other_tail = came[rows : rows + sensors].astype(f32) + came[rows + sensors :].astype(f32)
        low, high = pick(bit, other, own), pick(bit, own, other)
        low_tail, high_tail = pick(bit, other_tail, tail), pick(bit, tail, other_tail)
        total = low * fading(high_tail, start, low) + high
        saved.append((low, low_tail, start, bit))
        tail = tail + other_tail
        if level + 1 < shards:
            next_bit = (me >> (level + 1)) & 1
            size //= 2
            own = lax.dynamic_slice_in_dim(total, next_bit * size, size, 0)
            gone = lax.dynamic_slice_in_dim(total, (1 - next_bit) * size, size, 0)
            start = start + next_bit * size
        else:
            own = gone = total
        first = tail.astype(bf16)
        second = (tail - narrow(tail)).astype(bf16)
        send = jnp.concatenate([gone.astype(bf16).reshape(size * nstate, width), first, second], axis=0)
    before = jnp.zeros_like(own)
    before_tail = jnp.zeros_like(tail)
    for level in range(shards, levels):
        bit = (me >> level) & 1
        came = swap(send, 1 << level, count)
        rows = size * nstate
        other = came[0:rows].astype(f32).reshape(size, nstate, width)
        other_tail = came[rows : rows + sensors].astype(f32) + came[rows + sensors :].astype(f32)
        before = pick(bit, other * fading(before_tail, start, other) + before, before)
        before_tail = pick(bit, before_tail + other_tail, before_tail)
        if level + 1 < levels:
            low, high = pick(bit, other, own), pick(bit, own, other)
            own = low * fading(pick(bit, tail, other_tail), start, low) + high
            tail = tail + other_tail
            first = tail.astype(bf16)
            second = (tail - narrow(tail)).astype(bf16)
            send = jnp.concatenate([own.astype(bf16).reshape(rows, width), first, second], axis=0)
    for level in reversed(range(shards)):
        low, low_tail, start, bit = saved[level]
        after = before * fading(low_tail, start, low) + low
        mine, gone = pick(bit, after, before), pick(bit, before, after)
        came = swap(gone.astype(bf16), 1 << level, count).astype(f32)
        before = pick(bit, jnp.concatenate([came, mine], axis=0), jnp.concatenate([mine, came], axis=0))
    return before.astype(bf16)


def all_sum(keep, send, me, count, shards):
    levels = count.bit_length() - 1
    own = keep
    for level in range(shards):
        came = swap(send, 1 << level, count)
        own = own + came.astype(f32)
        if level + 1 < shards:
            bit = (me >> (level + 1)) & 1
            size = own.shape[0] // 2
            send = lax.dynamic_slice_in_dim(own, (1 - bit) * size, size, 0).astype(bf16)
            own = lax.dynamic_slice_in_dim(own, bit * size, size, 0)
    for level in range(shards, levels):
        own = narrow(own)
        own = own + swap(own.astype(bf16), 1 << level, count).astype(f32)
    out = own.astype(bf16)
    for level in reversed(range(shards)):
        bit = (me >> level) & 1
        came = swap(out, 1 << level, count)
        out = pick(bit, jnp.concatenate([came, out], axis=0), jnp.concatenate([out, came], axis=0))
    return out.astype(f32)


def per_device(
    count, readings, block_graph, cluster_of, mix_weight, boundaries, w_channels, w_state, w_step,
    step_bias, channel_fading_exponent, skip_gain, norm_gain, w_out, cotangent,
):
    sensors, span, width = readings.shape
    heads = channel_fading_exponent.shape[0]
    channels = w_channels.shape[1]
    maps = w_state.shape[1]
    nstate = maps // 2
    size = channels // heads
    lanes = sensors * heads
    me = lax.axis_index("seq")
    shards = min(max(count.bit_length() - 2, 1), 3)
    chunk = 16
    rows = sensors * chunk

    onehot = (cluster_of[:, None] == jnp.arange(sensors, dtype=jnp.int32)[None, :]).astype(f32)
    linked = jnp.dot(jnp.dot(onehot, block_graph.astype(f32)), onehot.T)
    coupling = (linked * mix_weight).astype(bf16)
    same = (jnp.arange(rows)[:, None] % chunk == jnp.arange(rows)[None, :] % chunk)
    kmix = jnp.where(same, jnp.repeat(jnp.repeat(coupling, chunk, 0), chunk, 1), 0).astype(bf16)
    bias = jnp.tile(step_bias, sensors)[None, :]
    rate = jnp.tile(-jnp.exp(channel_fading_exponent), sensors)[None, :]
    skip = jnp.repeat(skip_gain, size)[None, :]
    marks = boundaries.astype(f32)[:, None]
    half = (me & 1).astype(jnp.int32)[None]
    half_rows = sensors // 2 * nstate

    mixed, chans, maps_all, step, cum, cum_t, keep, send, tail = pl.pallas_call(
        functools.partial(front_kernel, heads=heads),
        name="front",
        grid_spec=pltpu.PrefetchScalarGridSpec(
            num_scalar_prefetch=1,
            grid=(span // chunk,),
            in_specs=[
                pl.BlockSpec((sensors, chunk, width), lambda i, *_: (0, i, 0)),
                whole((rows, rows)),
                whole((width, channels)),
                whole((width, maps)),
                whole((width, heads)),
                whole((1, lanes)),
                whole((1, lanes)),
                pl.BlockSpec((chunk, 1), lambda i, *_: (i, 0)),
            ],
            out_specs=[
                pl.BlockSpec((sensors, chunk, width), lambda i, *_: (0, i, 0)),
                whole((sensors, span, channels)),
                whole((sensors, span, maps)),
                whole((span, lanes)),
                whole((span, lanes)),
                whole((lanes, span)),
                whole((half_rows, channels)),
                whole((half_rows + sensors, channels)),
                whole((sensors, channels)),
            ],
            scratch_shapes=[
                pltpu.VMEM((width, maps + lanes), bf16),
                pltpu.VMEM((2 * lanes, channels), bf16),
                pltpu.VMEM((sensors, nstate, channels), f32),
                pltpu.VMEM((span, lanes), f32),
            ],
        ),
        out_shape=[
            jax.ShapeDtypeStruct((sensors, span, width), bf16),
            jax.ShapeDtypeStruct((sensors, span, channels), bf16),
            jax.ShapeDtypeStruct((sensors, span, maps), bf16),
            jax.ShapeDtypeStruct((span, lanes), f32),
            jax.ShapeDtypeStruct((span, lanes), f32),
            jax.ShapeDtypeStruct((lanes, span), f32),
            jax.ShapeDtypeStruct((half_rows, channels), f32),
            jax.ShapeDtypeStruct((half_rows + sensors, channels), f32),
            jax.ShapeDtypeStruct((sensors, channels), f32),
        ],
        compiler_params=pltpu.CompilerParams(
            dimension_semantics=("arbitrary",), vmem_limit_bytes=48 << 20
        ),
        cost_estimate=pl.CostEstimate(flops=5 * 10**9, bytes_accessed=14 << 20, transcendentals=0),
    )(half, readings, kmix, w_channels, w_state, w_step, bias, rate, marks)

    group = 2

    def by_sensor(*shape):
        return pl.BlockSpec((group,) + shape, lambda i, *_: (i,) + (0,) * len(shape))

    part, scaled, decay, grad = pl.pallas_call(
        functools.partial(within_kernel, heads=heads),
        name="within",
        grid_spec=pltpu.PrefetchScalarGridSpec(
            num_scalar_prefetch=0,
            grid=(sensors // group,),
            in_specs=[
                by_sensor(span, channels),
                by_sensor(span, maps),
                whole((span, lanes)),
                whole((span, lanes)),
                pl.BlockSpec((group * heads, span), lambda i, *_: (i, 0)),
                by_sensor(span, width),
                whole((channels, width)),
                whole((1, channels)),
            ],
            out_specs=[
                by_sensor(span, channels),
                by_sensor(span, channels),
                by_sensor(heads, span, span),
                by_sensor(span, channels),
            ],
            scratch_shapes=[pltpu.VMEM((2 * lanes, channels), bf16)],
        ),
        out_shape=[
            jax.ShapeDtypeStruct((sensors, span, channels), f32),
            jax.ShapeDtypeStruct((sensors, span, channels), bf16),
            jax.ShapeDtypeStruct((sensors, heads, span, span), bf16),
            jax.ShapeDtypeStruct((sensors, span, channels), f32),
        ],
        compiler_params=pltpu.CompilerParams(
            dimension_semantics=("arbitrary",), vmem_limit_bytes=48 << 20
        ),
        cost_estimate=pl.CostEstimate(flops=5 * 10**9, bytes_accessed=22 << 20, transcendentals=2 << 20),
    )(chans, maps_all, step, cum, cum_t, cotangent, w_out, skip)

    state = exchange(keep, send, tail, me, count, shards)

    total_rows = -(-(channels + nstate + 1) // 64) * 64
    keep_sum, send_sum = pl.pallas_call(
        functools.partial(back_kernel, heads=heads),
        name="back",
        grid_spec=pltpu.PrefetchScalarGridSpec(
            num_scalar_prefetch=1,
            grid=(sensors // group,),
            in_specs=[
                by_sensor(nstate, channels),
                by_sensor(span, maps),
                by_sensor(span, channels),
                by_sensor(heads, span, span),
                by_sensor(span, channels),
                by_sensor(span, channels),
                whole((span, lanes)),
                by_sensor(span, width),
                by_sensor(span, width),
                whole((1, channels)),
            ],
            out_specs=[whole((total_rows // 2, width)), whole((total_rows // 2, width))],
            scratch_shapes=[
                pltpu.VMEM((2 * lanes, channels), bf16),
                pltpu.VMEM((total_rows, width), f32),
                pltpu.VMEM((8, channels), f32),
            ],
        ),
        out_shape=[jax.ShapeDtypeStruct((total_rows // 2, width), f32)] * 2,
        compiler_params=pltpu.CompilerParams(
            dimension_semantics=("arbitrary",), vmem_limit_bytes=48 << 20
        ),
        cost_estimate=pl.CostEstimate(flops=5 * 10**9, bytes_accessed=26 << 20, transcendentals=0),
    )(half, state, maps_all, scaled, decay, part, grad, cum, cotangent, mixed, norm_gain[None, :])

    sums = all_sum(keep_sum, send_sum, me, count, shards)
    return (
        sums[0:channels],
        sums[channels : channels + nstate].T,
        sums[channels + nstate, 0:channels],
    )


def solution(mesh):
    in_specs = (
        P("groups", "seq", None), P("groups", None), P("groups"), P(), P(("groups", "seq")),
        P(), P(), P(), P(), P(), P(), P(), P(), P("groups", "seq", None),
    )
    out_specs = (P("groups", None), P("groups", None), P("groups"))
    return jax.shard_map(
        functools.partial(per_device, mesh.shape["seq"]),
        mesh=mesh, in_specs=in_specs, out_specs=out_specs, check_vma=False,
    )
```

```python
import functools
import math

import jax
import jax.numpy as jnp
from jax import lax
from jax.experimental import pallas as pl
from jax.experimental.pallas import tpu as pltpu
from jax.sharding import PartitionSpec as P

f32 = jnp.float32
bf16 = jnp.bfloat16
LOG2E = math.log2(math.e)
LOG_PULSE = math.log(0.7)
NT = (((1,), (1,)), ((), ()))
TN = (((0,), (0,)), ((), ()))


def dot(a, b, dims=(((1,), (0,)), ((), ()))):
    return lax.dot_general(a, b, dims, preferred_element_type=f32)


def split(x, terms):
    parts = []
    for _ in range(terms):
        part = x.astype(bf16)
        parts.append(part)
        x = x - part.astype(f32)
    return parts


def iota(shape, axis):
    return lax.broadcasted_iota(jnp.int32, shape, axis)


def spread_matrix(rows, heads, channels):
    size = channels // heads
    return (iota((rows, channels), 0) % heads == iota((rows, channels), 1) // size).astype(bf16)


def spread(values, sensor, heads, spread2):
    lane = iota(values.shape, 1)
    own = jnp.where(lane // heads == sensor, values, 0.0)
    return dot(jnp.concatenate(split(own, 2), axis=1), spread2)


def front_kernel(
    half_ref, readings, graph, cluster, mix, marks, w_channels, w_state, w_step_t, bias, fading_exponent,
    mixed_ref, channels_ref, maps_ref, step_ref, cum_ref, cum_t_ref, keep_ref, send_ref, tail_ref, token_ref,
    kmix, wms, spread2, rows_sc, state_sc, log_sc, *, heads,
):
    i = pl.program_id(0)
    sensors, chunk, width = readings.shape
    rows = sensors * chunk
    maps = w_state.shape[1]
    nstate = maps // 2
    channels = w_channels.shape[1]
    lanes = sensors * heads

    @pl.when(i == 0)
    def _():
        token_ref[...] = jnp.zeros_like(token_ref)
        wms[...] = jnp.zeros_like(wms)
        wms[:, 0:maps] = w_state[...]
        wms[:, maps : maps + heads] = w_step_t[...].astype(f32).T.astype(bf16)
        spread2[...] = spread_matrix(spread2.shape[0], heads, channels)
        picked = (iota((sensors, sensors), 0) == cluster[...]).astype(bf16)
        linked = dot(dot(picked, graph[...].astype(f32).astype(bf16), TN).astype(bf16), picked)
        coupling = (linked * mix[...]).astype(bf16)
        sensor_of = (iota((rows, sensors), 0) // chunk == iota((rows, sensors), 1)).astype(bf16)
        full = dot(dot(sensor_of, coupling).astype(bf16), sensor_of, NT)
        same = iota((rows, rows), 0) % chunk == iota((rows, rows), 1) % chunk
        kmix[...] = jnp.where(same, full, 0.0).astype(bf16)
        tiled = (iota((heads, lanes), 1) % heads == iota((heads, lanes), 0)).astype(bf16)
        both = jnp.concatenate([bias[...], -jnp.exp(fading_exponent[...]) * LOG2E], axis=0)
        rows_sc[0:2, :] = sum(dot(part, tiled) for part in split(both, 3))

    x = readings[...].reshape(rows, width)
    mixed = (x.astype(f32) + dot(kmix[...], x)).astype(bf16)
    mixed_ref[...] = mixed.reshape(sensors, chunk, width)
    here = pl.ds(pl.multiple_of(i * chunk, chunk), chunk)
    channels_ref[:, here, :] = dot(mixed, w_channels[...]).astype(bf16).reshape(sensors, chunk, channels)
    small = dot(mixed, wms[...])
    maps_ref[:, here, :] = small[:, 0:maps].astype(bf16).reshape(sensors, chunk, maps)
    steps = small[:, maps:].reshape(sensors, chunk, lanes)
    packed = steps[0]
    for s in range(1, sensors):
        packed = packed + pltpu.roll(steps[s], heads * s, 1)
    raw = (packed + rows_sc[0:1, :]).astype(bf16).astype(f32)
    step = jnp.maximum(raw, 0.0) + jnp.log1p(jnp.exp(-jnp.abs(raw)))
    step_ref[here, :] = step
    log_sc[here, :] = rows_sc[1:2, :] * step

    @pl.when(i == pl.num_programs(0) - 1)
    def _():
        span = log_sc.shape[0]
        at, to = iota((span, span), 0), iota((span, span), 1)
        marked = jnp.sum(jnp.where(at == to, marks[...].astype(f32), 0.0), axis=1, keepdims=True)
        log_decay = log_sc[...] + (LOG_PULSE * LOG2E) * marked
        lower = (at >= to).astype(bf16)
        cum = sum(dot(lower, part) for part in split(log_decay, 3))
        cum_ref[...] = cum
        cum_t_ref[...] = cum.T
        last = cum[span - 1 : span, :]
        weight = jnp.exp2(last - cum) * step_ref[...]

        def one(s, carry):
            scale = spread(weight, s, heads, spread2[...])
            scaled = (channels_ref[s].astype(f32) * scale).astype(bf16)
            state = dot(maps_ref[s], scaled, TN)
            state_sc[s] = state[0:nstate]
            return carry

        lax.fori_loop(0, sensors, one, 0)
        own = jnp.where(iota((sensors, lanes), 1) // heads == iota((sensors, lanes), 0), last, 0.0)
        tail = sum(dot(part, spread2[0:lanes, :]) for part in split(own, 3))
        tail_ref[...] = tail
        half = sensors // 2
        mine = half_ref[0] * half
        other = half - mine
        keep_ref[...] = state_sc[pl.ds(mine, half)].reshape(half * nstate, channels)
        send_ref[0 : half * nstate, :] = state_sc[pl.ds(other, half)].reshape(half * nstate, channels)
        send_ref[half * nstate :, :] = tail


def pair_blocks(x, size):
    lane = iota(x.shape, 1)
    zero = jnp.zeros_like(x)
    return jnp.concatenate([jnp.where(lane < size, x, zero), jnp.where(lane >= size, x, zero)], axis=0)


def within_kernel(
    channels, maps, step, cum_t, cot, w_out, skip_gain, *refs, heads, first, aliases,
):
    part_ref, scaled_ref, decay_ref, grad_ref, _, spread2, skip = refs[aliases:]
    i = pl.program_id(0)
    group, span, width = channels.shape
    nstate = maps.shape[2] // 2
    size = width // heads

    @pl.when(i == 0)
    def _():
        spread2[...] = spread_matrix(spread2.shape[0], heads, width)
        skip[0:1, :] = sum(dot(part, spread2[0:heads, :]) for part in split(skip_gain[...], 3))

    grad = dot(cot[...].reshape(group * span, cot.shape[2]), w_out[...], NT)
    grad_ref[...] = grad.reshape(group, span, width)
    causal = iota((span, span), 0) >= iota((span, span), 1)
    for k in range(group):
        s = (first + i) * group + k
        chan = channels[k].astype(f32)
        scaled = (chan * spread(step[...], s, heads, spread2[...])).astype(bf16)
        scaled_ref[k] = scaled
        both = maps[k]
        scores = dot(both[:, nstate:], both[:, 0:nstate], NT)
        row = cum_t[k * heads : (k + 1) * heads, :]
        col = row.T
        for pair in range(heads // 2):
            weighted = []
            for h in (2 * pair, 2 * pair + 1):
                gap = jnp.broadcast_to(col[:, h : h + 1], (span, span)) - row[h : h + 1, :]
                decay = jnp.exp2(jnp.where(causal, gap, -jnp.inf))
                decay_ref[k, h] = decay.astype(bf16)
                weighted.append((scores * decay).astype(bf16))
            lanes = slice(2 * pair * size, 2 * (pair + 1) * size)
            out = dot(jnp.concatenate(weighted, axis=1), pair_blocks(scaled[:, lanes], size))
            part_ref[k, :, lanes] = out + skip[0:1, lanes] * chan[:, lanes]


def back_kernel(
    first_ref, state, maps, scaled, decay, part, grad, cum, gain, *refs, heads, aliases,
):
    normed_ref, read_ref, gain_ref, _, spread2 = refs[aliases:]
    i = pl.program_id(0)
    group, span, width = part.shape
    nstate = maps.shape[2] // 2
    size = width // heads

    @pl.when(i == 0)
    def _():
        spread2[...] = spread_matrix(spread2.shape[0], heads, width)
        gain_ref[...] = jnp.zeros_like(gain_ref)

    fade = jnp.exp2(cum[...])
    for k in range(group):
        s = (first_ref[0] + i) * group + k
        both = maps[k]
        fade_s = spread(fade, s, heads, spread2[...])
        out = part[k] + dot(both[:, nstate:], state[k]) * fade_s
        inv = lax.rsqrt(jnp.mean(out * out, axis=-1, keepdims=True) + 1e-05)
        normed = out * inv
        normed_ref[k] = (normed * gain[...]).astype(bf16)
        g = grad[k]
        by_gain = normed * g
        gain_ref[...] += jnp.sum(by_gain.reshape(span // 8, 8, width), axis=0)
        mean = jnp.mean(by_gain * gain[...], axis=-1, keepdims=True)
        back = inv * (g * gain[...] - normed * mean)
        back16 = back.astype(bf16)
        carried = dot((back * fade_s).astype(bf16), state[k], NT)
        pairs = jnp.zeros((span, span), f32)
        for pair in range(heads // 2):
            lanes = slice(2 * pair * size, 2 * (pair + 1) * size)
            both_heads = dot(back16[:, lanes], pair_blocks(scaled[k][:, lanes], size), NT)
            pairs = pairs + both_heads[:, 0:span] * decay[k, 2 * pair].astype(f32)
            pairs = pairs + both_heads[:, span:] * decay[k, 2 * pair + 1].astype(f32)
        inner = dot(pairs.astype(bf16), both[:, 0:nstate])
        read_ref[k] = (carried + inner).astype(bf16)


def grads_kernel(half_ref, normed, cot, read, mixed, *refs):
    *gains, keep_ref, send_ref, total = refs
    i = pl.program_id(0)
    rows = normed.shape[0] * normed.shape[1]
    channels, width, nstate = normed.shape[2], cot.shape[2], read.shape[2]
    piece = total.shape[1]
    pieces = width // piece

    @pl.when(i == 0)
    def _():
        total[...] = jnp.zeros_like(total)
        gain = sum(jnp.sum(ref[...], axis=0, keepdims=True) for ref in gains)
        for j in range(channels // piece):
            at = pieces * (channels + nstate) + j
            total[at : at + 1, :] = gain[:, j * piece : (j + 1) * piece]

    out = dot(normed[...].reshape(rows, channels), cot[...].reshape(rows, width), TN)
    into = dot(read[...].reshape(rows, nstate), mixed[...].reshape(rows, width), TN)
    for j in range(pieces):
        lanes = slice(j * piece, (j + 1) * piece)
        total[j * channels : (j + 1) * channels, :] += out[:, lanes]
        at = pieces * channels + j * nstate
        total[at : at + nstate, :] += into[:, lanes]

    @pl.when(i == pl.num_programs(0) - 1)
    def _():
        half = keep_ref.shape[0]
        mine = pl.multiple_of(half_ref[0] * half, 8)
        other = pl.multiple_of(half - half_ref[0] * half, 8)
        keep_ref[...] = total[pl.ds(mine, half), :]
        send_ref[...] = total[pl.ds(other, half), :]


def finish_kernel(half_ref, mine, came, out_ref, read_ref, gain_ref):
    channels, width = out_ref.shape
    nstate = read_ref.shape[0]
    half, piece = mine.shape
    pieces = width // piece

    def write(low, high):
        def rows(start, size):
            parts = []
            if start < half:
                parts.append(low[start : min(start + size, half), :])
            if start + size > half:
                parts.append(high[max(start - half, 0) : start + size - half, :])
            return jnp.concatenate([part.astype(f32) for part in parts], axis=0)

        for j in range(pieces):
            lanes = slice(j * piece, (j + 1) * piece)
            out_ref[:, lanes] = rows(j * channels, channels)
            read_ref[:, lanes] = rows(pieces * channels + j * nstate, nstate)
        tail = rows(pieces * (channels + nstate), 8)
        for j in range(channels // piece):
            gain_ref[:, j * piece : (j + 1) * piece] = tail[j : j + 1, :]

    pl.when(half_ref[0] == 0)(lambda: write(mine, came))
    pl.when(half_ref[0] == 1)(lambda: write(came, mine))


def whole(shape):
    return pl.BlockSpec(shape, lambda *_: (0,) * len(shape), pipeline_mode=pl.Buffered(1))


BIG = 1 << 19
ANYWHERE = pl.BlockSpec(memory_space=pl.ANY)


def call(body, name, scalars, grid, in_specs, out_specs, out_shape, scratch, vmem, flops, moved, aliases=None):
    inner = pl.pallas_call(
        body,
        name=name,
        grid_spec=pltpu.PrefetchScalarGridSpec(
            num_scalar_prefetch=scalars, grid=grid, in_specs=in_specs, out_specs=out_specs, scratch_shapes=scratch
        ),
        out_shape=[
            (pltpu.HBM if math.prod(shape) >= BIG else jax.ShapeDtypeStruct)(shape, dtype) for shape, dtype in out_shape
        ],
        input_output_aliases=aliases or {},
        compiler_params=pltpu.CompilerParams(dimension_semantics=("arbitrary",), vmem_limit_bytes=vmem << 20),
        cost_estimate=pl.CostEstimate(flops=int(flops), bytes_accessed=int(moved), transcendentals=0),
    )

    def outer(*args):
        return inner(*[pltpu.with_memory_space_constraint(x, pltpu.HBM) if x.size >= BIG else x for x in args])

    return outer


def front(half, readings, graph, cluster, mix, boundaries, w_channels, w_state, w_step, bias, fading_exponent):
    sensors, span, width = readings.shape
    heads, channels, maps = w_step.shape[1], w_channels.shape[1], w_state.shape[1]
    nstate, lanes, chunk = maps // 2, sensors * heads, 16
    rows, half_rows = sensors * chunk, sensors // 2 * nstate
    return call(
        functools.partial(front_kernel, heads=heads), "front", 1, (span // chunk,),
        [
            pl.BlockSpec((sensors, chunk, width), lambda i, *_: (0, i, 0)),
            whole((sensors, sensors)), whole((1, sensors)), whole((sensors, sensors)), whole((1, span)),
            whole((width, channels)), whole((width, maps)), whole((heads, width)),
            whole((1, heads)), whole((1, heads)),
        ],
        [
            pl.BlockSpec((sensors, chunk, width), lambda i, *_: (0, i, 0)),
            whole((sensors, span, channels)), whole((sensors, span, maps)),
            whole((span, lanes)), whole((span, lanes)), whole((lanes, span)),
            whole((half_rows, channels)), whole((half_rows + sensors, channels)), whole((sensors, channels)),
            whole((8, 128)),
        ],
        [
            ((sensors, span, width), bf16), ((sensors, span, channels), bf16), ((sensors, span, maps), bf16),
            ((span, lanes), f32), ((span, lanes), f32), ((lanes, span), f32),
            ((half_rows, channels), f32), ((half_rows + sensors, channels), f32), ((sensors, channels), f32),
            ((8, 128), f32),
        ],
        [
            pltpu.VMEM((rows, rows), bf16), pltpu.VMEM((width, maps + lanes), bf16),
            pltpu.VMEM((2 * lanes, channels), bf16), pltpu.VMEM((8, lanes), f32),
            pltpu.VMEM((sensors, nstate, channels), f32), pltpu.VMEM((span, lanes), f32),
        ],
        28, 5e9, 14e6,
    )(
        half, readings, graph, cluster[None, :], mix, boundaries[None, :], w_channels, w_state, w_step.T,
        bias[None, :], fading_exponent[None, :],
    )


GROUP = 2


def within(first, count, channels, maps, step, cum_t, cot, w_out, skip_gain, done, token):
    sensors, span, width = channels.shape
    heads, nmaps = skip_gain.shape[0], maps.shape[2]
    lanes = sensors * heads

    def block(*shape):
        return pl.BlockSpec((GROUP,) + shape, lambda i, *_: (first + i,) + (0,) * len(shape))

    n_in = 7
    aliases = {n_in + k: k for k in range(len(done))}
    aliases[n_in + len(done)] = 4
    return call(
        functools.partial(within_kernel, heads=heads, first=first, aliases=len(done) + 1), "within", 0, (count,),
        [
            block(span, width), block(span, nmaps), whole((span, lanes)),
            pl.BlockSpec((GROUP * heads, span), lambda i, *_: (first + i, 0)),
            block(span, cot.shape[2]), whole(w_out.shape), whole((1, heads)),
        ] + [ANYWHERE] * (len(done) + 1),
        [block(span, width), block(span, width), block(heads, span, span), block(span, width), ANYWHERE],
        [
            ((sensors, span, width), f32), ((sensors, span, width), bf16),
            ((sensors, heads, span, span), bf16), ((sensors, span, width), f32), (token.shape, token.dtype),
        ],
        [pltpu.VMEM((2 * lanes, width), bf16), pltpu.VMEM((8, width), f32)],
        16, 6e8 * count, 3e6 * count, aliases,
    )(channels, maps, step, cum_t, cot, w_out, skip_gain[None, :], *done, token)


def back(first, state, maps, scaled, decay, part, grad, cum, gain, done, token):
    sensors, span, width = part.shape
    heads, nmaps = decay.shape[1], maps.shape[2]
    nstate, lanes = nmaps // 2, sensors * heads
    count = state.shape[0] // GROUP

    def block(*shape):
        return pl.BlockSpec((GROUP,) + shape, lambda i, at: (at[0] + i,) + (0,) * len(shape))

    n_in = 9
    aliases = {n_in + k: k for k in range(len(done))}
    aliases[n_in + len(done)] = 3
    return call(
        functools.partial(back_kernel, heads=heads, aliases=len(done) + 1), "back", 1, (count,),
        [
            pl.BlockSpec((GROUP, nstate, width), lambda i, at: (i, 0, 0)),
            block(span, nmaps), block(span, width), block(heads, span, span), block(span, width), block(span, width),
            whole((span, lanes)), whole((1, width)),
        ] + [ANYWHERE] * (len(done) + 1),
        [block(span, width), block(span, nstate), whole((8, width)), ANYWHERE],
        [
            ((sensors, span, width), bf16), ((sensors, span, nstate), bf16), ((8, width), f32),
            (token.shape, token.dtype),
        ],
        [pltpu.VMEM((2 * lanes, width), bf16)],
        16, 6e8 * count, 3e6 * count, aliases,
    )(first, state, maps, scaled, decay, part, grad, cum, gain[None, :], *done, token)


def grads(half, normed, cot, read, mixed, gains):
    sensors, span, channels = normed.shape
    width, nstate = cot.shape[2], read.shape[2]
    group, piece = 4, 256
    rows = -(-(width // piece * (channels + nstate) + channels // piece) // 64) * 64

    def block(*shape):
        return pl.BlockSpec((group,) + shape, lambda i, *_: (i,) + (0,) * len(shape))

    return call(
        grads_kernel, "grads", 1, (sensors // group,),
        [block(span, channels), block(span, width), block(span, nstate), block(span, width)]
        + [whole((8, channels))] * len(gains),
        [whole((rows // 2, piece))] * 2,
        [((rows // 2, piece), f32)] * 2,
        [pltpu.VMEM((rows, piece), f32)],
        28, 2.5e9, 14e6,
    )(half, normed, cot, read, mixed, *gains)


def finish(half, mine, came, channels, width, nstate):
    return call(
        finish_kernel, "finish", 1, (1,),
        [whole(mine.shape)] * 2,
        [whole((channels, width)), whole((nstate, width)), whole((1, channels))],
        [((channels, width), f32), ((nstate, width), f32), ((1, channels), f32)],
        [], 12, 1e6, 4e6,
    )(half, mine, came)


def swap(x, distance, count):
    return lax.ppermute(x, "seq", [(i, i ^ distance) for i in range(count)])


def narrow(x):
    return lax.reduce_precision(x, 8, 7)


def pick(bit, when_one, when_zero):
    return jnp.where(bit == 1, when_one, when_zero)


def fading(tail, start, states):
    own = lax.dynamic_slice_in_dim(tail, start, states.shape[0], 0)
    return jnp.exp2(own)[:, None, :]


def tied(x, token):
    return lax.optimization_barrier((x, token))


def exchange(keep, send, tail, me, count, shards, swap_beside, ready):
    sensors, width = tail.shape
    levels = count.bit_length() - 1
    size = sensors // 2
    nstate = keep.shape[0] // size
    own = keep.reshape(size, nstate, width)
    start = (me & 1) * size
    saved = []

    def pack(states, tails):
        return jnp.concatenate([states.astype(bf16).reshape(-1, width), tails.astype(bf16)], axis=0)

    def unpack(came):
        rows = size * nstate
        return came[0:rows].astype(f32).reshape(size, nstate, width), came[rows:].astype(f32)

    for level in range(shards):
        bit = (me >> level) & 1
        other, other_tail = unpack(swap_beside(send, level, True))
        low, high = pick(bit, other, own), pick(bit, own, other)
        low_tail, high_tail = pick(bit, other_tail, tail), pick(bit, tail, other_tail)
        total = low * fading(high_tail, start, low) + high
        saved.append((low, low_tail, start, bit))
        tail = tail + other_tail
        if level + 1 < shards:
            next_bit = (me >> (level + 1)) & 1
            size //= 2
            own = lax.dynamic_slice_in_dim(total, next_bit * size, size, 0)
            gone = lax.dynamic_slice_in_dim(total, (1 - next_bit) * size, size, 0)
            start = start + next_bit * size
        else:
            own = gone = total
        send = pack(gone, tail)
    before = jnp.zeros_like(own)
    before_tail = jnp.zeros_like(tail)
    for level in range(shards, levels):
        bit = (me >> level) & 1
        other, other_tail = unpack(swap_beside(send, level, True))
        before = pick(bit, other * fading(before_tail, start, other) + before, before)
        before_tail = pick(bit, before_tail + other_tail, before_tail)
        if level + 1 < levels:
            low, high = pick(bit, other, own), pick(bit, own, other)
            own = low * fading(pick(bit, tail, other_tail), start, low) + high
            tail = tail + other_tail
            send = pack(own, tail)

    def narrowed(states, start, level):
        for low, low_tail, low_start, bit in reversed(saved[:level]):
            here = lax.dynamic_slice_in_dim(low, start - low_start, states.shape[0], 0)
            states = pick(bit, states * fading(low_tail, start, states) + here, states)
        return states.astype(bf16)

    known, known_start, known_level = before, start, shards
    for level in reversed(range(shards)):
        low, low_tail, start, bit = saved[level]
        after = before * fading(low_tail, start, low) + low
        mine, gone = pick(bit, after, before), pick(bit, before, after)
        ready(narrowed(known, known_start, known_level), known_start, False)
        came = swap_beside(gone.astype(bf16), level, False).astype(f32)
        before = pick(bit, jnp.concatenate([came, mine], axis=0), jnp.concatenate([mine, came], axis=0))
        known, known_start, known_level = came, start + pick(bit, -low.shape[0], low.shape[0]), level
    ready(narrowed(known, known_start, known_level), known_start, True)


def all_sum(keep, send, me, count, shards):
    levels = count.bit_length() - 1
    own = keep
    for level in range(shards):
        came = swap(send, 1 << level, count)
        own = own + came.astype(f32)
        if level + 1 < shards:
            bit = (me >> (level + 1)) & 1
            size = own.shape[0] // 2
            send = lax.dynamic_slice_in_dim(own, (1 - bit) * size, size, 0).astype(bf16)
            own = lax.dynamic_slice_in_dim(own, bit * size, size, 0)
    for level in range(shards, levels):
        own = narrow(own)
        own = own + swap(own.astype(bf16), 1 << level, count).astype(f32)
    out = own.astype(bf16)
    for level in reversed(range(1, shards)):
        bit = (me >> level) & 1
        came = swap(out, 1 << level, count)
        out = pick(bit, jnp.concatenate([came, out], axis=0), jnp.concatenate([out, came], axis=0))
    return out, swap(out, 1, count)


def per_device(
    count, readings, block_graph, cluster_of, mix_weight, boundaries, w_channels, w_state, w_step,
    step_bias, channel_fading_exponent, skip_gain, norm_gain, w_out, cotangent,
):
    sensors, span, width = readings.shape
    channels = w_channels.shape[1]
    nstate = w_state.shape[1] // 2
    me = lax.axis_index("seq")
    half = (me & 1).astype(jnp.int32)[None]
    shards = min(max(count.bit_length() - 2, 1), 3)

    mixed, chans, maps, step, cum, cum_t, keep, send, tail, token = front(
        half, readings, block_graph, cluster_of, mix_weight, boundaries, w_channels, w_state, w_step,
        step_bias, channel_fading_exponent,
    )
    work = {"token": token, "within": (), "back": (), "gains": [], "next": None}
    plan = {1: (0, 3), 2: (3, 2), 3: (5, 3)}

    def inside(level):
        if level in plan:
            first, blocks = plan[level]
            *arrays, work["token"] = within(
                first, blocks, chans, maps, step, cum_t, cotangent, w_out, skip_gain, work["within"], work["token"]
            )
            work["within"] = tuple(arrays)

    def run_back():
        states, start = work["next"]
        part, scaled, decay, grad = work["within"]
        first = (start // GROUP).astype(jnp.int32)[None]
        normed, read, gain, work["token"] = back(
            first, states, maps, scaled, decay, part, grad, cum, norm_gain, work["back"], work["token"]
        )
        work["back"] = (normed, read)
        work["gains"].append(gain)

    def swap_beside(x, level, up):
        x, work["token"] = tied(x, work["token"])
        came = swap(x, 1 << level, count)
        if up:
            inside(level)
        else:
            run_back()
        return came

    def ready(states, start, last):
        work["next"] = (states, start)
        if last:
            run_back()

    exchange(keep, send, tail, me, count, shards, swap_beside, ready)
    keep_sum, send_sum = grads(half, work["back"][0], cotangent, work["back"][1], mixed, work["gains"])
    mine, came = all_sum(keep_sum, send_sum, me, count, shards)
    grad_out, grad_read, grad_gain = finish(half, mine, came, channels, width, nstate)
    return grad_out, grad_read.T, grad_gain[0]


def solution(mesh):
    in_specs = (
        P("groups", "seq", None), P("groups", None), P("groups"), P(), P(("groups", "seq")),
        P(), P(), P(), P(), P(), P(), P(), P(), P("groups", "seq", None),
    )
    out_specs = (P("groups", None), P("groups", None), P("groups"))
    return jax.shard_map(
        functools.partial(per_device, mesh.shape["seq"]),
        mesh=mesh, in_specs=in_specs, out_specs=out_specs, check_vma=False,
    )
```

```python
import functools
import math

import jax
import jax.numpy as jnp
from jax import lax
from jax.experimental import pallas as pl
from jax.experimental.pallas import tpu as pltpu
from jax.sharding import PartitionSpec as P

f32 = jnp.float32
bf16 = jnp.bfloat16
LOG2E = math.log2(math.e)
LOG_PULSE = math.log(0.7)
NT = (((1,), (1,)), ((), ()))
TN = (((0,), (0,)), ((), ()))


def dot(a, b, dims=(((1,), (0,)), ((), ()))):
    return lax.dot_general(a, b, dims, preferred_element_type=f32)


def split(x, terms):
    parts = []
    for _ in range(terms):
        part = x.astype(bf16)
        parts.append(part)
        x = x - part.astype(f32)
    return parts


def iota(shape, axis):
    return lax.broadcasted_iota(jnp.int32, shape, axis)


def spread_matrix(rows, heads, channels):
    size = channels // heads
    return (iota((rows, channels), 0) % heads == iota((rows, channels), 1) // size).astype(bf16)


def spread(values, sensor, heads, spread2):
    lane = iota(values.shape, 1)
    own = jnp.where(lane // heads == sensor, values, 0.0)
    return dot(jnp.concatenate(split(own, 2), axis=1), spread2)


def front_kernel(
    me_ref, readings, graph, cluster, mix, marks, w_channels, w_state, w_step_t, bias, fading_exponent, skip_gain, norm_gain, cot_hbm, w_out_hbm,
    mixed_ref, channels_ref, maps_ref, step_ref, cum_ref, cum_t_ref, keep_ref, send_ref, tail_ref, token_ref, consts_ref, cot_ref, w_out_ref,
    kmix, wms, spread2, rows_sc, state_sc, log_sc, sems, *, heads,
):
    i = pl.program_id(0)
    sensors, chunk, width = readings.shape
    rows = sensors * chunk
    maps = w_state.shape[1]
    nstate = maps // 2
    channels = w_channels.shape[1]
    lanes = sensors * heads
    last_step = pl.num_programs(0) - 1
    each = cot_ref.shape[0] // (cot_ref.shape[1] // chunk)

    def cot_copy(k):
        part = pl.ds(k * each, each)
        return pltpu.make_async_copy(cot_hbm.at[part], cot_ref.at[part], sems.at[k])

    w_out_copy = pltpu.make_async_copy(w_out_hbm, w_out_ref, sems.at[cot_ref.shape[1] // chunk])
    cot_copy(i).start()

    @pl.when(i == last_step)
    def _():
        w_out_copy.start()

    @pl.when(i == 0)
    def _():
        token_ref[...] = jnp.zeros_like(token_ref)
        wms[...] = jnp.zeros_like(wms)
        wms[:, 0:maps] = w_state[...]
        wms[:, maps : maps + heads] = w_step_t[...].astype(f32).T.astype(bf16)
        spread2[...] = spread_matrix(spread2.shape[0], heads, channels)
        picked = (iota((sensors, sensors), 0) == cluster[...]).astype(bf16)
        linked = dot(dot(picked, graph[...].astype(f32).astype(bf16), TN).astype(bf16), picked)
        coupling = (linked * mix[...]).astype(bf16)
        sensor_of = (iota((rows, sensors), 0) // chunk == iota((rows, sensors), 1)).astype(bf16)
        full = dot(dot(sensor_of, coupling).astype(bf16), sensor_of, NT)
        same = iota((rows, rows), 0) % chunk == iota((rows, rows), 1) % chunk
        kmix[...] = jnp.where(same, full, 0.0).astype(bf16)
        tiled = (iota((heads, lanes), 1) % heads == iota((heads, lanes), 0)).astype(bf16)
        both = jnp.concatenate([bias[...], -jnp.exp(fading_exponent[...]) * LOG2E], axis=0)
        rows_sc[0:2, :] = sum(dot(part, tiled) for part in split(both, 3))
        consts_ref[...] = jnp.zeros_like(consts_ref)
        consts_ref[0:1, :] = sum(dot(part, spread2[0:heads, :]) for part in split(skip_gain[...], 3))
        consts_ref[1:2, :] = norm_gain[...]

    x = readings[...].reshape(rows, width)
    mixed = (x.astype(f32) + dot(kmix[...], x)).astype(bf16)
    here = pl.ds(pl.multiple_of(i * chunk, chunk), chunk)
    mixed_ref[:, here, :] = mixed.reshape(sensors, chunk, width)
    channels_ref[:, here, :] = dot(mixed, w_channels[...]).astype(bf16).reshape(sensors, chunk, channels)
    small = dot(mixed, wms[...])
    maps_ref[:, here, :] = small[:, 0:maps].astype(bf16).reshape(sensors, chunk, maps)
    steps = small[:, maps:].reshape(sensors, chunk, lanes)
    packed = steps[0]
    for s in range(1, sensors):
        packed = packed + pltpu.roll(steps[s], heads * s, 1)
    raw = (packed + rows_sc[0:1, :]).astype(bf16).astype(f32)
    step = jnp.maximum(raw, 0.0) + jnp.log1p(jnp.exp(-jnp.abs(raw)))
    step_ref[here, :] = step
    log_sc[here, :] = rows_sc[1:2, :] * step

    @pl.when(i == pl.num_programs(0) - 1)
    def _():
        span = log_sc.shape[0]
        at, to = iota((span, span), 0), iota((span, span), 1)
        marked = jnp.sum(jnp.where(at == to, marks[...].astype(f32), 0.0), axis=1, keepdims=True)
        log_decay = log_sc[...] + (LOG_PULSE * LOG2E) * marked
        lower = (at >= to).astype(bf16)
        cum = sum(dot(lower, part) for part in split(log_decay, 3))
        cum_ref[...] = cum
        cum_t_ref[...] = cum.T
        last = cum[span - 1 : span, :]
        weight = jnp.exp2(last - cum) * step_ref[...]

        def one(s, carry):
            scale = spread(weight, s, heads, spread2[...])
            scaled = (channels_ref[s].astype(f32) * scale).astype(bf16)
            state = dot(maps_ref[s], scaled, TN)
            state_sc[s] = state[0:nstate]
            return carry

        lax.fori_loop(0, sensors, one, 0, unroll=4)
        own = jnp.where(iota((sensors, lanes), 1) // heads == iota((sensors, lanes), 0), last, 0.0)
        tail = sum(dot(part, spread2[0:lanes, :]) for part in split(own, 3))
        tail_ref[...] = tail
        half = sensors // 2
        mine = (me_ref[0] & 1) * half
        other = half - mine
        keep_ref[...] = state_sc[pl.ds(mine, half)]
        send_ref[0 : half * nstate, :] = state_sc[pl.ds(other, half)].reshape(half * nstate, channels).astype(bf16)
        send_ref[half * nstate :, :] = tail.astype(bf16)
        for k in range(cot_ref.shape[1] // chunk):
            cot_copy(k).wait()
        w_out_copy.wait()


def pair_blocks(x, size):
    lane = iota(x.shape, 1)
    zero = jnp.zeros_like(x)
    return jnp.concatenate([jnp.where(lane < size, x, zero), jnp.where(lane >= size, x, zero)], axis=0)


def within_kernel(channels, maps, step, cum_t, cot, w_out, consts, *refs, heads, first, count, aliases):
    part_ref, scaled_ref, decay_ref, grad_ref, _, spread2 = refs[aliases:]
    _, span, width = channels.shape
    nstate = maps.shape[2] // 2
    size = width // heads
    spread2[...] = spread_matrix(spread2.shape[0], heads, width)

    def block(i, carry):
        here = pl.ds((first + i) * GROUP, GROUP)
        grad = dot(cot[here].reshape(GROUP * span, cot.shape[2]), w_out[...], NT)
        grad_ref[here] = grad.reshape(GROUP, span, width)
        causal = iota((span, span), 0) >= iota((span, span), 1)
        for k in range(GROUP):
            s = (first + i) * GROUP + k
            chan = channels[s].astype(f32)
            scaled = (chan * spread(step[...], s, heads, spread2[...])).astype(bf16)
            scaled_ref[s] = scaled
            both = maps[s]
            scores = dot(both[:, nstate:], both[:, 0:nstate], NT)
            row = cum_t[pl.ds(pl.multiple_of(s * heads, heads), heads), :]
            col = row.T
            for pair in range(heads // 2):
                weighted = []
                for h in (2 * pair, 2 * pair + 1):
                    gap = jnp.broadcast_to(col[:, h : h + 1], (span, span)) - row[h : h + 1, :]
                    decay = jnp.exp2(jnp.where(causal, gap, -jnp.inf))
                    decay_ref[s, h] = decay.astype(bf16)
                    weighted.append((scores * decay).astype(bf16))
                lanes = slice(2 * pair * size, 2 * (pair + 1) * size)
                out = dot(jnp.concatenate(weighted, axis=1), pair_blocks(scaled[:, lanes], size))
                part_ref[s, :, lanes] = out + consts[0:1, lanes] * chan[:, lanes]
        return carry

    lax.fori_loop(0, count, block, 0)


def back_kernel(me_ref, state, maps, scaled, decay, part, grad, cum, consts, *refs, heads, aliases, first):
    normed_ref, read_ref, gain_ref, _, spread2 = refs[aliases:]
    _, span, width = part.shape
    nstate = maps.shape[2] // 2
    size = width // heads
    spread2[...] = spread_matrix(spread2.shape[0], heads, width)
    gain = consts[1:2, :]
    begin = first(me_ref[0])

    def sensor(k, gain_sum):
        s = begin + k
        both = maps[s]
        fade_s = spread(jnp.exp2(cum[...]), s, heads, spread2[...])
        out = part[s] + dot(both[:, nstate:], state[k]) * fade_s
        inv = lax.rsqrt(jnp.mean(out * out, axis=-1, keepdims=True) + 1e-05)
        normed = out * inv
        normed_ref[s] = (normed * gain).astype(bf16)
        g = grad[s]
        by_gain = normed * g
        gain_sum = gain_sum + jnp.sum(by_gain.reshape(span // 8, 8, width), axis=0)
        mean = jnp.mean(by_gain * gain, axis=-1, keepdims=True)
        back = inv * (g * gain - normed * mean)
        back16 = back.astype(bf16)
        carried = dot((back * fade_s).astype(bf16), state[k], NT)
        pairs = jnp.zeros((span, span), f32)
        for pair in range(heads // 2):
            lanes = slice(2 * pair * size, 2 * (pair + 1) * size)
            both_heads = dot(back16[:, lanes], pair_blocks(scaled[s, :, lanes], size), NT)
            pairs = pairs + both_heads[:, 0:span] * decay[s, 2 * pair].astype(f32)
            pairs = pairs + both_heads[:, span:] * decay[s, 2 * pair + 1].astype(f32)
        inner = dot(pairs.astype(bf16), both[:, 0:nstate])
        read_ref[s] = (carried + inner).astype(bf16)
        return gain_sum

    gain_ref[...] = lax.fori_loop(0, state.shape[0], sensor, jnp.zeros(gain_ref.shape, f32), unroll=2)


def grads_kernel(me_ref, normed, cot, read, mixed, *refs):
    *gains, keep_ref, send_ref, total = refs
    sensors, span, channels = normed.shape
    width, nstate = cot.shape[2], read.shape[2]
    piece = total.shape[1]
    pieces = width // piece
    rows = sensors * span

    total[pieces * (channels + nstate) :, :] = jnp.zeros((total.shape[0] - pieces * (channels + nstate), piece), f32)
    gain = sum(jnp.sum(ref[...], axis=0, keepdims=True) for ref in gains)
    for j in range(channels // piece):
        at = pieces * (channels + nstate) + j
        total[at : at + 1, :] = gain[:, j * piece : (j + 1) * piece]
    for j in range(pieces):
        lanes = slice(j * piece, (j + 1) * piece)
        right = cot[:, :, lanes].reshape(rows, piece)
        total[j * channels : (j + 1) * channels, :] = dot(normed[...].reshape(rows, channels), right, TN)
        at = pieces * channels + j * nstate
        total[at : at + nstate, :] = dot(read[...].reshape(rows, nstate), mixed[:, :, lanes].reshape(rows, piece), TN)
    half = keep_ref.shape[0]
    mine = pl.multiple_of((me_ref[0] & 1) * half, 8)
    other = pl.multiple_of(half - (me_ref[0] & 1) * half, 8)
    keep_ref[...] = total[pl.ds(mine, half), :]
    send_ref[...] = total[pl.ds(other, half), :].astype(bf16)


def finish_kernel(me_ref, mine, came, out_ref, read_ref, gain_ref):
    channels, width = out_ref.shape
    nstate = read_ref.shape[0]
    half, piece = mine.shape
    pieces = width // piece

    def write(low, high):
        def rows(start, size):
            parts = []
            if start < half:
                parts.append(low[start : min(start + size, half), :])
            if start + size > half:
                parts.append(high[max(start - half, 0) : start + size - half, :])
            return jnp.concatenate([part.astype(f32) for part in parts], axis=0)

        for j in range(pieces):
            lanes = slice(j * piece, (j + 1) * piece)
            out_ref[:, lanes] = rows(j * channels, channels)
            read_ref[:, lanes] = rows(pieces * channels + j * nstate, nstate)
        tail = rows(pieces * (channels + nstate), 8)
        for j in range(channels // piece):
            gain_ref[:, j * piece : (j + 1) * piece] = tail[j : j + 1, :]

    pl.when(me_ref[0] & 1 == 0)(lambda: write(mine, came))
    pl.when(me_ref[0] & 1 == 1)(lambda: write(came, mine))


def whole(shape):
    return pl.BlockSpec(shape, lambda *_: (0,) * len(shape), pipeline_mode=pl.Buffered(1))


ANYWHERE = pl.BlockSpec(memory_space=pl.ANY)
HELD = pl.BlockSpec(memory_space=pltpu.VMEM)
GROUP = 2


def held(x):
    return pltpu.with_memory_space_constraint(x, pltpu.VMEM)


def call(body, name, scalars, grid, in_specs, out_specs, out_shape, scratch, vmem, flops, moved, aliases=None):
    return pl.pallas_call(
        body,
        name=name,
        grid_spec=pltpu.PrefetchScalarGridSpec(
            num_scalar_prefetch=scalars, grid=grid, in_specs=in_specs, out_specs=out_specs, scratch_shapes=scratch
        ),
        out_shape=out_shape,
        input_output_aliases=aliases or {},
        compiler_params=pltpu.CompilerParams(vmem_limit_bytes=vmem << 20),
        cost_estimate=pl.CostEstimate(flops=int(flops), bytes_accessed=int(moved), transcendentals=0),
    )


def front(
    me, readings, graph, cluster, mix, boundaries, w_channels, w_state, w_step, bias, fading_exponent, skip_gain, gain,
    cot, w_out,
):
    sensors, span, width = readings.shape
    heads, channels, maps = w_step.shape[1], w_channels.shape[1], w_state.shape[1]
    nstate, lanes, chunk = maps // 2, sensors * heads, 16
    rows, half_rows = sensors * chunk, sensors // 2 * nstate
    small = [
        graph, cluster[None, :], mix, boundaries[None, :], w_channels, w_state, w_step.T,
        bias[None, :], fading_exponent[None, :], skip_gain[None, :], gain[None, :],
    ]
    outs = [
        ((sensors, span, width), bf16), ((sensors, span, channels), bf16), ((sensors, span, maps), bf16),
        ((span, lanes), f32), ((span, lanes), f32), ((lanes, span), f32),
        ((sensors // 2, nstate, channels), f32), ((half_rows + sensors, channels), bf16), ((sensors, channels), f32),
        ((8, 128), f32), ((8, channels), f32), (cot.shape, cot.dtype), (w_out.shape, w_out.dtype),
    ]
    return call(
        functools.partial(front_kernel, heads=heads), "front", 1, (span // chunk,),
        [pl.BlockSpec((sensors, chunk, width), lambda i, *_: (0, i, 0))] + [whole(x.shape) for x in small] + [ANYWHERE] * 2,
        [HELD] * len(outs),
        [pltpu.VMEM(shape, dtype) for shape, dtype in outs],
        [
            pltpu.VMEM((rows, rows), bf16), pltpu.VMEM((width, maps + lanes), bf16),
            pltpu.VMEM((2 * lanes, channels), bf16), pltpu.VMEM((8, lanes), f32),
            pltpu.VMEM((sensors, nstate, channels), f32), pltpu.VMEM((span, lanes), f32),
            pltpu.SemaphoreType.DMA((span // chunk + 1,)),
        ],
        14, 5e9, 14e6,
    )(me, *[pltpu.with_memory_space_constraint(x, pltpu.HBM) for x in [readings] + small + [cot, w_out]])


def within(first, count, channels, maps, step, cum_t, cot, w_out, consts, heads, done, token):
    sensors, span, width = channels.shape
    lanes = sensors * heads
    n_in = 7
    aliases = {n_in + k: k for k in range(len(done))}
    aliases[n_in + len(done)] = 4
    return call(
        functools.partial(within_kernel, heads=heads, first=first, count=count, aliases=len(done) + 1),
        "within", 0, (),
        [HELD] * (n_in + len(done)) + [ANYWHERE],
        [HELD] * 4 + [ANYWHERE],
        [
            pltpu.VMEM((sensors, span, width), f32), pltpu.VMEM((sensors, span, width), bf16),
            pltpu.VMEM((sensors, heads, span, span), bf16), pltpu.VMEM((sensors, span, width), f32),
            jax.ShapeDtypeStruct(token.shape, token.dtype),
        ],
        [pltpu.VMEM((2 * lanes, width), bf16)],
        6, 6e8 * count, 3e6 * count, aliases,
    )(*[held(x) for x in (channels, maps, step, cum_t, cot, w_out, consts) + done], token)


def back(me, first, state, maps, scaled, decay, part, grad, cum, consts, done, token):
    sensors, span, width = part.shape
    heads, nmaps = decay.shape[1], maps.shape[2]
    nstate, lanes = nmaps // 2, sensors * heads
    count = state.shape[0]
    n_in = 9
    aliases = {n_in + k: k for k in range(len(done))}
    aliases[n_in + len(done)] = 3
    return call(
        functools.partial(back_kernel, heads=heads, aliases=len(done) + 1, first=first), "back", 1, (),
        [HELD] * (n_in - 1 + len(done)) + [ANYWHERE],
        [HELD] * 3 + [ANYWHERE],
        [
            pltpu.VMEM((sensors, span, width), bf16), pltpu.VMEM((sensors, span, nstate), bf16),
            pltpu.VMEM((8, width), f32), jax.ShapeDtypeStruct(token.shape, token.dtype),
        ],
        [pltpu.VMEM((2 * lanes, width), bf16)],
        6, 3e8 * count, 1.5e6 * count, aliases,
    )(me, *[held(x) for x in (state, maps, scaled, decay, part, grad, cum, consts) + done], token)


def grads(me, normed, cot, read, mixed, gains):
    channels, width, nstate = normed.shape[2], cot.shape[2], read.shape[2]
    piece = 256
    rows = -(-(width // piece * (channels + nstate) + channels // piece) // 64) * 64
    return call(
        grads_kernel, "grads", 1, (),
        [HELD] * (4 + len(gains)),
        [HELD] * 2,
        [pltpu.VMEM((rows // 2, piece), f32), pltpu.VMEM((rows // 2, piece), bf16)],
        [pltpu.VMEM((rows, piece), f32)],
        14, 2.5e9, 14e6,
    )(me, *[held(x) for x in (normed, cot, read, mixed, *gains)])


def finish(me, mine, came, channels, width, nstate):
    return call(
        finish_kernel, "finish", 1, (1,),
        [whole(mine.shape)] * 2,
        [whole((channels, width)), whole((nstate, width)), whole((1, channels))],
        [
            jax.ShapeDtypeStruct((channels, width), f32), jax.ShapeDtypeStruct((nstate, width), f32),
            jax.ShapeDtypeStruct((1, channels), f32),
        ],
        [], 8, 1e6, 4e6,
    )(me, mine, came)


def swap(x, distance, count):
    return lax.ppermute(x, "seq", [(i, i ^ distance) for i in range(count)])


def narrow(x):
    return lax.reduce_precision(x, 8, 7)


def pick(bit, when_one, when_zero):
    return jnp.where(bit == 1, when_one, when_zero)


def tied(x, token):
    return lax.optimization_barrier((x, token))


def bit_of(me, level):
    return (me >> level) & 1


def shard_start(me, level, sensors):
    return sum(bit_of(me, k) * (sensors >> (k + 1)) for k in range(level + 1))


def row(ref, k):
    return ref[pl.ds(k, 1), :]


def rise_kernel(me_ref, own, tail, came, low_ref, low_tail_ref, tail_ref, next_ref, send_ref, other_tail, *, level, last):
    me = me_ref[0]
    bit = bit_of(me, level)
    size, nstate, width = own.shape
    sensors = tail.shape[0]
    start = shard_start(me, level, sensors)
    other_tail[...] = came[size * nstate :, :].astype(f32)
    low_tail_ref[...] = pick(bit, other_tail[...], tail[...])
    total_tail = tail[...] + other_tail[...]
    tail_ref[...] = total_tail

    def total(j):
        other = came[pl.ds(pl.multiple_of(j * nstate, nstate), nstate), :].astype(f32)
        low, high = pick(bit, other, own[j]), pick(bit, own[j], other)
        low_ref[j] = low
        fade = jnp.exp2(pick(bit, row(tail, start + j), row(other_tail, start + j)))
        return low * fade + high

    half = next_ref.shape[0]
    mine = 0 if last else bit_of(me, level + 1) * half
    for j in range(half):
        kept = total(mine + j)
        next_ref[j] = kept
        gone = kept if last else total(half - mine + j)
        send_ref[j * nstate : (j + 1) * nstate, :] = gone.astype(bf16)
    send_ref[half * nstate :, :] = total_tail.astype(bf16)


def rise(me, own, tail, came, level, last):
    size, nstate, width = own.shape
    half = size if last else size // 2
    return call(
        functools.partial(rise_kernel, level=level, last=last), "rise", 1, (),
        [HELD] * 3, [HELD] * 5,
        [
            pltpu.VMEM(own.shape, f32), pltpu.VMEM(tail.shape, f32), pltpu.VMEM(tail.shape, f32),
            pltpu.VMEM((half, nstate, width), f32), pltpu.VMEM((half * nstate + tail.shape[0], width), bf16),
        ],
        [pltpu.VMEM(tail.shape, f32)], 6, 1e6, 1e6,
    )(me, *[held(x) for x in (own, tail, came)])


def across_kernel(
    me_ref, own, tail, before, before_tail, came, next_ref, tail_ref, before_ref, before_tail_ref, send_ref, other_tail,
    *, level, shards,
):
    me = me_ref[0]
    bit = bit_of(me, level)
    size, nstate, width = own.shape
    start = shard_start(me, shards - 1, tail.shape[0])
    other_tail[...] = came[size * nstate :, :].astype(f32)
    before_tail_ref[...] = before_tail[...] + pick(bit, other_tail[...], jnp.zeros_like(other_tail))
    total_tail = tail[...] + other_tail[...]
    tail_ref[...] = total_tail
    for j in range(size):
        other = came[j * nstate : (j + 1) * nstate, :].astype(f32)
        passed = other * jnp.exp2(row(before_tail, start + j)) + before[j]
        before_ref[j] = pick(bit, passed, before[j])
        low, high = pick(bit, other, own[j]), pick(bit, own[j], other)
        total = low * jnp.exp2(pick(bit, row(tail, start + j), row(other_tail, start + j))) + high
        next_ref[j] = total
        send_ref[j * nstate : (j + 1) * nstate, :] = total.astype(bf16)
    send_ref[size * nstate :, :] = total_tail.astype(bf16)


def across(me, own, tail, before, before_tail, came, level, shards):
    return call(
        functools.partial(across_kernel, level=level, shards=shards), "across", 1, (),
        [HELD] * 5, [HELD] * 5,
        [
            pltpu.VMEM(own.shape, f32), pltpu.VMEM(tail.shape, f32), pltpu.VMEM(own.shape, f32),
            pltpu.VMEM(tail.shape, f32), pltpu.VMEM(came.shape, bf16),
        ],
        [pltpu.VMEM(tail.shape, f32)], 6, 1e6, 1e6,
    )(me, *[held(x) for x in (own, tail, before, before_tail, came)])


def fall_kernel(me_ref, *refs, level, first, last_across, ways):
    me = me_ref[0]
    lows, tails = refs[: level + 1], refs[level + 1 : 2 * (level + 1)]
    refs = refs[2 * (level + 1) :]
    sensors = tails[0].shape[0]
    low = lows[level]
    size, nstate, width = low.shape
    start = shard_start(me, level, sensors)

    def step(state, q, sensor):
        at = sensor - shard_start(me, q, sensors)
        return state * jnp.exp2(row(tails[q], sensor)) + lows[q][at]

    def split_at(j, before, state_ref, k):
        after = step(before, level, start + j)
        bit = bit_of(me, level)
        mine = pick(bit, after, before)
        mine_ref[j] = mine
        gone_ref[j] = pick(bit, before, after).astype(bf16)
        if state_ref is not None:
            for q in reversed(range(level)):
                mine = pick(bit_of(me, q), step(mine, q, start + j), mine)
            state_ref[k] = mine.astype(bf16)

    if first:
        came, mine_ref, gone_ref, state_ref = refs
        for j in range(size):
            if last_across is None:
                before = came[j]
            else:
                other = came[j * nstate : (j + 1) * nstate, :].astype(f32)
                before = pick(bit_of(me, last_across), other, jnp.zeros_like(other))
            split_at(j, before, state_ref, j)
    else:
        had, came, mine_ref, gone_ref, state_ref = refs
        half = size // 2
        at = bit_of(me, level + 1) * half
        for k in range(half):
            split_at(at + k, had[k], None, k)
            split_at(half - at + k, came[k].astype(f32), state_ref, k)


def fall(me, saved, level, had, came, last_across):
    lows = [low for low, _ in saved[: level + 1]]
    tails = [tail for _, tail in saved[: level + 1]]
    size, nstate, width = lows[level].shape
    first = had is None
    arrays = lows + tails + ([came] if first else [had, came])
    return call(
        functools.partial(fall_kernel, level=level, first=first, last_across=last_across, ways=len(saved)), "fall", 1, (),
        [HELD] * len(arrays), [HELD] * 3,
        [
            pltpu.VMEM((size, nstate, width), f32), pltpu.VMEM((size, nstate, width), bf16),
            pltpu.VMEM((size if first else size // 2, nstate, width), bf16),
        ],
        [], 6, 1e6, 1e6,
    )(me, *[held(x) for x in arrays])


def exchange(keep, send, tail, me, count, shards, swap_beside, ready):
    sensors = tail.shape[0]
    levels = count.bit_length() - 1
    own = keep
    saved = []
    for level in range(shards):
        came = swap_beside(send, level, True)
        low, low_tail, tail, own, send = rise(me, own, tail, came, level, level + 1 == shards)
        saved.append((low, low_tail))
    if levels == shards + 1:
        came = swap_beside(send, shards, True)
        parts = (None, came, shards)
    else:
        before, before_tail = jnp.zeros_like(own), jnp.zeros_like(tail)
        for level in range(shards, levels):
            came = swap_beside(send, level, True)
            own, tail, before, before_tail, send = across(me, own, tail, before, before_tail, came, level, shards)
        parts = (None, before, None)
    for level in reversed(range(shards)):
        mine, gone, states = fall(me, saved, level, *parts)

        def first(at, level=level):
            if level + 1 == shards:
                return shard_start(at, level, sensors)
            size = sensors >> (level + 2)
            return shard_start(at, level + 1, sensors) + pick(bit_of(at, level + 1), -size, size)

        ready(states, first, False)
        came = swap_beside(gone, level, False)
        parts = (mine, came, None)
    ready(came, lambda at: (1 - bit_of(at, 0)) * (sensors // 2), True)


def all_sum(keep, send, me, count, shards):
    levels = count.bit_length() - 1
    own = keep
    for level in range(shards):
        came = swap(send, 1 << level, count)
        own = own + came.astype(f32)
        if level + 1 < shards:
            bit = (me >> (level + 1)) & 1
            size = own.shape[0] // 2
            send = lax.dynamic_slice_in_dim(own, (1 - bit) * size, size, 0).astype(bf16)
            own = lax.dynamic_slice_in_dim(own, bit * size, size, 0)
    for level in range(shards, levels):
        own = narrow(own)
        own = own + swap(own.astype(bf16), 1 << level, count).astype(f32)
    out = own.astype(bf16)
    for level in reversed(range(1, shards)):
        bit = (me >> level) & 1
        came = swap(out, 1 << level, count)
        out = pick(bit, jnp.concatenate([came, out], axis=0), jnp.concatenate([out, came], axis=0))
    return out, swap(out, 1, count)


def per_device(
    count, readings, block_graph, cluster_of, mix_weight, boundaries, w_channels, w_state, w_step,
    step_bias, channel_fading_exponent, skip_gain, norm_gain, w_out, cotangent,
):
    sensors, span, width = readings.shape
    channels = w_channels.shape[1]
    nstate = w_state.shape[1] // 2
    me = lax.axis_index("seq").astype(jnp.int32)
    at = me[None]
    shards = min(max(count.bit_length() - 2, 1), 3)
    heads = skip_gain.shape[0]

    mixed, chans, maps, step, cum, cum_t, keep, send, tail, token, consts, cot, w_out = front(
        at, readings, block_graph, cluster_of, mix_weight, boundaries, w_channels, w_state, w_step,
        step_bias, channel_fading_exponent, skip_gain, norm_gain, cotangent, w_out,
    )
    work = {"token": token, "within": (), "back": (), "gains": [], "next": None}
    plan = {1: (0, 3), 2: (3, 2), 3: (5, 3)}

    def run_back():
        states, first = work["next"]
        part, scaled, decay, grad = work["within"]
        normed, read, gain, work["token"] = back(
            at, first, states, maps, scaled, decay, part, grad, cum, consts, work["back"], work["token"]
        )
        work["back"] = (normed, read)
        work["gains"].append(gain)

    def swap_beside(x, level, up):
        x, work["token"] = tied(x, work["token"])
        came = swap(x, 1 << level, count)
        if not up:
            run_back()
        elif level in plan:
            first, blocks = plan[level]
            *arrays, work["token"] = within(
                first, blocks, chans, maps, step, cum_t, cot, w_out, consts, heads, work["within"], work["token"]
            )
            work["within"] = tuple(arrays)
        return came

    def ready(states, first, last):
        work["next"] = (states, first)
        if last:
            run_back()

    exchange(keep, send, tail, at, count, shards, swap_beside, ready)
    keep_sum, send_sum = grads(at, work["back"][0], cot, work["back"][1], mixed, work["gains"])
    mine, came = all_sum(keep_sum, send_sum, me, count, shards)
    grad_out, grad_read, grad_gain = finish(at, mine, came, channels, width, nstate)
    return grad_out, grad_read.T, grad_gain[0]


def solution(mesh):
    in_specs = (
        P("groups", "seq", None), P("groups", None), P("groups"), P(), P(("groups", "seq")),
        P(), P(), P(), P(), P(), P(), P(), P(), P("groups", "seq", None),
    )
    out_specs = (P("groups", None), P("groups", None), P("groups"))
    return jax.shard_map(
        functools.partial(per_device, mesh.shape["seq"]),
        mesh=mesh, in_specs=in_specs, out_specs=out_specs, check_vma=False,
    )
```

```python
import functools
import math

import jax
import jax.numpy as jnp
from jax import lax
from jax.experimental import pallas as pl
from jax.experimental.pallas import tpu as pltpu
from jax.sharding import PartitionSpec as P

f32 = jnp.float32
bf16 = jnp.bfloat16
LOG2E = math.log2(math.e)
LOG_PULSE = math.log(0.7)
NT = (((1,), (1,)), ((), ()))
TN = (((0,), (0,)), ((), ()))


def dot(a, b, dims=(((1,), (0,)), ((), ()))):
    return lax.dot_general(a, b, dims, preferred_element_type=f32)


def split(x, terms):
    parts = []
    for _ in range(terms):
        part = x.astype(bf16)
        parts.append(part)
        x = x - part.astype(f32)
    return parts


def iota(shape, axis):
    return lax.broadcasted_iota(jnp.int32, shape, axis)


def spread_matrix(rows, heads, channels):
    size = channels // heads
    return (iota((rows, channels), 0) % heads == iota((rows, channels), 1) // size).astype(bf16)


def spread(values, sensor, heads, spread2):
    lane = iota(values.shape, 1)
    own = jnp.where(lane // heads == sensor, values, 0.0)
    return dot(jnp.concatenate(split(own, 2), axis=1), spread2)


def front_kernel(
    me_ref, readings_hbm, *refs, heads, chunk, n_small,
):
    hbm, refs = refs[:n_small], refs[n_small:]
    (mixed_ref, channels_ref, maps_ref, step_ref, cum_ref, cum_t_ref, keep_ref, send_ref, tail_ref, token_ref,
     consts_ref), refs = refs[:11], refs[11:]
    vmem, refs = refs[:n_small], refs[n_small:]
    readings, kmix, wms, spread2, state_sc, log_sc, scaled_sc, sems = refs
    graph, cluster, mix, marks, w_step_t, bias, fading_exponent, skip_gain, norm_gain, w_state, w_channels = vmem
    sensors, span, width = readings.shape
    rows = sensors * chunk
    maps = w_state.shape[1]
    nstate = maps // 2
    channels = w_channels.shape[1]
    lanes = sensors * heads
    chunks = span // chunk

    def reading_copy(k):
        part = pl.ds(k * chunk, chunk)
        return pltpu.make_async_copy(readings_hbm.at[:, part], readings.at[:, part], sems.at[n_small + k])

    copies = [pltpu.make_async_copy(hbm[k], vmem[k], sems.at[k]) for k in range(n_small)]
    for copy in copies[:-2]:
        copy.start()
    reading_copy(0).start()
    copies[-2].start()
    copies[-1].start()
    for k in range(1, chunks):
        reading_copy(k).start()

    token_ref[...] = jnp.zeros_like(token_ref)
    wms[...] = jnp.zeros_like(wms)
    spread2[...] = spread_matrix(spread2.shape[0], heads, channels)
    for copy in copies[:-2]:
        copy.wait()
    wms[:, maps : maps + heads] = w_step_t[...].astype(f32).T.astype(bf16)
    picked = (iota((sensors, sensors), 0) == cluster[...]).astype(bf16)
    linked = dot(dot(picked, graph[...].astype(f32).astype(bf16), TN).astype(bf16), picked)
    coupling = (linked * mix[...]).astype(bf16)
    sensor_of = (iota((rows, sensors), 0) // chunk == iota((rows, sensors), 1)).astype(bf16)
    full = dot(dot(sensor_of, coupling).astype(bf16), sensor_of, NT)
    same = iota((rows, rows), 0) % chunk == iota((rows, rows), 1) % chunk
    kmix[...] = jnp.where(same, full, 0.0).astype(bf16)
    tiled = (iota((heads, lanes), 1) % heads == iota((heads, lanes), 0)).astype(bf16)
    both = jnp.concatenate([bias[...], -jnp.exp(fading_exponent[...]) * LOG2E], axis=0)
    wide = sum(dot(part, tiled) for part in split(both, 3))
    bias_row, rate_row = wide[0:1], wide[1:2]
    consts_ref[...] = jnp.zeros_like(consts_ref)
    consts_ref[0:1, :] = sum(dot(part, spread2[0:heads, :]) for part in split(skip_gain[...], 3))
    consts_ref[1:2, :] = norm_gain[...]

    def mix_chunk(i):
        here = slice(i * chunk, (i + 1) * chunk)
        reading_copy(i).wait()
        x = readings[:, here, :].reshape(rows, width)
        mixed_ref[:, here, :] = (x.astype(f32) + dot(kmix[...], x)).astype(bf16).reshape(sensors, chunk, width)

    mix_chunk(0)
    copies[-2].wait()
    wms[:, 0:maps] = w_state[...]
    copies[-1].wait()
    for i in range(chunks):
        here = slice(i * chunk, (i + 1) * chunk)
        if i + 1 < chunks:
            mix_chunk(i + 1)
        mixed = mixed_ref[:, here, :].reshape(rows, width)
        small = dot(mixed, wms[...])
        channels_ref[:, here, :] = dot(mixed, w_channels[...]).astype(bf16).reshape(sensors, chunk, channels)
        maps_ref[:, here, :] = small[:, 0:maps].astype(bf16).reshape(sensors, chunk, maps)
        steps = small[:, maps:].reshape(sensors, chunk, lanes)
        packed = steps[0]
        for s in range(1, sensors):
            packed = packed + pltpu.roll(steps[s], heads * s, 1)
        raw = (packed + bias_row).astype(bf16).astype(f32)
        step = jnp.maximum(raw, 0.0) + jnp.log1p(jnp.exp(-jnp.abs(raw)))
        step_ref[here, :] = step
        log_sc[here, :] = rate_row * step

    at, to = iota((span, span), 0), iota((span, span), 1)
    marked = jnp.sum(jnp.where(at == to, marks[...].astype(f32), 0.0), axis=1, keepdims=True)
    log_decay = log_sc[...] + (LOG_PULSE * LOG2E) * marked
    lower = (at >= to).astype(bf16)
    cum = sum(dot(lower, part) for part in split(log_decay, 3))
    cum_ref[...] = cum
    cum_t_ref[...] = cum.T
    last = cum[span - 1 : span, :]
    weight = jnp.exp2(last - cum) * step_ref[...]

    def scale(s):
        scaled_sc[s % 4] = (channels_ref[s].astype(f32) * spread(weight, s, heads, spread2[...])).astype(bf16)

    scale(0)
    scale(1)
    for s in range(sensors):
        if s + 2 < sensors:
            scale(s + 2)
        state_sc[s] = dot(maps_ref[s], scaled_sc[s % 4], TN)[0:nstate]
    own = jnp.where(iota((sensors, lanes), 1) // heads == iota((sensors, lanes), 0), last, 0.0)
    tail = sum(dot(part, spread2[0:lanes, :]) for part in split(own, 3))
    tail_ref[...] = tail
    half = sensors // 2
    mine = (me_ref[0] & 1) * half
    other = half - mine
    keep_ref[...] = state_sc[pl.ds(mine, half)]
    send_ref[0 : half * nstate, :] = state_sc[pl.ds(other, half)].reshape(half * nstate, channels).astype(bf16)
    send_ref[half * nstate :, :] = tail.astype(bf16)


def pair_blocks(x, size):
    lane = iota(x.shape, 1)
    zero = jnp.zeros_like(x)
    return jnp.concatenate([jnp.where(lane < size, x, zero), jnp.where(lane >= size, x, zero)], axis=0)


def within_kernel(channels, maps, step, cum_t, consts, cot_hbm, w_out_hbm, *refs, heads, first, count, aliases):
    part_ref, scaled_ref, decay_ref, grad_ref, cot_ref, w_out_ref, _, spread2, sems = refs[aliases:]
    _, span, width = channels.shape
    nstate = maps.shape[2] // 2
    size = width // heads
    own = slice(first, first + count)
    cot_copy = pltpu.make_async_copy(cot_hbm.at[own], cot_ref.at[own], sems.at[0])
    if first == 0:
        w_out_copy = pltpu.make_async_copy(w_out_hbm, w_out_ref, sems.at[1])
        w_out_copy.start()
    cot_copy.start()
    spread2[...] = spread_matrix(spread2.shape[0], heads, width)

    def sensor(k, carry):
        s = first + k
        causal = iota((span, span), 0) >= iota((span, span), 1)
        chan = channels[s].astype(f32)
        scaled = (chan * spread(step[...], s, heads, spread2[...])).astype(bf16)
        scaled_ref[s] = scaled
        both = maps[s]
        scores = dot(both[:, nstate:], both[:, 0:nstate], NT)
        row = cum_t[pl.ds(pl.multiple_of(s * heads, heads), heads), :]
        col = row.T
        for pair in range(heads // 2):
            weighted = []
            for h in (2 * pair, 2 * pair + 1):
                gap = jnp.broadcast_to(col[:, h : h + 1], (span, span)) - row[h : h + 1, :]
                decay = jnp.exp2(jnp.where(causal, gap, -jnp.inf))
                decay_ref[s, h] = decay.astype(bf16)
                weighted.append((scores * decay).astype(bf16))
            lanes = slice(2 * pair * size, 2 * (pair + 1) * size)
            out = dot(jnp.concatenate(weighted, axis=1), pair_blocks(scaled[:, lanes], size))
            part_ref[s, :, lanes] = out + consts[0:1, lanes] * chan[:, lanes]
        return carry

    lax.fori_loop(0, count, sensor, 0, unroll=2)
    if first == 0:
        w_out_copy.wait()
    cot_copy.wait()
    grad = dot(cot_ref[own].reshape(count * span, cot_ref.shape[2]), w_out_ref[...], NT)
    grad_ref[own] = grad.reshape(count, span, width)


def back_kernel(me_ref, state, maps, scaled, decay, part, grad, cum, consts, *refs, heads, aliases, first):
    normed_ref, read_ref, gain_ref, _, spread2, fade_sc, carried_sc, spread_sc, back_sc, faded_sc = refs[aliases:]
    _, span, width = part.shape
    nstate = maps.shape[2] // 2
    size = width // heads
    at_once = carried_sc.shape[0]
    spread2[...] = spread_matrix(spread2.shape[0], heads, width)
    fade_sc[...] = jnp.exp2(cum[...])
    begin = first(me_ref[0])
    chunk = 32

    def carry_in(k, slot):
        s = begin + k
        carried_sc[slot] = dot(maps[s][:, nstate:], state[k])
        spread_sc[slot] = spread(fade_sc[...], s, heads, spread2[...])

    def normalize(k, slot, gain_sum):
        s = begin + k
        gain = consts[1:2, :]
        for c in range(0, span, chunk):
            rows = slice(c, c + chunk)
            fade = spread_sc[slot, rows, :]
            out = part[s, rows, :] + carried_sc[slot, rows, :] * fade
            inv = lax.rsqrt(jnp.mean(out * out, axis=-1, keepdims=True) + 1e-05)
            normed = out * inv
            normed_ref[s, rows, :] = (normed * gain).astype(bf16)
            g = grad[s, rows, :]
            gain_sum = gain_sum + jnp.sum((normed * g).reshape(chunk // 8, 8, width), axis=0)
            by_gain = g * gain
            mean = jnp.mean(by_gain * normed, axis=-1, keepdims=True)
            back = inv * (by_gain - normed * mean)
            back_sc[slot, rows, :] = back.astype(bf16)
            faded_sc[slot, rows, :] = (back * fade).astype(bf16)
        return gain_sum

    def read_out(k, slot):
        s = begin + k
        read = dot(faded_sc[slot], state[k], NT)
        pairs = jnp.zeros((span, span), f32)
        for pair in range(heads // 2):
            lanes = slice(2 * pair * size, 2 * (pair + 1) * size)
            both_heads = dot(back_sc[slot, :, lanes], pair_blocks(scaled[s, :, lanes], size), NT)
            pairs = pairs + both_heads[:, 0:span] * decay[s, 2 * pair].astype(f32)
            pairs = pairs + both_heads[:, span:] * decay[s, 2 * pair + 1].astype(f32)
        read_ref[s] = (read + dot(pairs.astype(bf16), maps[s][:, 0:nstate])).astype(bf16)

    def block(i, gain_sum):
        for slot in range(at_once):
            carry_in(i * at_once + slot, slot)
        for slot in range(at_once):
            gain_sum = normalize(i * at_once + slot, slot, gain_sum)
        for slot in range(at_once):
            read_out(i * at_once + slot, slot)
        return gain_sum

    gain_ref[...] = lax.fori_loop(0, state.shape[0] // at_once, block, jnp.zeros(gain_ref.shape, f32))


def grads_kernel(me_ref, normed, cot, read, mixed, *refs, starts, more, n_gains):
    if more:
        before, gains, (keep_ref, send_ref, total) = refs[0], refs[1 : 1 + n_gains], refs[1 + n_gains :]
    else:
        total = refs[0]
    block = normed.shape[0] // 4
    span, channels = normed.shape[1:]
    width, nstate = cot.shape[2], read.shape[2]
    piece = total.shape[1]
    pieces = width // piece
    rows = block * span
    blocks = [pl.ds(start, block) for start in starts(me_ref[0])]

    def put(at, size, value):
        total[at : at + size, :] = value + before[at : at + size, :] if more else value

    for j in range(pieces):
        lanes = slice(j * piece, (j + 1) * piece)
        put(j * channels, channels, sum(
            dot(normed[here].reshape(rows, channels), cot[here, :, lanes].reshape(rows, piece), TN) for here in blocks
        ))
        put(pieces * channels + j * nstate, nstate, sum(
            dot(read[here].reshape(rows, nstate), mixed[here, :, lanes].reshape(rows, piece), TN) for here in blocks
        ))
    if not more:
        return
    used = pieces * (channels + nstate)
    total[used:, :] = jnp.zeros((total.shape[0] - used, piece), f32)
    gain = sum(jnp.sum(ref[...], axis=0, keepdims=True) for ref in gains)
    for j in range(channels // piece):
        total[used + j : used + j + 1, :] = gain[:, j * piece : (j + 1) * piece]
    half = keep_ref.shape[0]
    mine = pl.multiple_of((me_ref[0] & 1) * half, 8)
    other = pl.multiple_of(half - (me_ref[0] & 1) * half, 8)
    keep_ref[...] = total[pl.ds(mine, half), :]
    send_ref[...] = total[pl.ds(other, half), :].astype(bf16)


def finish_kernel(me_ref, mine, came, out_ref, read_ref, gain_ref):
    channels, width = out_ref.shape
    nstate = read_ref.shape[0]
    half, piece = mine.shape
    pieces = width // piece

    def write(low, high):
        def rows(start, size):
            parts = []
            if start < half:
                parts.append(low[start : min(start + size, half), :])
            if start + size > half:
                parts.append(high[max(start - half, 0) : start + size - half, :])
            return jnp.concatenate([part.astype(f32) for part in parts], axis=0)

        for j in range(pieces):
            lanes = slice(j * piece, (j + 1) * piece)
            out_ref[:, lanes] = rows(j * channels, channels)
            read_ref[:, lanes] = rows(pieces * channels + j * nstate, nstate)
        tail = rows(pieces * (channels + nstate), 8)
        for j in range(channels // piece):
            gain_ref[:, j * piece : (j + 1) * piece] = tail[j : j + 1, :]

    pl.when(me_ref[0] & 1 == 0)(lambda: write(mine, came))
    pl.when(me_ref[0] & 1 == 1)(lambda: write(came, mine))


def whole(shape):
    return pl.BlockSpec(shape, lambda *_: (0,) * len(shape), pipeline_mode=pl.Buffered(1))


ANYWHERE = pl.BlockSpec(memory_space=pl.ANY)
HELD = pl.BlockSpec(memory_space=pltpu.VMEM)


def held(x):
    return pltpu.with_memory_space_constraint(x, pltpu.VMEM)


def call(body, name, scalars, grid, in_specs, out_specs, out_shape, scratch, vmem, flops, moved, aliases=None):
    return pl.pallas_call(
        body,
        name=name,
        grid_spec=pltpu.PrefetchScalarGridSpec(
            num_scalar_prefetch=scalars, grid=grid, in_specs=in_specs, out_specs=out_specs, scratch_shapes=scratch
        ),
        out_shape=out_shape,
        input_output_aliases=aliases or {},
        compiler_params=pltpu.CompilerParams(vmem_limit_bytes=vmem << 20),
        cost_estimate=pl.CostEstimate(flops=int(flops), bytes_accessed=int(moved), transcendentals=0),
    )


def front(me, readings, graph, cluster, mix, boundaries, w_channels, w_state, w_step, bias, fading_exponent, skip_gain, gain):
    sensors, span, width = readings.shape
    heads, channels, maps = w_step.shape[1], w_channels.shape[1], w_state.shape[1]
    nstate, lanes, chunk = maps // 2, sensors * heads, 16
    rows, half_rows = sensors * chunk, sensors // 2 * nstate
    small = [
        graph, cluster[None, :], mix, boundaries[None, :], w_step.T, bias[None, :], fading_exponent[None, :],
        skip_gain[None, :], gain[None, :], w_state, w_channels,
    ]
    outs = [
        ((sensors, span, width), bf16), ((sensors, span, channels), bf16), ((sensors, span, maps), bf16),
        ((span, lanes), f32), ((span, lanes), f32), ((lanes, span), f32),
        ((sensors // 2, nstate, channels), f32), ((half_rows + sensors, channels), bf16), ((sensors, channels), f32),
        ((8, 128), f32), ((8, channels), f32),
    ]
    return call(
        functools.partial(front_kernel, heads=heads, chunk=chunk, n_small=len(small)), "front", 1, (),
        [ANYWHERE] * (1 + len(small)),
        [HELD] * len(outs),
        [pltpu.VMEM(shape, dtype) for shape, dtype in outs],
        [pltpu.VMEM(x.shape, x.dtype) for x in small] + [
            pltpu.VMEM(readings.shape, bf16), pltpu.VMEM((rows, rows), bf16), pltpu.VMEM((width, maps + lanes), bf16),
            pltpu.VMEM((2 * lanes, channels), bf16), pltpu.VMEM((sensors, nstate, channels), f32),
            pltpu.VMEM((span, lanes), f32), pltpu.VMEM((4, span, channels), bf16),
            pltpu.SemaphoreType.DMA((len(small) + span // chunk,)),
        ],
        20, 5e9, 14e6,
    )(me, *[pltpu.with_memory_space_constraint(x, pltpu.HBM) for x in [readings] + small])


def within(first, count, channels, maps, step, cum_t, consts, cot, w_out, heads, done, token):
    sensors, span, width = channels.shape
    lanes = sensors * heads
    n_in = 7
    aliases = {n_in + k: k for k in range(len(done))}
    aliases[n_in + len(done)] = 6
    return call(
        functools.partial(within_kernel, heads=heads, first=first, count=count, aliases=len(done) + 1),
        "within", 0, (),
        [HELD] * 5 + [ANYWHERE] * 2 + [HELD] * len(done) + [ANYWHERE],
        [HELD] * 6 + [ANYWHERE],
        [
            pltpu.VMEM((sensors, span, width), f32), pltpu.VMEM((sensors, span, width), bf16),
            pltpu.VMEM((sensors, heads, span, span), bf16), pltpu.VMEM((sensors, span, width), f32),
            pltpu.VMEM(cot.shape, bf16), pltpu.VMEM(w_out.shape, bf16),
            jax.ShapeDtypeStruct(token.shape, token.dtype),
        ],
        [pltpu.VMEM((2 * lanes, width), bf16), pltpu.SemaphoreType.DMA((2,))],
        8, 3e8 * count, 1.5e6 * count, aliases,
    )(
        *[held(x) for x in (channels, maps, step, cum_t, consts)],
        *[pltpu.with_memory_space_constraint(x, pltpu.HBM) for x in (cot, w_out)], *[held(x) for x in done], token,
    )


def back(me, first, state, maps, scaled, decay, part, grad, cum, consts, done, token):
    sensors, span, width = part.shape
    heads, nmaps = decay.shape[1], maps.shape[2]
    nstate, lanes = nmaps // 2, sensors * heads
    count = state.shape[0]
    at_once = min(count, 4)
    n_in = 9
    aliases = {n_in + k: k for k in range(len(done))}
    aliases[n_in + len(done)] = 3
    return call(
        functools.partial(back_kernel, heads=heads, aliases=len(done) + 1, first=first), "back", 1, (),
        [HELD] * (n_in - 1 + len(done)) + [ANYWHERE],
        [HELD] * 3 + [ANYWHERE],
        [
            pltpu.VMEM((sensors, span, width), bf16), pltpu.VMEM((sensors, span, nstate), bf16),
            pltpu.VMEM((8, width), f32), jax.ShapeDtypeStruct(token.shape, token.dtype),
        ],
        [
            pltpu.VMEM((2 * lanes, width), bf16), pltpu.VMEM((span, lanes), f32),
            pltpu.VMEM((at_once, span, width), f32), pltpu.VMEM((at_once, span, width), f32),
            pltpu.VMEM((at_once, span, width), bf16), pltpu.VMEM((at_once, span, width), bf16),
        ],
        8, 3e8 * count, 1.5e6 * count, aliases,
    )(me, *[held(x) for x in (state, maps, scaled, decay, part, grad, cum, consts) + done], token)


def grads(me, normed, cot, read, mixed, starts, before, gains, token):
    channels, width, nstate = normed.shape[2], cot.shape[2], read.shape[2]
    piece = 256
    rows = -(-(width // piece * (channels + nstate) + channels // piece) // 128) * 128
    more = before is not None
    body = functools.partial(grads_kernel, starts=starts, more=more, n_gains=len(gains))
    if not more:

        def first(me_ref, normed, cot, read, mixed, _, total, __):
            body(me_ref, normed, cot, read, mixed, total)

        return call(
            first, "grads", 1, (), [HELD] * 4 + [ANYWHERE], [HELD, ANYWHERE],
            [pltpu.VMEM((rows, piece), f32), jax.ShapeDtypeStruct(token.shape, token.dtype)],
            [], 8, 1.2e9, 7e6, {5: 1},
        )(me, *[held(x) for x in (normed, cot, read, mixed)], token)
    return call(
        body, "grads", 1, (), [HELD] * (5 + len(gains)), [HELD] * 2,
        [pltpu.VMEM((rows // 2, piece), f32), pltpu.VMEM((rows // 2, piece), bf16)],
        [pltpu.VMEM((rows, piece), f32)], 12, 1.2e9, 7e6,
    )(me, *[held(x) for x in (normed, cot, read, mixed, before, *gains)])


def finish(me, mine, came, channels, width, nstate):
    return call(
        finish_kernel, "finish", 1, (1,),
        [whole(mine.shape)] * 2,
        [whole((channels, width)), whole((nstate, width)), whole((1, channels))],
        [
            jax.ShapeDtypeStruct((channels, width), f32), jax.ShapeDtypeStruct((nstate, width), f32),
            jax.ShapeDtypeStruct((1, channels), f32),
        ],
        [], 8, 1e6, 4e6,
    )(me, mine, came)


def swap(x, distance, count):
    return lax.ppermute(x, "seq", [(i, i ^ distance) for i in range(count)])


def narrow(x):
    return lax.reduce_precision(x, 8, 7)


def pick(bit, when_one, when_zero):
    return jnp.where(bit == 1, when_one, when_zero)


def tied(x, token):
    return lax.optimization_barrier((x, token))


def bit_of(me, level):
    return (me >> level) & 1


def shard_start(me, level, sensors):
    return sum(bit_of(me, k) * (sensors >> (k + 1)) for k in range(level + 1))


def row(ref, k):
    return ref[pl.ds(k, 1), :]


def rise_kernel(me_ref, own, tail, came, low_ref, low_tail_ref, tail_ref, next_ref, send_ref, other_tail, *, level, last):
    me = me_ref[0]
    bit = bit_of(me, level)
    size, nstate, width = own.shape
    sensors = tail.shape[0]
    start = shard_start(me, level, sensors)
    other_tail[...] = came[size * nstate :, :].astype(f32)
    low_tail_ref[...] = pick(bit, other_tail[...], tail[...])
    total_tail = tail[...] + other_tail[...]
    tail_ref[...] = total_tail

    def total(j):
        other = came[pl.ds(pl.multiple_of(j * nstate, nstate), nstate), :].astype(f32)
        low, high = pick(bit, other, own[j]), pick(bit, own[j], other)
        low_ref[j] = low
        fade = jnp.exp2(pick(bit, row(tail, start + j), row(other_tail, start + j)))
        return low * fade + high

    half = next_ref.shape[0]
    mine = 0 if last else bit_of(me, level + 1) * half
    for j in range(half):
        kept = total(mine + j)
        next_ref[j] = kept
        gone = kept if last else total(half - mine + j)
        send_ref[j * nstate : (j + 1) * nstate, :] = gone.astype(bf16)
    send_ref[half * nstate :, :] = total_tail.astype(bf16)


def rise(me, own, tail, came, level, last):
    size, nstate, width = own.shape
    half = size if last else size // 2
    return call(
        functools.partial(rise_kernel, level=level, last=last), "rise", 1, (),
        [HELD] * 3, [HELD] * 5,
        [
            pltpu.VMEM(own.shape, f32), pltpu.VMEM(tail.shape, f32), pltpu.VMEM(tail.shape, f32),
            pltpu.VMEM((half, nstate, width), f32), pltpu.VMEM((half * nstate + tail.shape[0], width), bf16),
        ],
        [pltpu.VMEM(tail.shape, f32)], 6, 1e6, 1e6,
    )(me, *[held(x) for x in (own, tail, came)])


def across_kernel(
    me_ref, own, tail, before, before_tail, came, next_ref, tail_ref, before_ref, before_tail_ref, send_ref, other_tail,
    *, level, shards,
):
    me = me_ref[0]
    bit = bit_of(me, level)
    size, nstate, width = own.shape
    start = shard_start(me, shards - 1, tail.shape[0])
    other_tail[...] = came[size * nstate :, :].astype(f32)
    before_tail_ref[...] = before_tail[...] + pick(bit, other_tail[...], jnp.zeros_like(other_tail))
    total_tail = tail[...] + other_tail[...]
    tail_ref[...] = total_tail
    for j in range(size):
        other = came[j * nstate : (j + 1) * nstate, :].astype(f32)
        passed = other * jnp.exp2(row(before_tail, start + j)) + before[j]
        before_ref[j] = pick(bit, passed, before[j])
        low, high = pick(bit, other, own[j]), pick(bit, own[j], other)
        total = low * jnp.exp2(pick(bit, row(tail, start + j), row(other_tail, start + j))) + high
        next_ref[j] = total
        send_ref[j * nstate : (j + 1) * nstate, :] = total.astype(bf16)
    send_ref[size * nstate :, :] = total_tail.astype(bf16)


def across(me, own, tail, before, before_tail, came, level, shards):
    return call(
        functools.partial(across_kernel, level=level, shards=shards), "across", 1, (),
        [HELD] * 5, [HELD] * 5,
        [
            pltpu.VMEM(own.shape, f32), pltpu.VMEM(tail.shape, f32), pltpu.VMEM(own.shape, f32),
            pltpu.VMEM(tail.shape, f32), pltpu.VMEM(came.shape, bf16),
        ],
        [pltpu.VMEM(tail.shape, f32)], 6, 1e6, 1e6,
    )(me, *[held(x) for x in (own, tail, before, before_tail, came)])


def fall_kernel(me_ref, *refs, level, first, across_level):
    me = me_ref[0]
    lows, tails = refs[: level + 1], refs[level + 1 : 2 * (level + 1)]
    refs = refs[2 * (level + 1) :]
    sensors = tails[0].shape[0]
    size, nstate, width = lows[level].shape
    start = shard_start(me, level, sensors)

    def step(state, q, sensor):
        return state * jnp.exp2(row(tails[q], sensor)) + lows[q][sensor - shard_start(me, q, sensors)]

    def choose(before, q, sensor):
        after = step(before, q, sensor)
        bit = bit_of(me, q)
        return pick(bit, after, before), pick(bit, before, after)

    def land(state, top, sensor, k):
        for q in reversed(range(1, top)):
            state, _ = choose(state, q, sensor)
        state, other = choose(state, 0, sensor)
        state_ref[k] = state.astype(bf16)
        other_ref[k] = other.astype(bf16)

    if level == 0:
        came, state_ref, other_ref = refs
        came_size = came.shape[0]
        came_start = shard_start(me, 1, sensors) + pick(bit_of(me, 1), -came_size, came_size)
        for k in range(came_size):
            land(came[k].astype(f32), 1, came_start + k, k)
        return
    if first:
        came, mine_ref, gone_ref, state_ref, other_ref = refs
        for j in range(size):
            if across_level is None:
                before = came[j]
            else:
                before = came[j * nstate : (j + 1) * nstate, :].astype(f32)
                before = pick(bit_of(me, across_level), before, jnp.zeros_like(before))
            mine, gone = choose(before, level, start + j)
            mine_ref[j] = mine
            gone_ref[j] = gone.astype(bf16)
            land(mine, level, start + j, j)
    else:
        had, came, mine_ref, gone_ref, state_ref, other_ref = refs
        half = size // 2
        at = bit_of(me, level + 1) * half
        for k in range(half):
            mine, gone = choose(had[k], level, start + at + k)
            mine_ref[at + k] = mine
            gone_ref[at + k] = gone.astype(bf16)
            mine, gone = choose(came[k].astype(f32), level, start + half - at + k)
            mine_ref[half - at + k] = mine
            gone_ref[half - at + k] = gone.astype(bf16)
            land(mine, level, start + half - at + k, k)


def fall(me, saved, level, had, came, across_level):
    lows = [low for low, _ in saved[: level + 1]]
    tails = [tail for _, tail in saved[: level + 1]]
    size, nstate, width = lows[level].shape
    first = had is None
    arrays = lows + tails + ([came] if first else [had, came])
    known = size if first and level else size // 2
    outs = [pltpu.VMEM((size, nstate, width), f32), pltpu.VMEM((size, nstate, width), bf16)] if level else []
    outs += [pltpu.VMEM((known, nstate, width), bf16)] * 2
    return call(
        functools.partial(fall_kernel, level=level, first=first, across_level=across_level), "fall", 1, (),
        [HELD] * len(arrays), [HELD] * len(outs), outs, [], 6, 1e6, 1e6,
    )(me, *[held(x) for x in arrays])


def exchange(keep, send, tail, me, count, shards, swap_beside, ready):
    sensors = tail.shape[0]
    levels = count.bit_length() - 1
    own = keep
    saved = []
    for level in range(shards):
        came = swap_beside(send, level)
        low, low_tail, tail, own, send = rise(me, own, tail, came, level, level + 1 == shards)
        saved.append((low, low_tail))
    if levels == shards + 1:
        parts = (None, swap_beside(send, shards), shards)
    else:
        before, before_tail = jnp.zeros_like(own), jnp.zeros_like(tail)
        for level in range(shards, levels):
            came = swap_beside(send, level)
            own, tail, before, before_tail, send = across(me, own, tail, before, before_tail, came, level, shards)
        parts = (None, before, None)

    def first_of(at, level):
        if level + 1 == shards:
            return shard_start(at, level, sensors)
        size = sensors >> (level + 2)
        return shard_start(at, level + 1, sensors) + pick(bit_of(at, level + 1), -size, size)

    for level in reversed(range(1, shards)):
        mine, gone, states, other = fall(me, saved, level, *parts)
        came = ready(states, other, functools.partial(first_of, level=level), level, gone)
        parts = (mine, came, None)
    states, other = fall(me, saved, 0, None, came, None)
    ready(states, other, functools.partial(first_of, level=0), 0, None)


def all_sum(keep, send, me, count):
    levels = count.bit_length() - 1
    own = keep + swap(send, 1, count).astype(f32)
    half = own.shape[0] // 2
    parts = [own[:half], own[half:]]
    orders = [(1, 2), (2, 1)]
    for turn in range(2):
        sent = []
        for part, order in zip(parts, orders):
            size = part.shape[0] // 2
            bit = bit_of(me, order[turn])
            gone = lax.dynamic_slice_in_dim(part, (1 - bit) * size, size, 0).astype(bf16)
            sent.append(swap(gone, 1 << order[turn], count))
        for k, order in enumerate(orders):
            size = parts[k].shape[0] // 2
            kept = lax.dynamic_slice_in_dim(parts[k], bit_of(me, order[turn]) * size, size, 0)
            parts[k] = kept + sent[k].astype(f32)
    both = jnp.concatenate(parts, axis=0)
    for level in range(3, levels):
        both = narrow(both)
        both = both + swap(both.astype(bf16), 1 << level, count).astype(f32)
    size = both.shape[0] // 2
    both = both.astype(bf16)
    parts = [both[:size], both[size:]]
    for turn in (1, 0):
        came = [swap(part, 1 << order[turn], count) for part, order in zip(parts, orders)]
        for k, order in enumerate(orders):
            bit = bit_of(me, order[turn])
            parts[k] = pick(
                bit, jnp.concatenate([came[k], parts[k]], axis=0), jnp.concatenate([parts[k], came[k]], axis=0)
            )
    out = jnp.concatenate(parts, axis=0)
    return out, swap(out, 1, count)


def per_device(
    count, readings, block_graph, cluster_of, mix_weight, boundaries, w_channels, w_state, w_step,
    step_bias, channel_fading_exponent, skip_gain, norm_gain, w_out, cotangent,
):
    sensors, span, width = readings.shape
    channels = w_channels.shape[1]
    nstate = w_state.shape[1] // 2
    me = lax.axis_index("seq").astype(jnp.int32)
    at = me[None]
    shards = 3
    heads = skip_gain.shape[0]

    mixed, chans, maps, step, cum, cum_t, keep, send, tail, token, consts = front(
        at, readings, block_graph, cluster_of, mix_weight, boundaries, w_channels, w_state, w_step,
        step_bias, channel_fading_exponent, skip_gain, norm_gain,
    )
    work = {"token": token, "within": (), "back": (), "gains": []}
    plan = {1: (0, 6), 2: (6, 4), 3: (10, 6)}

    def run_back(states, first):
        part, scaled, decay, grad = work["within"][:4]
        normed, read, gain, work["token"] = back(
            at, first, states, maps, scaled, decay, part, grad, cum, consts, work["back"], work["token"]
        )
        work["back"] = (normed, read)
        work["gains"].append(gain)

    def swap_beside(x, level):
        x, work["token"] = tied(x, work["token"])
        came = swap(x, 1 << level, count)
        if level in plan:
            first, size = plan[level]
            *arrays, work["token"] = within(
                first, size, chans, maps, step, cum_t, consts, cotangent, w_out, heads, work["within"], work["token"]
            )
            work["within"] = tuple(arrays)
            came, work["token"] = tied(came, work["token"])
        return came

    def known(level):
        def starts(where):
            size = sensors // 4
            for device in (where, where ^ 1):
                begin = shard_start(device, 1, sensors)
                yield begin if level else begin + pick(bit_of(device, 1), -size, size)

        return starts

    def ready(states, other, first, level, gone):
        if level:
            gone, work["token"] = tied(gone, work["token"])
            gone = swap(gone, 1 << level, count)
        came = swap(other, 1, count)
        run_back(states, first)
        run_back(came, lambda where: first(where ^ 1))
        if level == 1:
            work["total"], work["token"] = grads(
                at, work["back"][0], work["within"][4], work["back"][1], mixed, known(1), None, [], work["token"]
            )
        if level:
            gone, work["token"] = tied(gone, work["token"])
        return gone

    exchange(keep, send, tail, at, count, shards, swap_beside, ready)
    keep_sum, send_sum = grads(
        at, work["back"][0], work["within"][4], work["back"][1], mixed, known(0), work["total"], work["gains"], None
    )
    mine, came = all_sum(keep_sum, send_sum, me, count)
    grad_out, grad_read, grad_gain = finish(at, mine, came, channels, width, nstate)
    return grad_out, grad_read.T, grad_gain[0]


def solution(mesh):
    in_specs = (
        P("groups", "seq", None), P("groups", None), P("groups"), P(), P(("groups", "seq")),
        P(), P(), P(), P(), P(), P(), P(), P(), P("groups", "seq", None),
    )
    out_specs = (P("groups", None), P("groups", None), P("groups"))
    return jax.shard_map(
        functools.partial(per_device, mesh.shape["seq"]),
        mesh=mesh, in_specs=in_specs, out_specs=out_specs, check_vma=False,
    )
```

```python
import functools
import math

import jax
import jax.numpy as jnp
from jax import lax
from jax.experimental import pallas as pl
from jax.experimental.pallas import tpu as pltpu
from jax.sharding import PartitionSpec as P

f32 = jnp.float32
bf16 = jnp.bfloat16
LOG2E = math.log2(math.e)
LOG_PULSE = math.log(0.7)
NT = (((1,), (1,)), ((), ()))
TN = (((0,), (0,)), ((), ()))


def dot(a, b, dims=(((1,), (0,)), ((), ()))):
    return lax.dot_general(a, b, dims, preferred_element_type=f32)


def split(x, terms):
    parts = []
    for _ in range(terms):
        part = x.astype(bf16)
        parts.append(part)
        x = x - part.astype(f32)
    return parts


def iota(shape, axis):
    return lax.broadcasted_iota(jnp.int32, shape, axis)


def spread_matrix(rows, heads, channels):
    size = channels // heads
    return (iota((rows, channels), 0) % heads == iota((rows, channels), 1) // size).astype(bf16)


def spread(values, sensor, heads, spread2):
    lane = iota(values.shape, 1)
    own = jnp.where(lane // heads == sensor, values, 0.0)
    return dot(jnp.concatenate(split(own, 2), axis=1), spread2)


def front_kernel(
    me_ref, readings_hbm, *refs, heads, chunk, n_small,
):
    hbm, refs = refs[:n_small], refs[n_small:]
    (mixed_ref, channels_ref, maps_ref, step_ref, cum_ref, cum_t_ref, keep_ref, send_ref, tail_ref, token_ref,
     consts_ref), refs = refs[:11], refs[11:]
    vmem, refs = refs[:n_small], refs[n_small:]
    readings, kmix, wms, spread2, state_sc, log_sc, scaled_sc, sems = refs
    graph, cluster, mix, marks, w_step_t, bias, fading_exponent, skip_gain, norm_gain, w_state, w_channels = vmem
    sensors, span, width = readings.shape
    rows = sensors * chunk
    maps = w_state.shape[1]
    nstate = maps // 2
    channels = w_channels.shape[1]
    lanes = sensors * heads
    chunks = span // chunk

    def reading_copy(k):
        part = pl.ds(k * chunk, chunk)
        return pltpu.make_async_copy(readings_hbm.at[:, part], readings.at[:, part], sems.at[n_small + k])

    copies = [pltpu.make_async_copy(hbm[k], vmem[k], sems.at[k]) for k in range(n_small)]
    for copy in copies[:-2]:
        copy.start()
    reading_copy(0).start()
    copies[-2].start()
    copies[-1].start()
    for k in range(1, chunks):
        reading_copy(k).start()

    token_ref[...] = jnp.zeros_like(token_ref)
    wms[...] = jnp.zeros_like(wms)
    spread2[...] = spread_matrix(spread2.shape[0], heads, channels)
    for copy in copies[:-2]:
        copy.wait()
    wms[:, maps : maps + heads] = w_step_t[...].astype(f32).T.astype(bf16)
    picked = (iota((sensors, sensors), 0) == cluster[...]).astype(bf16)
    linked = dot(dot(picked, graph[...].astype(f32).astype(bf16), TN).astype(bf16), picked)
    coupling = (linked * mix[...]).astype(bf16)
    sensor_of = (iota((rows, sensors), 0) // chunk == iota((rows, sensors), 1)).astype(bf16)
    full = dot(dot(sensor_of, coupling).astype(bf16), sensor_of, NT)
    same = iota((rows, rows), 0) % chunk == iota((rows, rows), 1) % chunk
    kmix[...] = jnp.where(same, full, 0.0).astype(bf16)
    tiled = (iota((heads, lanes), 1) % heads == iota((heads, lanes), 0)).astype(bf16)
    both = jnp.concatenate([bias[...], -jnp.exp(fading_exponent[...]) * LOG2E], axis=0)
    wide = sum(dot(part, tiled) for part in split(both, 3))
    bias_row, rate_row = wide[0:1], wide[1:2]
    consts_ref[...] = jnp.zeros_like(consts_ref)
    consts_ref[0:1, :] = sum(dot(part, spread2[0:heads, :]) for part in split(skip_gain[...], 3))
    consts_ref[1:2, :] = norm_gain[...]

    def mix_chunk(i):
        here = slice(i * chunk, (i + 1) * chunk)
        reading_copy(i).wait()
        x = readings[:, here, :].reshape(rows, width)
        mixed_ref[:, here, :] = (x.astype(f32) + dot(kmix[...], x)).astype(bf16).reshape(sensors, chunk, width)

    mix_chunk(0)
    copies[-2].wait()
    wms[:, 0:maps] = w_state[...]
    copies[-1].wait()
    for i in range(chunks):
        here = slice(i * chunk, (i + 1) * chunk)
        if i + 1 < chunks:
            mix_chunk(i + 1)
        mixed = mixed_ref[:, here, :].reshape(rows, width)
        small = dot(mixed, wms[...])
        channels_ref[:, here, :] = dot(mixed, w_channels[...]).astype(bf16).reshape(sensors, chunk, channels)
        maps_ref[:, here, :] = small[:, 0:maps].astype(bf16).reshape(sensors, chunk, maps)
        steps = small[:, maps:].reshape(sensors, chunk, lanes)
        packed = steps[0]
        for s in range(1, sensors):
            packed = packed + pltpu.roll(steps[s], heads * s, 1)
        raw = (packed + bias_row).astype(bf16).astype(f32)
        step = jnp.maximum(raw, 0.0) + jnp.log1p(jnp.exp(-jnp.abs(raw)))
        step_ref[here, :] = step
        log_sc[here, :] = rate_row * step

    at, to = iota((span, span), 0), iota((span, span), 1)
    marked = jnp.sum(jnp.where(at == to, marks[...].astype(f32), 0.0), axis=1, keepdims=True)
    log_decay = log_sc[...] + (LOG_PULSE * LOG2E) * marked
    lower = (at >= to).astype(bf16)
    cum = sum(dot(lower, part) for part in split(log_decay, 3))
    cum_ref[...] = cum
    cum_t_ref[...] = cum.T
    last = cum[span - 1 : span, :]
    weight = jnp.exp2(last - cum) * step_ref[...]

    def scale(s):
        scaled_sc[s % 4] = (channels_ref[s].astype(f32) * spread(weight, s, heads, spread2[...])).astype(bf16)

    scale(0)
    scale(1)
    for s in range(sensors):
        if s + 2 < sensors:
            scale(s + 2)
        state_sc[s] = dot(maps_ref[s], scaled_sc[s % 4], TN)[0:nstate]
    own = jnp.where(iota((sensors, lanes), 1) // heads == iota((sensors, lanes), 0), last, 0.0)
    tail = sum(dot(part, spread2[0:lanes, :]) for part in split(own, 3))
    tail_ref[...] = tail
    half = sensors // 2
    mine = (me_ref[0] & 1) * half
    other = half - mine
    keep_ref[...] = state_sc[pl.ds(mine, half)]
    send_ref[0 : half * nstate, :] = state_sc[pl.ds(other, half)].reshape(half * nstate, channels).astype(bf16)
    send_ref[half * nstate :, :] = tail.astype(bf16)


def pair_blocks(x, size):
    lane = iota(x.shape, 1)
    zero = jnp.zeros_like(x)
    return jnp.concatenate([jnp.where(lane < size, x, zero), jnp.where(lane >= size, x, zero)], axis=0)


def within_kernel(channels, maps, step, cum_t, consts, cot_hbm, w_out_hbm, *refs, heads, first, count, aliases):
    part_ref, scaled_ref, decay_ref, grad_ref, cot_ref, w_out_ref, _, spread2, sems = refs[aliases:]
    _, span, width = channels.shape
    nstate = maps.shape[2] // 2
    size = width // heads
    own = slice(first, first + count)
    cot_copy = pltpu.make_async_copy(cot_hbm.at[own], cot_ref.at[own], sems.at[0])
    if first == 0:
        w_out_copy = pltpu.make_async_copy(w_out_hbm, w_out_ref, sems.at[1])
        w_out_copy.start()
    cot_copy.start()
    spread2[...] = spread_matrix(spread2.shape[0], heads, width)

    def sensor(k, carry):
        s = first + k
        causal = iota((span, span), 0) >= iota((span, span), 1)
        chan = channels[s].astype(f32)
        scaled = (chan * spread(step[...], s, heads, spread2[...])).astype(bf16)
        scaled_ref[s] = scaled
        both = maps[s]
        scores = dot(both[:, nstate:], both[:, 0:nstate], NT)
        row = cum_t[pl.ds(pl.multiple_of(s * heads, heads), heads), :]
        col = row.T
        for pair in range(heads // 2):
            weighted = []
            for h in (2 * pair, 2 * pair + 1):
                gap = jnp.broadcast_to(col[:, h : h + 1], (span, span)) - row[h : h + 1, :]
                decay = jnp.exp2(jnp.where(causal, gap, -jnp.inf))
                decay_ref[s, h] = decay.astype(bf16)
                weighted.append((scores * decay).astype(bf16))
            lanes = slice(2 * pair * size, 2 * (pair + 1) * size)
            out = dot(jnp.concatenate(weighted, axis=1), pair_blocks(scaled[:, lanes], size))
            part_ref[s, :, lanes] = out + consts[0:1, lanes] * chan[:, lanes]
        return carry

    lax.fori_loop(0, count, sensor, 0, unroll=2)
    if first == 0:
        w_out_copy.wait()
    cot_copy.wait()
    grad = dot(cot_ref[own].reshape(count * span, cot_ref.shape[2]), w_out_ref[...], NT)
    grad_ref[own] = grad.reshape(count, span, width)


def block_start(me, flips, sensors):
    return shard_start(me ^ flips, 2, sensors)


def back_kernel(me_ref, *refs, heads, blocks, aliases):
    states, refs = refs[0], refs[1:]
    maps, scaled, decay, part, grad, cum, consts = refs[:7]
    normed_ref, read_ref, gain_ref, _, spread2, fade_sc, carried_sc, spread_sc, back_sc, faded_sc = refs[7 + aliases :]
    sensors, span, width = part.shape
    nstate = maps.shape[2] // 2
    size = width // heads
    each = states.shape[0] // len(blocks)
    spread2[...] = spread_matrix(spread2.shape[0], heads, width)
    fade_sc[...] = jnp.exp2(cum[...])
    chunk = 32
    todo = [
        (block_start(me_ref[0], flips, sensors) + k, states, n * each + k)
        for n, flips in enumerate(blocks)
        for k in range(each)
    ]

    def carry_in(slot):
        s, state, k = todo[slot]
        carried_sc[slot] = dot(maps[s][:, nstate:], state[k])
        spread_sc[slot] = spread(fade_sc[...], s, heads, spread2[...])

    def normalize(slot, gain_sum):
        s = todo[slot][0]
        gain = consts[1:2, :]
        for c in range(0, span, chunk):
            rows = slice(c, c + chunk)
            fade = spread_sc[slot, rows, :]
            out = part[s, rows, :] + carried_sc[slot, rows, :] * fade
            inv = lax.rsqrt(jnp.mean(out * out, axis=-1, keepdims=True) + 1e-05)
            normed = out * inv
            normed_ref[s, rows, :] = (normed * gain).astype(bf16)
            g = grad[s, rows, :]
            gain_sum = gain_sum + jnp.sum((normed * g).reshape(chunk // 8, 8, width), axis=0)
            by_gain = g * gain
            mean = jnp.mean(by_gain * normed, axis=-1, keepdims=True)
            back = inv * (by_gain - normed * mean)
            back_sc[slot, rows, :] = back.astype(bf16)
            faded_sc[slot, rows, :] = (back * fade).astype(bf16)
        return gain_sum

    def read_out(slot):
        s, state, k = todo[slot]
        read = dot(faded_sc[slot], state[k], NT)
        pairs = jnp.zeros((span, span), f32)
        for pair in range(heads // 2):
            lanes = slice(2 * pair * size, 2 * (pair + 1) * size)
            both_heads = dot(back_sc[slot, :, lanes], pair_blocks(scaled[s, :, lanes], size), NT)
            pairs = pairs + both_heads[:, 0:span] * decay[s, 2 * pair].astype(f32)
            pairs = pairs + both_heads[:, span:] * decay[s, 2 * pair + 1].astype(f32)
        read_ref[s] = (read + dot(pairs.astype(bf16), maps[s][:, 0:nstate])).astype(bf16)

    gain_sum = jnp.zeros(gain_ref.shape, f32)
    for slot in range(len(todo)):
        carry_in(slot)
    for slot in range(len(todo)):
        gain_sum = normalize(slot, gain_sum)
    for slot in range(len(todo)):
        read_out(slot)
    gain_ref[...] = gain_sum


PIECE = 256


def grad_piece(normed, cot, read, mixed, blocks, piece):
    span, channels = normed.shape[1:]
    lanes = slice(piece * PIECE, (piece + 1) * PIECE)

    def product(left, right, start, size):
        here = pl.ds(start, size)
        rows = size * span
        return dot(left[here].reshape(rows, left.shape[2]), right[here, :, lanes].reshape(rows, PIECE), TN)

    return (
        sum(product(normed, cot, *block) for block in blocks),
        sum(product(read, mixed, *block) for block in blocks),
    )


def early_blocks(me, sensors):
    return [(block_start(me, flips, sensors), 2) for flips in (0, 1)]


def late_blocks(me, sensors):
    size = sensors // 4
    for other in (0, 1):
        yield block_start(me, 4 ^ other, sensors), 2
        yield shard_start(me ^ 2 ^ other, 1, sensors), size


def early_kernel(me_ref, normed, cot, read, mixed, _, total, __):
    channels, nstate = normed.shape[2], read.shape[2]
    for piece in range(total.shape[0]):
        out, into = grad_piece(normed, cot, read, mixed, early_blocks(me_ref[0], normed.shape[0]), piece)
        total[piece, 0:channels, :] = out
        total[piece, channels : channels + nstate, :] = into


def late_kernel(me_ref, normed, cot, read, mixed, before, *refs, part):
    *gains, keep_ref, send_ref, total = refs
    channels, nstate = normed.shape[2], read.shape[2]
    pieces = before.shape[0]
    own = channels // pieces
    bit = me_ref[0] & 1
    gain = sum(jnp.sum(ref[...], axis=0, keepdims=True) for ref in gains)
    for half in range(2):
        piece = half * (pieces // 2) + part
        out, into = grad_piece(normed, cot, read, mixed, list(late_blocks(me_ref[0], normed.shape[0])), piece)
        total[half, 0:channels, :] = out + before[piece, 0:channels, :]
        total[half, channels : channels + nstate, :] = into + before[piece, channels : channels + nstate, :]
        rest = total.shape[1] - channels - nstate
        total[half, channels + nstate :, :] = jnp.zeros((rest, PIECE), f32)
        total[half, channels + nstate : channels + nstate + 1, 0:own] = gain[:, piece * own : (piece + 1) * own]
    keep_ref[...] = total[bit]
    send_ref[...] = total[1 - bit].astype(bf16)


def finish_kernel(me_ref, mine, came, *refs, part, aliases):
    out_hbm, read_hbm, gain_hbm, out_sc, read_sc, gain_sc, sems = refs[aliases:]
    nstate = read_hbm.shape[0]
    channels, width = out_hbm.shape
    pieces = width // PIECE
    own = channels // pieces

    def write(halves):
        copies = []
        for half, rows in enumerate(halves):
            piece = half * (pieces // 2) + part
            out_sc[half] = rows[0:channels, :].astype(f32)
            read_sc[half] = rows[channels : channels + nstate, :].astype(f32)
            gain_sc[half] = rows[channels + nstate : channels + nstate + 1, 0:own].astype(f32)
            lanes = pl.ds(piece * PIECE, PIECE)
            copies += [
                pltpu.make_async_copy(out_sc.at[half], out_hbm.at[:, lanes], sems.at[half, 0]),
                pltpu.make_async_copy(read_sc.at[half], read_hbm.at[:, lanes], sems.at[half, 1]),
                pltpu.make_async_copy(gain_sc.at[half], gain_hbm.at[:, pl.ds(piece * own, own)], sems.at[half, 2]),
            ]
            for copy in copies[-3:]:
                copy.start()
        for copy in copies:
            copy.wait()

    pl.when(me_ref[0] & 1 == 0)(lambda: write((mine, came)))
    pl.when(me_ref[0] & 1 == 1)(lambda: write((came, mine)))


def whole(shape):
    return pl.BlockSpec(shape, lambda *_: (0,) * len(shape), pipeline_mode=pl.Buffered(1))


ANYWHERE = pl.BlockSpec(memory_space=pl.ANY)
HELD = pl.BlockSpec(memory_space=pltpu.VMEM)


def held(x):
    return pltpu.with_memory_space_constraint(x, pltpu.VMEM)


def call(body, name, scalars, grid, in_specs, out_specs, out_shape, scratch, vmem, flops, moved, aliases=None):
    return pl.pallas_call(
        body,
        name=name,
        grid_spec=pltpu.PrefetchScalarGridSpec(
            num_scalar_prefetch=scalars, grid=grid, in_specs=in_specs, out_specs=out_specs, scratch_shapes=scratch
        ),
        out_shape=out_shape,
        input_output_aliases=aliases or {},
        compiler_params=pltpu.CompilerParams(vmem_limit_bytes=vmem << 20),
        cost_estimate=pl.CostEstimate(flops=int(flops), bytes_accessed=int(moved), transcendentals=0),
    )


def front(me, readings, graph, cluster, mix, boundaries, w_channels, w_state, w_step, bias, fading_exponent, skip_gain, gain):
    sensors, span, width = readings.shape
    heads, channels, maps = w_step.shape[1], w_channels.shape[1], w_state.shape[1]
    nstate, lanes, chunk = maps // 2, sensors * heads, 16
    rows, half_rows = sensors * chunk, sensors // 2 * nstate
    small = [
        graph, cluster[None, :], mix, boundaries[None, :], w_step.T, bias[None, :], fading_exponent[None, :],
        skip_gain[None, :], gain[None, :], w_state, w_channels,
    ]
    outs = [
        ((sensors, span, width), bf16), ((sensors, span, channels), bf16), ((sensors, span, maps), bf16),
        ((span, lanes), f32), ((span, lanes), f32), ((lanes, span), f32),
        ((sensors // 2, nstate, channels), f32), ((half_rows + sensors, channels), bf16), ((sensors, channels), f32),
        ((8, 128), f32), ((8, channels), f32),
    ]
    return call(
        functools.partial(front_kernel, heads=heads, chunk=chunk, n_small=len(small)), "front", 1, (),
        [ANYWHERE] * (1 + len(small)),
        [HELD] * len(outs),
        [pltpu.VMEM(shape, dtype) for shape, dtype in outs],
        [pltpu.VMEM(x.shape, x.dtype) for x in small] + [
            pltpu.VMEM(readings.shape, bf16), pltpu.VMEM((rows, rows), bf16), pltpu.VMEM((width, maps + lanes), bf16),
            pltpu.VMEM((2 * lanes, channels), bf16), pltpu.VMEM((sensors, nstate, channels), f32),
            pltpu.VMEM((span, lanes), f32), pltpu.VMEM((4, span, channels), bf16),
            pltpu.SemaphoreType.DMA((len(small) + span // chunk,)),
        ],
        20, 5e9, 14e6,
    )(me, *[pltpu.with_memory_space_constraint(x, pltpu.HBM) for x in [readings] + small])


def within(first, count, channels, maps, step, cum_t, consts, cot, w_out, heads, done, token):
    sensors, span, width = channels.shape
    lanes = sensors * heads
    n_in = 7
    aliases = {n_in + k: k for k in range(len(done))}
    aliases[n_in + len(done)] = 6
    return call(
        functools.partial(within_kernel, heads=heads, first=first, count=count, aliases=len(done) + 1),
        "within", 0, (),
        [HELD] * 5 + [ANYWHERE] * 2 + [HELD] * len(done) + [ANYWHERE],
        [HELD] * 6 + [ANYWHERE],
        [
            pltpu.VMEM((sensors, span, width), f32), pltpu.VMEM((sensors, span, width), bf16),
            pltpu.VMEM((sensors, heads, span, span), bf16), pltpu.VMEM((sensors, span, width), f32),
            pltpu.VMEM(cot.shape, bf16), pltpu.VMEM(w_out.shape, bf16),
            jax.ShapeDtypeStruct(token.shape, token.dtype),
        ],
        [pltpu.VMEM((2 * lanes, width), bf16), pltpu.SemaphoreType.DMA((2,))],
        8, 3e8 * count, 1.5e6 * count, aliases,
    )(
        *[held(x) for x in (channels, maps, step, cum_t, consts)],
        *[pltpu.with_memory_space_constraint(x, pltpu.HBM) for x in (cot, w_out)], *[held(x) for x in done], token,
    )


def back(me, blocks, states, maps, scaled, decay, part, grad, cum, consts, done, token):
    sensors, span, width = part.shape
    heads, lanes = decay.shape[1], cum.shape[1]
    at_once = sum(state.shape[0] for state in states)
    n_in = 8 + len(states)
    aliases = {n_in + k: k for k in range(len(done))}
    aliases[n_in + len(done)] = 3
    return call(
        functools.partial(back_kernel, heads=heads, blocks=blocks, aliases=len(done) + 1), "back", 1, (),
        [HELD] * (n_in - 1 + len(done)) + [ANYWHERE],
        [HELD] * 3 + [ANYWHERE],
        [
            pltpu.VMEM((sensors, span, width), bf16), pltpu.VMEM((sensors, span, maps.shape[2] // 2), bf16),
            pltpu.VMEM((8, width), f32), jax.ShapeDtypeStruct(token.shape, token.dtype),
        ],
        [
            pltpu.VMEM((2 * lanes, width), bf16), pltpu.VMEM((span, lanes), f32),
            pltpu.VMEM((at_once, span, width), f32), pltpu.VMEM((at_once, span, width), f32),
            pltpu.VMEM((at_once, span, width), bf16), pltpu.VMEM((at_once, span, width), bf16),
        ],
        8, 3e8 * at_once, 1.5e6 * at_once, aliases,
    )(me, *[held(x) for x in (*states, maps, scaled, decay, part, grad, cum, consts) + done], token)


def grad_rows(channels, nstate):
    return -(-(channels + nstate + 1) // 32) * 32


def early_grads(me, normed, cot, read, mixed, token):
    rows = grad_rows(normed.shape[2], read.shape[2])
    return call(
        early_kernel, "early", 1, (), [HELD] * 4 + [ANYWHERE], [HELD, ANYWHERE],
        [pltpu.VMEM((cot.shape[2] // PIECE, rows, PIECE), f32), jax.ShapeDtypeStruct(token.shape, token.dtype)],
        [], 8, 6e8, 4e6, {5: 1},
    )(me, *[held(x) for x in (normed, cot, read, mixed)], token)


def late_grads(me, normed, cot, read, mixed, before, gains, part):
    rows = before.shape[1]
    return call(
        functools.partial(late_kernel, part=part), "late", 1, (), [HELD] * (5 + len(gains)), [HELD] * 2,
        [pltpu.VMEM((rows, PIECE), f32), pltpu.VMEM((rows, PIECE), bf16)],
        [pltpu.VMEM((2, rows, PIECE), f32)], 10, 8e8, 5e6,
    )(me, *[held(x) for x in (normed, cot, read, mixed, before, *gains)])


def finish(me, mine, came, part, channels, width, nstate, done):
    pieces = width // PIECE
    return call(
        functools.partial(finish_kernel, part=part, aliases=len(done)), "finish", 1, (),
        [HELD] * 2 + [ANYWHERE] * len(done), [ANYWHERE] * 3,
        [
            pltpu.HBM((channels, width), f32), pltpu.HBM((nstate, width), f32), pltpu.HBM((1, channels), f32),
        ],
        [
            pltpu.VMEM((2, channels, PIECE), f32), pltpu.VMEM((2, nstate, PIECE), f32),
            pltpu.VMEM((2, 1, channels // pieces), f32), pltpu.SemaphoreType.DMA((2, 3)),
        ],
        8, 1e6, 2e6, {3 + k: k for k in range(len(done))},
    )(me, held(mine), held(came), *[pltpu.with_memory_space_constraint(x, pltpu.HBM) for x in done])


def swap(x, distance, count):
    return lax.ppermute(x, "seq", [(i, i ^ distance) for i in range(count)])


def narrow(x):
    return lax.reduce_precision(x, 8, 7)


def pick(bit, when_one, when_zero):
    return jnp.where(bit == 1, when_one, when_zero)


def tied(x, token):
    return lax.optimization_barrier((x, token))


def bit_of(me, level):
    return (me >> level) & 1


def shard_start(me, level, sensors):
    return sum(bit_of(me, k) * (sensors >> (k + 1)) for k in range(level + 1))


def row(ref, k):
    return ref[pl.ds(k, 1), :]


def rise_kernel(me_ref, own, tail, came, low_ref, low_tail_ref, tail_ref, next_ref, send_ref, other_tail, *, level, last):
    me = me_ref[0]
    bit = bit_of(me, level)
    size, nstate, width = own.shape
    sensors = tail.shape[0]
    start = shard_start(me, level, sensors)
    other_tail[...] = came[size * nstate :, :].astype(f32)
    low_tail_ref[...] = pick(bit, other_tail[...], tail[...])
    total_tail = tail[...] + other_tail[...]
    tail_ref[...] = total_tail

    def total(j):
        other = came[pl.ds(pl.multiple_of(j * nstate, nstate), nstate), :].astype(f32)
        low, high = pick(bit, other, own[j]), pick(bit, own[j], other)
        low_ref[j] = low
        fade = jnp.exp2(pick(bit, row(tail, start + j), row(other_tail, start + j)))
        return low * fade + high

    half = next_ref.shape[0]
    mine = 0 if last else bit_of(me, level + 1) * half
    for j in range(half):
        kept = total(mine + j)
        next_ref[j] = kept
        gone = kept if last else total(half - mine + j)
        send_ref[j * nstate : (j + 1) * nstate, :] = gone.astype(bf16)
    send_ref[half * nstate :, :] = total_tail.astype(bf16)


def rise(me, own, tail, came, level, last):
    size, nstate, width = own.shape
    half = size if last else size // 2
    return call(
        functools.partial(rise_kernel, level=level, last=last), "rise", 1, (),
        [HELD] * 3, [HELD] * 5,
        [
            pltpu.VMEM(own.shape, f32), pltpu.VMEM(tail.shape, f32), pltpu.VMEM(tail.shape, f32),
            pltpu.VMEM((half, nstate, width), f32), pltpu.VMEM((half * nstate + tail.shape[0], width), bf16),
        ],
        [pltpu.VMEM(tail.shape, f32)], 6, 1e6, 1e6,
    )(me, *[held(x) for x in (own, tail, came)])


def across_kernel(
    me_ref, own, tail, before, before_tail, came, next_ref, tail_ref, before_ref, before_tail_ref, send_ref, other_tail,
    *, level, shards,
):
    me = me_ref[0]
    bit = bit_of(me, level)
    size, nstate, width = own.shape
    start = shard_start(me, shards - 1, tail.shape[0])
    other_tail[...] = came[size * nstate :, :].astype(f32)
    before_tail_ref[...] = before_tail[...] + pick(bit, other_tail[...], jnp.zeros_like(other_tail))
    total_tail = tail[...] + other_tail[...]
    tail_ref[...] = total_tail
    for j in range(size):
        other = came[j * nstate : (j + 1) * nstate, :].astype(f32)
        passed = other * jnp.exp2(row(before_tail, start + j)) + before[j]
        before_ref[j] = pick(bit, passed, before[j])
        low, high = pick(bit, other, own[j]), pick(bit, own[j], other)
        total = low * jnp.exp2(pick(bit, row(tail, start + j), row(other_tail, start + j))) + high
        next_ref[j] = total
        send_ref[j * nstate : (j + 1) * nstate, :] = total.astype(bf16)
    send_ref[size * nstate :, :] = total_tail.astype(bf16)


def across(me, own, tail, before, before_tail, came, level, shards):
    return call(
        functools.partial(across_kernel, level=level, shards=shards), "across", 1, (),
        [HELD] * 5, [HELD] * 5,
        [
            pltpu.VMEM(own.shape, f32), pltpu.VMEM(tail.shape, f32), pltpu.VMEM(own.shape, f32),
            pltpu.VMEM(tail.shape, f32), pltpu.VMEM(came.shape, bf16),
        ],
        [pltpu.VMEM(tail.shape, f32)], 6, 1e6, 1e6,
    )(me, *[held(x) for x in (own, tail, before, before_tail, came)])


def fall_kernel(me_ref, *refs, levels, sources, across_level, n_outs):
    me = me_ref[0]
    lows, tails = refs[:levels], refs[levels : 2 * levels]
    cames, outs = refs[2 * levels : 2 * levels + len(sources)], refs[2 * levels + len(sources) :]
    sensors = tails[0].shape[0]
    nstate = lows[0].shape[1]
    each = 2

    for n, ((flips, top), came) in enumerate(zip(sources, cames)):
        for k in range(each):
            sensor = block_start(me, flips, sensors) + k
            if len(came.shape) == 3:
                state = came[k].astype(f32)
            else:
                state = came[k * nstate : (k + 1) * nstate, :].astype(f32)
                state = pick(bit_of(me, across_level), state, jnp.zeros_like(state))
            for q in reversed(range(top)):
                after = state * jnp.exp2(row(tails[q], sensor)) + lows[q][sensor - shard_start(me, q, sensors)]
                bit = bit_of(me, q)
                other = pick(bit, state, after)
                state = pick(bit, after, state)
                if q == 0:
                    outs[1][n * each + k] = other.astype(bf16)
                else:
                    outs[1 + q][k] = other.astype(bf16)
            outs[0][n * each + k] = state.astype(bf16)


def fall(me, saved, sources, cames, across_level):
    levels = max(top for _, top in sources)
    lows = [low for low, _ in saved[:levels]]
    tails = [tail for _, tail in saved[:levels]]
    nstate, width = lows[0].shape[1:]
    arrays = lows + tails + cames
    outs = [pltpu.VMEM((2 * len(sources), nstate, width), bf16)] * 2 + [pltpu.VMEM((2, nstate, width), bf16)] * (levels - 1)
    return call(
        functools.partial(
            fall_kernel, levels=levels, sources=sources, across_level=across_level, n_outs=len(outs)
        ), "fall", 1, (), [HELD] * len(arrays), [HELD] * len(outs), outs, [], 6, 1e6, 1e6,
    )(me, *[held(x) for x in arrays])


SHARDED = 3


def rise_all(keep, send, tail, me, count, swap_beside):
    levels = count.bit_length() - 1
    own = keep
    saved = []
    for level in range(SHARDED):
        came = swap_beside(send, level)
        low, low_tail, tail, own, send = rise(me, own, tail, came, level, level + 1 == SHARDED)
        saved.append((low, low_tail))
    if levels == SHARDED + 1:
        return swap_beside(send, SHARDED), SHARDED, saved
    before, before_tail = jnp.zeros_like(own), jnp.zeros_like(tail)
    for level in range(SHARDED, levels):
        came = swap_beside(send, level)
        own, tail, before, before_tail, send = across(me, own, tail, before, before_tail, came, level, SHARDED)
    return before, None, saved


def halve_kernel(me_ref, part, came, kept_ref, gone_ref, *, level):
    size = kept_ref.shape[0]
    total = part[...] + came[...].astype(f32)
    bit = bit_of(me_ref[0], level)
    low, high = total[0:size], total[size:]
    kept_ref[...] = pick(bit, high, low)
    gone_ref[...] = pick(bit, low, high).astype(bf16)


def halve(me, part, came, level):
    shape = (part.shape[0] // 2, part.shape[1])
    return call(
        functools.partial(halve_kernel, level=level), "halve", 1, (), [HELD] * 2, [HELD] * 2,
        [pltpu.VMEM(shape, f32), pltpu.VMEM(shape, bf16)], [], 6, 1e6, 1e6,
    )(me, held(part), held(came))


def join_kernel(me_ref, part, came, out_ref, *, level):
    size = part.shape[0]
    bit = bit_of(me_ref[0], level)
    own, other = part[...].astype(f32), came[...].astype(f32)
    out_ref[0:size, :] = pick(bit, other, own).astype(bf16)
    out_ref[size:, :] = pick(bit, own, other).astype(bf16)


def join(me, part, came, level):
    return call(
        functools.partial(join_kernel, level=level), "join", 1, (), [HELD] * 2, [HELD],
        [pltpu.VMEM((2 * part.shape[0], part.shape[1]), bf16)], [], 6, 1e6, 1e6,
    )(me, held(part), held(came))[0]


def all_sum(keep, send, me, count, order):
    levels = count.bit_length() - 1
    part, came = keep, swap(send, 1, count)
    for level in order:
        part, gone = halve(me, part, came, level)
        came = swap(gone, 1 << level, count)
    part = part + came.astype(f32)
    for level in range(SHARDED, levels):
        part = narrow(part)
        part = part + swap(part.astype(bf16), 1 << level, count).astype(f32)
    part = part.astype(bf16)
    for level in reversed(order):
        part = join(me, part, swap(part, 1 << level, count), level)
    return part, swap(part, 1, count)


def per_device(
    count, readings, block_graph, cluster_of, mix_weight, boundaries, w_channels, w_state, w_step,
    step_bias, channel_fading_exponent, skip_gain, norm_gain, w_out, cotangent,
):
    sensors, span, width = readings.shape
    channels = w_channels.shape[1]
    nstate = w_state.shape[1] // 2
    me = lax.axis_index("seq").astype(jnp.int32)
    at = me[None]
    heads = skip_gain.shape[0]

    mixed, chans, maps, step, cum, cum_t, keep, send, tail, token, consts = front(
        at, readings, block_graph, cluster_of, mix_weight, boundaries, w_channels, w_state, w_step,
        step_bias, channel_fading_exponent, skip_gain, norm_gain,
    )
    work = {"token": token, "within": (), "back": (), "gains": []}
    plan = {1: (0, 6), 2: (6, 4), 3: (10, 6)}

    def run_back(blocks, *states):
        part, scaled, decay, grad = work["within"][:4]
        normed, read, gain, work["token"] = back(
            at, blocks, states, maps, scaled, decay, part, grad, cum, consts, work["back"], work["token"]
        )
        work["back"] = (normed, read)
        work["gains"].append(gain)

    def tie(x):
        x, work["token"] = tied(x, work["token"])
        return x

    def swap_beside(x, level):
        came = swap(tie(x), 1 << level, count)
        if level in plan:
            first, size = plan[level]
            *arrays, work["token"] = within(
                first, size, chans, maps, step, cum_t, consts, cotangent, w_out, heads, work["within"], work["token"]
            )
            work["within"] = tuple(arrays)
            came = tie(came)
        return came

    came, across_level, saved = rise_all(keep, send, tail, at, count, swap_beside)
    states, to_core, to_one, to_two = fall(at, saved, [(0, 3)], [came], across_level)
    to_core, to_one, to_two = tie((to_core, to_one, to_two))
    from_two, from_one, core = swap(to_two, 4, count), swap(to_one, 2, count), swap(to_core, 1, count)
    run_back((0,), states)
    run_back((1,), core)
    cot = work["within"][4]
    early, work["token"] = early_grads(at, work["back"][0], cot, work["back"][1], mixed, work["token"])
    from_two, from_one = tie((from_two, from_one))
    states, to_core, to_one = fall(at, saved, [(4, 2), (2, 1)], [from_two, from_one], None)
    to_core, to_one = tie((to_core, to_one))
    from_one, core = swap(to_one, 2, count), swap(to_core, 1, count)
    run_back((4, 2), states)
    run_back((5, 3), core)
    from_one = tie(from_one)
    states, to_core = fall(at, saved, [(6, 1)], [from_one], None)
    core = swap(tie(to_core), 1, count)
    run_back((6,), states)
    run_back((7,), core)
    results = ()
    sums = []
    for part, order in ((0, (1, 2)), (1, (2, 1))):
        keep_part, send_part = late_grads(
            at, work["back"][0], cot, work["back"][1], mixed, early, work["gains"], part
        )
        sums.append(all_sum(keep_part, send_part, at, count, order))
    for part in (0, 1):
        results = finish(at, *sums[part], part, channels, width, nstate, tuple(results))
    grad_out, grad_read, grad_gain = results
    return grad_out, grad_read.T, grad_gain[0]


def solution(mesh):
    in_specs = (
        P("groups", "seq", None), P("groups", None), P("groups"), P(), P(("groups", "seq")),
        P(), P(), P(), P(), P(), P(), P(), P(), P("groups", "seq", None),
    )
    out_specs = (P("groups", None), P("groups", None), P("groups"))
    return jax.shard_map(
        functools.partial(per_device, mesh.shape["seq"]),
        mesh=mesh, in_specs=in_specs, out_specs=out_specs, check_vma=False,
    )
```

```python
import functools
import math

import jax
import jax.numpy as jnp
from jax import lax
from jax.experimental import pallas as pl
from jax.experimental.pallas import tpu as pltpu
from jax.sharding import PartitionSpec as P

f32 = jnp.float32
bf16 = jnp.bfloat16
LOG2E = math.log2(math.e)
LOG_PULSE = math.log(0.7)
NT = (((1,), (1,)), ((), ()))
TN = (((0,), (0,)), ((), ()))


def dot(a, b, dims=(((1,), (0,)), ((), ()))):
    return lax.dot_general(a, b, dims, preferred_element_type=f32)


def split(x, terms):
    parts = []
    for _ in range(terms):
        part = x.astype(bf16)
        parts.append(part)
        x = x - part.astype(f32)
    return parts


def iota(shape, axis):
    return lax.broadcasted_iota(jnp.int32, shape, axis)


def spread_matrix(rows, heads, channels):
    size = channels // heads
    return (iota((rows, channels), 0) % heads == iota((rows, channels), 1) // size).astype(bf16)


def spread(values, sensor, heads, spread2):
    lane = iota(values.shape, 1)
    own = jnp.where(lane // heads == sensor, values, 0.0)
    return dot(jnp.concatenate(split(own, 2), axis=1), spread2)


def front_kernel(
    me_ref, readings_hbm, *refs, heads, chunk, n_small,
):
    hbm, refs = refs[:n_small], refs[n_small:]
    (mixed_ref, channels_ref, maps_ref, step_ref, cum_ref, cum_t_ref, keep_ref, send_ref, tail_ref, token_ref,
     consts_ref), refs = refs[:11], refs[11:]
    vmem, refs = refs[:n_small], refs[n_small:]
    readings, kmix, wms, spread2, log_sc, scaled_sc, sems = refs
    graph, cluster, mix, marks, w_step_t, bias, fading_exponent, skip_gain, norm_gain, w_state, w_channels = vmem
    sensors, span, width = readings.shape
    rows = sensors * chunk
    maps = w_state.shape[1]
    nstate = maps // 2
    channels = w_channels.shape[1]
    lanes = sensors * heads
    chunks = span // chunk

    def reading_copy(k):
        part = pl.ds(k * chunk, chunk)
        return pltpu.make_async_copy(readings_hbm.at[:, part], readings.at[:, part], sems.at[n_small + k])

    copies = [pltpu.make_async_copy(hbm[k], vmem[k], sems.at[k]) for k in range(n_small)]
    for copy in copies[:-2]:
        copy.start()
    reading_copy(0).start()
    copies[-2].start()
    copies[-1].start()
    for k in range(1, chunks):
        reading_copy(k).start()

    token_ref[...] = jnp.zeros_like(token_ref)
    wms[...] = jnp.zeros_like(wms)
    spread2[...] = spread_matrix(spread2.shape[0], heads, channels)
    for copy in copies[:-2]:
        copy.wait()
    wms[:, maps : maps + heads] = w_step_t[...].astype(f32).T.astype(bf16)
    picked = (iota((sensors, sensors), 0) == cluster[...]).astype(bf16)
    sensor_of = (iota((sensors, rows), 1) // chunk == iota((sensors, rows), 0)).astype(bf16)
    linked = dot(dot(picked, graph[...].astype(f32).astype(bf16), TN).astype(bf16), dot(picked, sensor_of).astype(bf16))
    coupling = (linked * sum(dot(part, sensor_of) for part in split(mix[...], 3))).astype(bf16).astype(f32)
    full = jnp.broadcast_to(coupling[:, None, :], (sensors, chunk, rows)).reshape(rows, rows)
    same = iota((rows, rows), 0) % chunk == iota((rows, rows), 1) % chunk
    kmix[...] = jnp.where(same, full, 0.0).astype(bf16)
    tiled = (iota((heads, lanes), 1) % heads == iota((heads, lanes), 0)).astype(bf16)
    both = jnp.concatenate([bias[...], -jnp.exp(fading_exponent[...]) * LOG2E], axis=0)
    wide = sum(dot(part, tiled) for part in split(both, 3))
    bias_row, rate_row = wide[0:1], wide[1:2]
    consts_ref[...] = jnp.zeros_like(consts_ref)
    consts_ref[0:1, :] = sum(dot(part, spread2[0:heads, :]) for part in split(skip_gain[...], 3))
    consts_ref[1:2, :] = norm_gain[...]

    def mix_chunk(i):
        here = slice(i * chunk, (i + 1) * chunk)
        reading_copy(i).wait()
        x = readings[:, here, :].reshape(rows, width)
        mixed_ref[:, here, :] = (x.astype(f32) + dot(kmix[...], x)).astype(bf16).reshape(sensors, chunk, width)

    mix_chunk(0)
    copies[-2].wait()
    wms[:, 0:maps] = w_state[...]
    copies[-1].wait()
    for i in range(chunks):
        here = slice(i * chunk, (i + 1) * chunk)
        if i + 1 < chunks:
            mix_chunk(i + 1)
        mixed = mixed_ref[:, here, :].reshape(rows, width)
        small = dot(mixed, wms[...])
        channels_ref[:, here, :] = dot(mixed, w_channels[...]).astype(bf16).reshape(sensors, chunk, channels)
        maps_ref[:, here, :] = small[:, 0:maps].astype(bf16).reshape(sensors, chunk, maps)
        steps = small[:, maps:].reshape(sensors, chunk, lanes)
        packed = steps[0]
        for s in range(1, sensors):
            packed = packed + pltpu.roll(steps[s], heads * s, 1)
        raw = (packed + bias_row).astype(bf16).astype(f32)
        step = jnp.maximum(raw, 0.0) + jnp.log1p(jnp.exp(-jnp.abs(raw)))
        step_ref[here, :] = step
        log_sc[here, :] = rate_row * step

    at, to = iota((span, span), 0), iota((span, span), 1)
    marked = jnp.sum(jnp.where(at == to, marks[...].astype(f32), 0.0), axis=1, keepdims=True)
    log_decay = log_sc[...] + (LOG_PULSE * LOG2E) * marked
    lower = (at >= to).astype(bf16)
    cum = sum(dot(lower, part) for part in split(log_decay, 3))
    cum_ref[...] = cum
    cum_t_ref[...] = cum.T
    last = cum[span - 1 : span, :]
    weight = jnp.exp2(last - cum) * step_ref[...]

    half = sensors // 2
    mine = (me_ref[0] & 1) * half

    def sensor_at(n):
        return (half - mine if n < half else mine - half) + n

    def scale(n):
        s = sensor_at(n)
        scaled_sc[n % 4] = (channels_ref[s].astype(f32) * spread(weight, s, heads, spread2[...])).astype(bf16)

    own = jnp.where(iota((sensors, lanes), 1) // heads == iota((sensors, lanes), 0), last, 0.0)
    tail = sum(dot(part, spread2[0:lanes, :]) for part in split(own, 3))
    tail_ref[...] = tail
    send_ref[half * nstate :, :] = tail.astype(bf16)
    scale(0)
    scale(1)
    for n in range(sensors):
        if n + 2 < sensors:
            scale(n + 2)
        state = dot(maps_ref[sensor_at(n)], scaled_sc[n % 4], TN)[0:nstate]
        if n < half:
            send_ref[n * nstate : (n + 1) * nstate, :] = state.astype(bf16)
        else:
            keep_ref[n - half] = state


def pair_blocks(x, size):
    lane = iota(x.shape, 1)
    zero = jnp.zeros_like(x)
    return jnp.concatenate([jnp.where(lane < size, x, zero), jnp.where(lane >= size, x, zero)], axis=0)


def within_kernel(channels, maps, step, cum_t, consts, cot_hbm, w_out_hbm, *refs, heads, first, count, aliases):
    part_ref, scaled_ref, decay_ref, grad_ref, cot_ref, w_out_ref, _, spread2, sems = refs[aliases:]
    _, span, width = channels.shape
    nstate = maps.shape[2] // 2
    size = width // heads
    own = slice(first, first + count)
    cot_copy = pltpu.make_async_copy(cot_hbm.at[own], cot_ref.at[own], sems.at[0])
    if first == 0:
        w_out_copy = pltpu.make_async_copy(w_out_hbm, w_out_ref, sems.at[1])
        w_out_copy.start()
    cot_copy.start()
    spread2[...] = spread_matrix(spread2.shape[0], heads, width)

    def sensor(k, carry):
        s = first + k
        causal = iota((span, span), 0) >= iota((span, span), 1)
        chan = channels[s].astype(f32)
        scaled = (chan * spread(step[...], s, heads, spread2[...])).astype(bf16)
        scaled_ref[s] = scaled
        both = maps[s]
        scores = dot(both[:, nstate:], both[:, 0:nstate], NT)
        row = cum_t[pl.ds(pl.multiple_of(s * heads, heads), heads), :]
        col = row.T
        for pair in range(heads // 2):
            weighted = []
            for h in (2 * pair, 2 * pair + 1):
                gap = jnp.broadcast_to(col[:, h : h + 1], (span, span)) - row[h : h + 1, :]
                decay = jnp.exp2(jnp.where(causal, gap, -jnp.inf))
                decay_ref[s, h] = decay.astype(bf16)
                weighted.append((scores * decay).astype(bf16))
            lanes = slice(2 * pair * size, 2 * (pair + 1) * size)
            out = dot(jnp.concatenate(weighted, axis=1), pair_blocks(scaled[:, lanes], size))
            part_ref[s, :, lanes] = out + consts[0:1, lanes] * chan[:, lanes]
        return carry

    lax.fori_loop(0, count, sensor, 0, unroll=2)
    if first == 0:
        w_out_copy.wait()
    cot_copy.wait()
    grad = dot(cot_ref[own].reshape(count * span, cot_ref.shape[2]), w_out_ref[...], NT)
    grad_ref[own] = grad.reshape(count, span, width)


def block_start(me, flips, sensors):
    return shard_start(me ^ flips, 2, sensors)


def back_kernel(me_ref, *refs, heads, blocks, aliases):
    states, refs = refs[0], refs[1:]
    maps, scaled, decay, part, grad, cum, consts = refs[:7]
    normed_ref, read_ref, gain_ref, _, spread2, fade_sc, carried_sc, spread_sc, back_sc, faded_sc = refs[7 + aliases :]
    sensors, span, width = part.shape
    nstate = maps.shape[2] // 2
    size = width // heads
    each = states.shape[0] // len(blocks)
    spread2[...] = spread_matrix(spread2.shape[0], heads, width)
    fade_sc[...] = jnp.exp2(cum[...])
    chunk = 32
    todo = [
        (block_start(me_ref[0], flips, sensors) + k, states, n * each + k)
        for n, flips in enumerate(blocks)
        for k in range(each)
    ]

    def carry_in(slot):
        s, state, k = todo[slot]
        carried_sc[slot] = dot(maps[s][:, nstate:], state[k])
        spread_sc[slot] = spread(fade_sc[...], s, heads, spread2[...])

    def normalize(slot, gain_sum):
        s = todo[slot][0]
        gain = consts[1:2, :]
        for c in range(0, span, chunk):
            rows = slice(c, c + chunk)
            fade = spread_sc[slot, rows, :]
            out = part[s, rows, :] + carried_sc[slot, rows, :] * fade
            inv = lax.rsqrt(jnp.mean(out * out, axis=-1, keepdims=True) + 1e-05)
            normed = out * inv
            normed_ref[s, rows, :] = (normed * gain).astype(bf16)
            g = grad[s, rows, :]
            gain_sum = gain_sum + jnp.sum((normed * g).reshape(chunk // 8, 8, width), axis=0)
            by_gain = g * gain
            mean = jnp.mean(by_gain * normed, axis=-1, keepdims=True)
            back = inv * (by_gain - normed * mean)
            back_sc[slot, rows, :] = back.astype(bf16)
            faded_sc[slot, rows, :] = (back * fade).astype(bf16)
        return gain_sum

    def read_out(slot):
        s, state, k = todo[slot]
        read = dot(faded_sc[slot], state[k], NT)
        pairs = jnp.zeros((span, span), f32)
        for pair in range(heads // 2):
            lanes = slice(2 * pair * size, 2 * (pair + 1) * size)
            both_heads = dot(back_sc[slot, :, lanes], pair_blocks(scaled[s, :, lanes], size), NT)
            pairs = pairs + both_heads[:, 0:span] * decay[s, 2 * pair].astype(f32)
            pairs = pairs + both_heads[:, span:] * decay[s, 2 * pair + 1].astype(f32)
        read_ref[s] = (read + dot(pairs.astype(bf16), maps[s][:, 0:nstate])).astype(bf16)

    gain_sum = jnp.zeros(gain_ref.shape, f32)
    for slot in range(len(todo)):
        carry_in(slot)
    for slot in range(len(todo)):
        gain_sum = normalize(slot, gain_sum)
    for slot in range(len(todo)):
        read_out(slot)
    gain_ref[...] = gain_sum


PIECE = 256


def grad_piece(normed, cot, read, mixed, blocks, piece):
    span, channels = normed.shape[1:]
    lanes = slice(piece * PIECE, (piece + 1) * PIECE)

    def product(left, right, start, size):
        here = pl.ds(start, size)
        rows = size * span
        return dot(left[here].reshape(rows, left.shape[2]), right[here, :, lanes].reshape(rows, PIECE), TN)

    return (
        sum(product(normed, cot, *block) for block in blocks),
        sum(product(read, mixed, *block) for block in blocks),
    )


def early_blocks(me, sensors):
    return [(block_start(me, flips, sensors), 2) for flips in (0, 1)]


def late_blocks(me, sensors):
    size = sensors // 4
    for other in (0, 1):
        yield block_start(me, 4 ^ other, sensors), 2
        yield shard_start(me ^ 2 ^ other, 1, sensors), size


def early_kernel(me_ref, normed, cot, read, mixed, _, total, __):
    channels, nstate = normed.shape[2], read.shape[2]
    for piece in range(total.shape[0]):
        out, into = grad_piece(normed, cot, read, mixed, early_blocks(me_ref[0], normed.shape[0]), piece)
        total[piece, 0:channels, :] = out
        total[piece, channels : channels + nstate, :] = into


def late_kernel(me_ref, normed, cot, read, mixed, before, *refs, part):
    *gains, keep_ref, send_ref, total = refs
    channels, nstate = normed.shape[2], read.shape[2]
    pieces = before.shape[0]
    own = channels // pieces
    bit = me_ref[0] & 1
    gain = sum(jnp.sum(ref[...], axis=0, keepdims=True) for ref in gains)
    for half in range(2):
        piece = half * (pieces // 2) + part
        out, into = grad_piece(normed, cot, read, mixed, list(late_blocks(me_ref[0], normed.shape[0])), piece)
        total[half, 0:channels, :] = out + before[piece, 0:channels, :]
        total[half, channels : channels + nstate, :] = into + before[piece, channels : channels + nstate, :]
        rest = total.shape[1] - channels - nstate
        total[half, channels + nstate :, :] = jnp.zeros((rest, PIECE), f32)
        total[half, channels + nstate : channels + nstate + 1, 0:own] = gain[:, piece * own : (piece + 1) * own]
    keep_ref[...] = total[bit]
    send_ref[...] = total[1 - bit].astype(bf16)


def finish_kernel(me_ref, mine, came, *refs, part, aliases):
    out_hbm, read_hbm, gain_hbm, out_sc, read_sc, gain_sc, sems = refs[aliases:]
    nstate = read_hbm.shape[0]
    channels, width = out_hbm.shape
    pieces = width // PIECE
    own = channels // pieces

    def write(halves):
        copies = []
        for half, rows in enumerate(halves):
            piece = half * (pieces // 2) + part
            out_sc[half] = rows[0:channels, :].astype(f32)
            read_sc[half] = rows[channels : channels + nstate, :].astype(f32)
            gain_sc[half] = rows[channels + nstate : channels + nstate + 1, 0:own].astype(f32)
            lanes = pl.ds(piece * PIECE, PIECE)
            copies += [
                pltpu.make_async_copy(out_sc.at[half], out_hbm.at[:, lanes], sems.at[half, 0]),
                pltpu.make_async_copy(read_sc.at[half], read_hbm.at[:, lanes], sems.at[half, 1]),
                pltpu.make_async_copy(gain_sc.at[half], gain_hbm.at[:, pl.ds(piece * own, own)], sems.at[half, 2]),
            ]
            for copy in copies[-3:]:
                copy.start()
        for copy in copies:
            copy.wait()

    pl.when(me_ref[0] & 1 == 0)(lambda: write((mine, came)))
    pl.when(me_ref[0] & 1 == 1)(lambda: write((came, mine)))


def whole(shape):
    return pl.BlockSpec(shape, lambda *_: (0,) * len(shape), pipeline_mode=pl.Buffered(1))


ANYWHERE = pl.BlockSpec(memory_space=pl.ANY)
HELD = pl.BlockSpec(memory_space=pltpu.VMEM)


def held(x):
    return pltpu.with_memory_space_constraint(x, pltpu.VMEM)


def call(body, name, scalars, grid, in_specs, out_specs, out_shape, scratch, vmem, flops, moved, aliases=None):
    return pl.pallas_call(
        body,
        name=name,
        grid_spec=pltpu.PrefetchScalarGridSpec(
            num_scalar_prefetch=scalars, grid=grid, in_specs=in_specs, out_specs=out_specs, scratch_shapes=scratch
        ),
        out_shape=out_shape,
        input_output_aliases=aliases or {},
        compiler_params=pltpu.CompilerParams(vmem_limit_bytes=vmem << 20),
        cost_estimate=pl.CostEstimate(flops=int(flops), bytes_accessed=int(moved), transcendentals=0),
    )


def front(me, readings, graph, cluster, mix, boundaries, w_channels, w_state, w_step, bias, fading_exponent, skip_gain, gain):
    sensors, span, width = readings.shape
    heads, channels, maps = w_step.shape[1], w_channels.shape[1], w_state.shape[1]
    nstate, lanes, chunk = maps // 2, sensors * heads, 16
    rows, half_rows = sensors * chunk, sensors // 2 * nstate
    small = [
        graph, cluster[None, :], mix, boundaries[None, :], w_step.T, bias[None, :], fading_exponent[None, :],
        skip_gain[None, :], gain[None, :], w_state, w_channels,
    ]
    outs = [
        ((sensors, span, width), bf16), ((sensors, span, channels), bf16), ((sensors, span, maps), bf16),
        ((span, lanes), f32), ((span, lanes), f32), ((lanes, span), f32),
        ((sensors // 2, nstate, channels), f32), ((half_rows + sensors, channels), bf16), ((sensors, channels), f32),
        ((8, 128), f32), ((8, channels), f32),
    ]
    return call(
        functools.partial(front_kernel, heads=heads, chunk=chunk, n_small=len(small)), "front", 1, (),
        [ANYWHERE] * (1 + len(small)),
        [HELD] * len(outs),
        [pltpu.VMEM(shape, dtype) for shape, dtype in outs],
        [pltpu.VMEM(x.shape, x.dtype) for x in small] + [
            pltpu.VMEM(readings.shape, bf16), pltpu.VMEM((rows, rows), bf16), pltpu.VMEM((width, maps + lanes), bf16),
            pltpu.VMEM((2 * lanes, channels), bf16),
            pltpu.VMEM((span, lanes), f32), pltpu.VMEM((4, span, channels), bf16),
            pltpu.SemaphoreType.DMA((len(small) + span // chunk,)),
        ],
        20, 5e9, 14e6,
    )(me, *[pltpu.with_memory_space_constraint(x, pltpu.HBM) for x in [readings] + small])


def within(first, count, channels, maps, step, cum_t, consts, cot, w_out, heads, done, token):
    sensors, span, width = channels.shape
    lanes = sensors * heads
    n_in = 7
    aliases = {n_in + k: k for k in range(len(done))}
    aliases[n_in + len(done)] = 6
    return call(
        functools.partial(within_kernel, heads=heads, first=first, count=count, aliases=len(done) + 1),
        "within", 0, (),
        [HELD] * 5 + [ANYWHERE] * 2 + [HELD] * len(done) + [ANYWHERE],
        [HELD] * 6 + [ANYWHERE],
        [
            pltpu.VMEM((sensors, span, width), f32), pltpu.VMEM((sensors, span, width), bf16),
            pltpu.VMEM((sensors, heads, span, span), bf16), pltpu.VMEM((sensors, span, width), f32),
            pltpu.VMEM(cot.shape, bf16), pltpu.VMEM(w_out.shape, bf16),
            jax.ShapeDtypeStruct(token.shape, token.dtype),
        ],
        [pltpu.VMEM((2 * lanes, width), bf16), pltpu.SemaphoreType.DMA((2,))],
        8, 3e8 * count, 1.5e6 * count, aliases,
    )(
        *[held(x) for x in (channels, maps, step, cum_t, consts)],
        *[pltpu.with_memory_space_constraint(x, pltpu.HBM) for x in (cot, w_out)], *[held(x) for x in done], token,
    )


def back(me, blocks, states, maps, scaled, decay, part, grad, cum, consts, done, token):
    sensors, span, width = part.shape
    heads, lanes = decay.shape[1], cum.shape[1]
    at_once = sum(state.shape[0] for state in states)
    n_in = 8 + len(states)
    aliases = {n_in + k: k for k in range(len(done))}
    aliases[n_in + len(done)] = 3
    return call(
        functools.partial(back_kernel, heads=heads, blocks=blocks, aliases=len(done) + 1), "back", 1, (),
        [HELD] * (n_in - 1 + len(done)) + [ANYWHERE],
        [HELD] * 3 + [ANYWHERE],
        [
            pltpu.VMEM((sensors, span, width), bf16), pltpu.VMEM((sensors, span, maps.shape[2] // 2), bf16),
            pltpu.VMEM((8, width), f32), jax.ShapeDtypeStruct(token.shape, token.dtype),
        ],
        [
            pltpu.VMEM((2 * lanes, width), bf16), pltpu.VMEM((span, lanes), f32),
            pltpu.VMEM((at_once, span, width), f32), pltpu.VMEM((at_once, span, width), f32),
            pltpu.VMEM((at_once, span, width), bf16), pltpu.VMEM((at_once, span, width), bf16),
        ],
        8, 3e8 * at_once, 1.5e6 * at_once, aliases,
    )(me, *[held(x) for x in (*states, maps, scaled, decay, part, grad, cum, consts) + done], token)


def grad_rows(channels, nstate):
    return -(-(channels + nstate + 1) // 32) * 32


def early_grads(me, normed, cot, read, mixed, token):
    rows = grad_rows(normed.shape[2], read.shape[2])
    return call(
        early_kernel, "early", 1, (), [HELD] * 4 + [ANYWHERE], [HELD, ANYWHERE],
        [pltpu.VMEM((cot.shape[2] // PIECE, rows, PIECE), f32), jax.ShapeDtypeStruct(token.shape, token.dtype)],
        [], 8, 6e8, 4e6, {5: 1},
    )(me, *[held(x) for x in (normed, cot, read, mixed)], token)


def late_grads(me, normed, cot, read, mixed, before, gains, part):
    rows = before.shape[1]
    return call(
        functools.partial(late_kernel, part=part), "late", 1, (), [HELD] * (5 + len(gains)), [HELD] * 2,
        [pltpu.VMEM((rows, PIECE), f32), pltpu.VMEM((rows, PIECE), bf16)],
        [pltpu.VMEM((2, rows, PIECE), f32)], 10, 8e8, 5e6,
    )(me, *[held(x) for x in (normed, cot, read, mixed, before, *gains)])


def finish(me, mine, came, part, channels, width, nstate, done):
    pieces = width // PIECE
    return call(
        functools.partial(finish_kernel, part=part, aliases=len(done)), "finish", 1, (),
        [HELD] * 2 + [ANYWHERE] * len(done), [ANYWHERE] * 3,
        [
            pltpu.HBM((channels, width), f32), pltpu.HBM((nstate, width), f32), pltpu.HBM((1, channels), f32),
        ],
        [
            pltpu.VMEM((2, channels, PIECE), f32), pltpu.VMEM((2, nstate, PIECE), f32),
            pltpu.VMEM((2, 1, channels // pieces), f32), pltpu.SemaphoreType.DMA((2, 3)),
        ],
        8, 1e6, 2e6, {3 + k: k for k in range(len(done))},
    )(me, held(mine), held(came), *[pltpu.with_memory_space_constraint(x, pltpu.HBM) for x in done])


def swap(x, distance, count):
    return lax.ppermute(x, "seq", [(i, i ^ distance) for i in range(count)])


def narrow(x):
    return lax.reduce_precision(x, 8, 7)


def pick(bit, when_one, when_zero):
    return jnp.where(bit == 1, when_one, when_zero)


def tied(x, token):
    return lax.optimization_barrier((x, token))


def bit_of(me, level):
    return (me >> level) & 1


def shard_start(me, level, sensors):
    return sum(bit_of(me, k) * (sensors >> (k + 1)) for k in range(level + 1))


def row(ref, k):
    return ref[pl.ds(k, 1), :]


EACH = 2


def widened(came, k, nstate):
    return came[k * nstate : (k + 1) * nstate, :].astype(f32)


def tails_of(came, nstate):
    return came[EACH * nstate :, :].astype(f32)


def core_kernel(me_ref, own, tail, came, low_ref, low_tail_ref, tail_ref, kept_ref, *refs):
    send_refs, other_tail = refs[:-1], refs[-1]
    me = me_ref[0]
    bit = bit_of(me, 0)
    size, nstate, width = own.shape
    sensors = tail.shape[0]
    start = shard_start(me, 0, sensors)
    other_tail[...] = came[size * nstate :, :].astype(f32)
    low_tail_ref[...] = pick(bit, other_tail[...], tail[...])
    total_tail = tail[...] + other_tail[...]
    tail_ref[...] = total_tail
    for n in range(1 + len(send_refs)):
        for k in range(EACH):
            sensor = block_start(me, 2 * n, sensors) + k
            j = sensor - start
            other = came[pl.ds(pl.multiple_of(j * nstate, nstate), nstate), :].astype(f32)
            low, high = pick(bit, other, own[j]), pick(bit, own[j], other)
            low_ref[j] = low
            total = low * jnp.exp2(pick(bit, row(tail, sensor), row(other_tail, sensor))) + high
            if n == 0:
                kept_ref[k] = total
            else:
                send_refs[n - 1][k * nstate : (k + 1) * nstate, :] = total.astype(bf16)
    for ref in send_refs:
        ref[EACH * nstate :, :] = total_tail.astype(bf16)


def join_cores(me, own, tail, came):
    size, nstate, width = own.shape
    sent = pltpu.VMEM((EACH * nstate + tail.shape[0], width), bf16)
    return call(
        core_kernel, "cores", 1, (), [HELD] * 3, [HELD] * 7,
        [
            pltpu.VMEM(own.shape, f32), pltpu.VMEM(tail.shape, f32), pltpu.VMEM(tail.shape, f32),
            pltpu.VMEM((EACH, nstate, width), f32), sent, sent, sent,
        ],
        [pltpu.VMEM(tail.shape, f32)], 6, 1e6, 1e6,
    )(me, *[held(x) for x in (own, tail, came)])


def chip_of(me):
    return (me >> 1) & 3


def group_kernel(me_ref, own, tail, *refs):
    cames, (first_ref, pair_ref, third_ref, first_tail, pair_tail, third_tail, send_ref, tail_sc) = refs[:3], refs[3:]
    me = me_ref[0]
    nstate = own.shape[1]
    sensors = tail.shape[0]
    chip = chip_of(me)

    def at(position, values):
        flip = chip ^ position
        return jnp.where(flip == 0, values[0], jnp.where(flip == 1, values[1], jnp.where(flip == 2, values[2], values[3])))

    tails = [tail[...]] + [tails_of(came, nstate) for came in cames]
    for position in range(4):
        tail_sc[position] = at(position, tails)
    first_tail[...] = tail_sc[0]
    pair_tail[...] = tail_sc[0] + tail_sc[1]
    third_tail[...] = tail_sc[2]
    if send_ref.shape[0] > EACH * nstate:
        send_ref[EACH * nstate :, :] = (tail_sc[0] + tail_sc[1] + tail_sc[2] + tail_sc[3]).astype(bf16)
    for k in range(EACH):
        sensor = pl.ds(block_start(me, 0, sensors) + k, 1)
        values = [own[k]] + [widened(came, k, nstate) for came in cames]
        first, second, third, fourth = [at(position, values) for position in range(4)]
        pair = first * jnp.exp2(tail_sc[1, sensor, :]) + second
        first_ref[k] = first
        pair_ref[k] = pair
        third_ref[k] = third
        both = tail_sc[2, sensor, :] + tail_sc[3, sensor, :]
        total = pair * jnp.exp2(both) + (third * jnp.exp2(tail_sc[3, sensor, :]) + fourth)
        send_ref[k * nstate : (k + 1) * nstate, :] = total.astype(bf16)


def join_group(me, own, tail, cames, with_tail):
    state, tails = pltpu.VMEM(own.shape, f32), pltpu.VMEM(tail.shape, f32)
    rows = cames[0].shape[0] - (0 if with_tail else tail.shape[0])
    return call(
        group_kernel, "group", 1, (), [HELD] * 5, [HELD] * 7,
        [state] * 3 + [tails] * 3 + [pltpu.VMEM((rows, own.shape[2]), bf16)],
        [pltpu.VMEM((4,) + tail.shape, f32)], 6, 1e6, 1e6,
    )(me, *[held(x) for x in (own, tail, *cames)])


def across_kernel(me_ref, own, before, came, next_ref, before_ref, *, level):
    me = me_ref[0]
    bit = bit_of(me, level)
    nstate = (own.shape[0] - own.shape[0] // 9) // EACH
    sensors = own.shape[0] - EACH * nstate
    rows = EACH * nstate
    for k in range(EACH):
        sensor = block_start(me, 0, sensors) + k
        here = slice(k * nstate, (k + 1) * nstate)
        other, mine, ahead = came[here, :].astype(f32), own[here, :], before[here, :]
        other_tail = came[rows:, :].astype(f32)
        mask = (iota(other_tail.shape, 0) == sensor).astype(f32)

        def of_sensor(tails):
            return jnp.sum(tails * mask, axis=0, keepdims=True)

        before_ref[here, :] = pick(bit, other * jnp.exp2(of_sensor(before[rows:, :])) + ahead, ahead)
        low, high = pick(bit, other, mine), pick(bit, mine, other)
        next_ref[here, :] = low * jnp.exp2(of_sensor(pick(bit, own[rows:, :], other_tail))) + high
    other_tail = came[rows:, :].astype(f32)
    next_ref[rows:, :] = own[rows:, :] + other_tail
    before_ref[rows:, :] = before[rows:, :] + pick(bit, other_tail, jnp.zeros_like(other_tail))


def across(me, own, before, came, level):
    out = pltpu.VMEM(own.shape, f32)
    return call(
        functools.partial(across_kernel, level=level), "across", 1, (), [HELD] * 3, [HELD] * 2, [out, out],
        [], 6, 1e6, 1e6,
    )(me, *[held(x) for x in (own, before, came)])


def landed(me, state, sensor, low, low_tail):
    start = shard_start(me, 0, low_tail.shape[0])
    after = state * jnp.exp2(row(low_tail, sensor)) + low[sensor - start]
    bit = bit_of(me, 0)
    return pick(bit, after, state).astype(bf16), pick(bit, state, after).astype(bf16)


def fall_kernel(
    me_ref, came, first, pair, third, first_tail, pair_tail, third_tail, low, low_tail,
    state_ref, core_ref, *send_refs, level,
):
    me = me_ref[0]
    nstate = first.shape[1]
    sensors = low_tail.shape[0]
    for k in range(EACH):
        sensor = block_start(me, 0, sensors) + k
        before = widened(came, k, nstate)
        if level is not None:
            before = pick(bit_of(me, level), before, jnp.zeros_like(before))
        third_start = before * jnp.exp2(row(pair_tail, sensor)) + pair[k]
        starts = [
            before,
            before * jnp.exp2(row(first_tail, sensor)) + first[k],
            third_start,
            third_start * jnp.exp2(row(third_tail, sensor)) + third[k],
        ]
        for n in range(4):
            chip = chip_of(me) ^ n
            state = jnp.where(
                chip == 0, starts[0], jnp.where(chip == 1, starts[1], jnp.where(chip == 2, starts[2], starts[3]))
            )
            if n == 0:
                state_ref[k], core_ref[k] = landed(me, state, sensor, low, low_tail)
            else:
                send_refs[n - 1][k] = state.astype(bf16)


def fall(me, came, level, group, low, low_tail):
    nstate, width = low.shape[1:]
    return call(
        functools.partial(fall_kernel, level=level), "fall", 1, (), [HELD] * 9, [HELD] * 5,
        [pltpu.VMEM((EACH, nstate, width), bf16)] * 5, [], 6, 1e6, 1e6,
    )(me, *[held(x) for x in (came, *group, low, low_tail)])


def land_kernel(me_ref, low, low_tail, *refs, blocks):
    cames, (state_ref, core_ref) = refs[: len(blocks)], refs[len(blocks) :]
    me = me_ref[0]
    for n, (flips, came) in enumerate(zip(blocks, cames)):
        for k in range(EACH):
            sensor = block_start(me, flips, low_tail.shape[0]) + k
            state_ref[n * EACH + k], core_ref[n * EACH + k] = landed(me, came[k].astype(f32), sensor, low, low_tail)


def land(me, low, low_tail, blocks, cames):
    out = pltpu.VMEM((EACH * len(blocks),) + low.shape[1:], bf16)
    return call(
        functools.partial(land_kernel, blocks=blocks), "land", 1, (), [HELD] * (2 + len(blocks)), [HELD] * 2,
        [out, out], [], 6, 1e6, 1e6,
    )(me, *[held(x) for x in (low, low_tail, *cames)])


SHARDED = 3


def halve_kernel(me_ref, part, came, kept_ref, gone_ref, *, level):
    size = kept_ref.shape[0]
    total = part[...] + came[...].astype(f32)
    bit = bit_of(me_ref[0], level)
    low, high = total[0:size], total[size:]
    kept_ref[...] = pick(bit, high, low)
    gone_ref[...] = pick(bit, low, high).astype(bf16)


def halve(me, part, came, level):
    shape = (part.shape[0] // 2, part.shape[1])
    return call(
        functools.partial(halve_kernel, level=level), "halve", 1, (), [HELD] * 2, [HELD] * 2,
        [pltpu.VMEM(shape, f32), pltpu.VMEM(shape, bf16)], [], 6, 1e6, 1e6,
    )(me, held(part), held(came))


def join_kernel(me_ref, part, came, out_ref, *, level):
    size = part.shape[0]
    bit = bit_of(me_ref[0], level)
    own, other = part[...].astype(f32), came[...].astype(f32)
    out_ref[0:size, :] = pick(bit, other, own).astype(bf16)
    out_ref[size:, :] = pick(bit, own, other).astype(bf16)


def join(me, part, came, level):
    return call(
        functools.partial(join_kernel, level=level), "join", 1, (), [HELD] * 2, [HELD],
        [pltpu.VMEM((2 * part.shape[0], part.shape[1]), bf16)], [], 6, 1e6, 1e6,
    )(me, held(part), held(came))[0]


def all_sum(keep, send, me, count, order):
    levels = count.bit_length() - 1
    part, came = keep, swap(send, 1, count)
    for level in order:
        part, gone = halve(me, part, came, level)
        came = swap(gone, 1 << level, count)
    part = part + came.astype(f32)
    for level in range(SHARDED, levels):
        part = narrow(part)
        part = part + swap(part.astype(bf16), 1 << level, count).astype(f32)
    part = part.astype(bf16)
    for level in reversed(order):
        part = join(me, part, swap(part, 1 << level, count), level)
    return part, swap(part, 1, count)


def per_device(
    count, readings, block_graph, cluster_of, mix_weight, boundaries, w_channels, w_state, w_step,
    step_bias, channel_fading_exponent, skip_gain, norm_gain, w_out, cotangent,
):
    sensors, span, width = readings.shape
    channels = w_channels.shape[1]
    nstate = w_state.shape[1] // 2
    me = lax.axis_index("seq").astype(jnp.int32)
    at = me[None]
    heads = skip_gain.shape[0]

    mixed, chans, maps, step, cum, cum_t, keep, send, tail, token, consts = front(
        at, readings, block_graph, cluster_of, mix_weight, boundaries, w_channels, w_state, w_step,
        step_bias, channel_fading_exponent, skip_gain, norm_gain,
    )
    work = {"token": token, "within": (), "back": (), "gains": []}

    def run_back(blocks, *states):
        part, scaled, decay, grad = work["within"][:4]
        normed, read, gain, work["token"] = back(
            at, blocks, states, maps, scaled, decay, part, grad, cum, consts, work["back"], work["token"]
        )
        work["back"] = (normed, read)
        work["gains"].append(gain)

    def tie(x):
        x, work["token"] = tied(x, work["token"])
        return x

    def run_within(first, size):
        *arrays, work["token"] = within(
            first, size, chans, maps, step, cum_t, consts, cotangent, w_out, heads, work["within"], work["token"]
        )
        work["within"] = tuple(arrays)

    came = swap(send, 1, count)
    low, low_tail, tail, kept, *sends = join_cores(at, keep, tail, came)
    sends = tie(sends)
    cames = [swap(x, 2 * (n + 1), count) for n, x in enumerate(sends)]
    run_within(0, 10)
    cames = tie(cames)
    levels = count.bit_length() - 1
    *group, send = join_group(at, kept, tail, cames, levels > SHARDED + 1)
    if levels == SHARDED + 1:
        came, level = swap(tie(send), 1 << SHARDED, count), SHARDED
        run_within(10, sensors - 10)
        came = tie(came)
    else:
        run_within(10, sensors - 10)
        own, before, level = send.astype(f32), jnp.zeros(send.shape, f32), None
        for k in range(SHARDED, levels):
            own, before = across(at, own, before, swap(own.astype(bf16), 1 << k, count), k)
        came = before
    states, to_core, *sends = fall(at, came, level, group, low, low_tail)
    to_core, sends = tie((to_core, sends))
    core = swap(to_core, 1, count)
    from_one, from_two, from_three = [swap(x, 2 * (n + 1), count) for n, x in enumerate(sends)]
    run_back((0,), states)
    run_back((1,), core)
    cot = work["within"][4]
    early, work["token"] = early_grads(at, work["back"][0], cot, work["back"][1], mixed, work["token"])
    arrived = tie((from_two, from_one, from_three))
    states, to_core = land(at, low, low_tail, (4, 2, 6), arrived)
    core = swap(tie(to_core), 1, count)
    run_back((4, 2, 6), states)
    run_back((5, 3, 7), core)
    results = ()
    sums = []
    for part, order in ((0, (1, 2)), (1, (2, 1))):
        keep_part, send_part = late_grads(
            at, work["back"][0], cot, work["back"][1], mixed, early, work["gains"], part
        )
        sums.append(all_sum(keep_part, send_part, at, count, order))
    for part in (0, 1):
        results = finish(at, *sums[part], part, channels, width, nstate, tuple(results))
    grad_out, grad_read, grad_gain = results
    return grad_out, grad_read.T, grad_gain[0]


def solution(mesh):
    in_specs = (
        P("groups", "seq", None), P("groups", None), P("groups"), P(), P(("groups", "seq")),
        P(), P(), P(), P(), P(), P(), P(), P(), P("groups", "seq", None),
    )
    out_specs = (P("groups", None), P("groups", None), P("groups"))
    return jax.shard_map(
        functools.partial(per_device, mesh.shape["seq"]),
        mesh=mesh, in_specs=in_specs, out_specs=out_specs, check_vma=False,
    )
```

```python
import functools
import math

import jax
import jax.numpy as jnp
from jax import lax
from jax.experimental import pallas as pl
from jax.experimental.pallas import tpu as pltpu
from jax.sharding import PartitionSpec as P

f32 = jnp.float32
bf16 = jnp.bfloat16
LOG2E = math.log2(math.e)
LOG_PULSE = math.log(0.7)
NT = (((1,), (1,)), ((), ()))
TN = (((0,), (0,)), ((), ()))


def dot(a, b, dims=(((1,), (0,)), ((), ()))):
    return lax.dot_general(a, b, dims, preferred_element_type=f32)


def split(x, terms):
    parts = []
    for _ in range(terms):
        part = x.astype(bf16)
        parts.append(part)
        x = x - part.astype(f32)
    return parts


def iota(shape, axis):
    return lax.broadcasted_iota(jnp.int32, shape, axis)


def spread_matrix(rows, heads, channels):
    size = channels // heads
    return (iota((rows, channels), 0) % heads == iota((rows, channels), 1) // size).astype(bf16)


def spread(values, sensor, heads, spread2):
    lane = iota(values.shape, 1)
    own = jnp.where(lane // heads == sensor, values, 0.0)
    return dot(jnp.concatenate(split(own, 2), axis=1), spread2)


def front_kernel(
    me_ref, readings_hbm, *refs, heads, chunk, n_small,
):
    hbm, refs = refs[:n_small], refs[n_small:]
    (mixed_ref, channels_ref, maps_ref, step_ref, cum_ref, cum_t_ref, weight_ref, send_ref, tail_ref, token_ref,
     consts_ref), refs = refs[:11], refs[11:]
    vmem, refs = refs[:n_small], refs[n_small:]
    readings, kmix, wms, spread2, log_sc, scaled_sc, sems = refs
    graph, cluster, mix, marks, w_step_t, bias, fading_exponent, skip_gain, norm_gain, w_state, w_channels = vmem
    sensors, span, width = readings.shape
    rows = sensors * chunk
    maps = w_state.shape[1]
    nstate = maps // 2
    channels = w_channels.shape[1]
    lanes = sensors * heads
    chunks = span // chunk

    def reading_copy(k):
        part = pl.ds(k * chunk, chunk)
        return pltpu.make_async_copy(readings_hbm.at[:, part], readings.at[:, part], sems.at[n_small + k])

    copies = [pltpu.make_async_copy(hbm[k], vmem[k], sems.at[k]) for k in range(n_small)]
    for copy in copies[:-2]:
        copy.start()
    reading_copy(0).start()
    copies[-2].start()
    copies[-1].start()
    for k in range(1, chunks):
        reading_copy(k).start()

    token_ref[...] = jnp.zeros_like(token_ref)
    wms[...] = jnp.zeros_like(wms)
    spread2[...] = spread_matrix(spread2.shape[0], heads, channels)
    for copy in copies[:-2]:
        copy.wait()
    wms[:, maps : maps + heads] = w_step_t[...].astype(f32).T.astype(bf16)
    picked = (iota((sensors, sensors), 0) == cluster[...]).astype(bf16)
    sensor_of = (iota((sensors, rows), 1) // chunk == iota((sensors, rows), 0)).astype(bf16)
    linked = dot(dot(picked, graph[...].astype(f32).astype(bf16), TN).astype(bf16), dot(picked, sensor_of).astype(bf16))
    coupling = (linked * sum(dot(part, sensor_of) for part in split(mix[...], 3))).astype(bf16).astype(f32)
    full = jnp.broadcast_to(coupling[:, None, :], (sensors, chunk, rows)).reshape(rows, rows)
    same = iota((rows, rows), 0) % chunk == iota((rows, rows), 1) % chunk
    kmix[...] = jnp.where(same, full, 0.0).astype(bf16)
    tiled = (iota((heads, lanes), 1) % heads == iota((heads, lanes), 0)).astype(bf16)
    both = jnp.concatenate([bias[...], -jnp.exp(fading_exponent[...]) * LOG2E], axis=0)
    wide = sum(dot(part, tiled) for part in split(both, 3))
    bias_row, rate_row = wide[0:1], wide[1:2]
    consts_ref[...] = jnp.zeros_like(consts_ref)
    consts_ref[0:1, :] = sum(dot(part, spread2[0:heads, :]) for part in split(skip_gain[...], 3))
    consts_ref[1:2, :] = norm_gain[...]

    def mix_chunk(i):
        here = slice(i * chunk, (i + 1) * chunk)
        reading_copy(i).wait()
        x = readings[:, here, :].reshape(rows, width)
        mixed_ref[:, here, :] = (x.astype(f32) + dot(kmix[...], x)).astype(bf16).reshape(sensors, chunk, width)

    mix_chunk(0)
    copies[-2].wait()
    wms[:, 0:maps] = w_state[...]
    copies[-1].wait()
    for i in range(chunks):
        here = slice(i * chunk, (i + 1) * chunk)
        if i + 1 < chunks:
            mix_chunk(i + 1)
        mixed = mixed_ref[:, here, :].reshape(rows, width)
        small = dot(mixed, wms[...])
        channels_ref[:, here, :] = dot(mixed, w_channels[...]).astype(bf16).reshape(sensors, chunk, channels)
        maps_ref[:, here, :] = small[:, 0:maps].astype(bf16).reshape(sensors, chunk, maps)
        steps = small[:, maps:].reshape(sensors, chunk, lanes)
        packed = steps[0]
        for s in range(1, sensors):
            packed = packed + pltpu.roll(steps[s], heads * s, 1)
        raw = (packed + bias_row).astype(bf16).astype(f32)
        step = jnp.maximum(raw, 0.0) + jnp.log1p(jnp.exp(-jnp.abs(raw)))
        step_ref[here, :] = step
        log_sc[here, :] = rate_row * step

    at, to = iota((span, span), 0), iota((span, span), 1)
    marked = jnp.sum(jnp.where(at == to, marks[...].astype(f32), 0.0), axis=1, keepdims=True)
    log_decay = log_sc[...] + (LOG_PULSE * LOG2E) * marked
    lower = (at >= to).astype(bf16)
    cum = sum(dot(lower, part) for part in split(log_decay, 3))
    cum_ref[...] = cum
    cum_t_ref[...] = cum.T
    last = cum[span - 1 : span, :]
    weight = jnp.exp2(last - cum) * step_ref[...]
    weight_ref[...] = weight

    half = sensors // 2
    mine = (me_ref[0] & 1) * half

    def scale(n):
        s = half - mine + n
        scaled_sc[n % 4] = (channels_ref[s].astype(f32) * spread(weight, s, heads, spread2[...])).astype(bf16)

    own = jnp.where(iota((sensors, lanes), 1) // heads == iota((sensors, lanes), 0), last, 0.0)
    tail = sum(dot(part, spread2[0:lanes, :]) for part in split(own, 3))
    tail_ref[...] = tail
    send_ref[half * nstate :, :] = tail.astype(bf16)
    scale(0)
    scale(1)
    for n in range(half):
        if n + 2 < half:
            scale(n + 2)
        state = dot(maps_ref[half - mine + n], scaled_sc[n % 4], TN)[0:nstate]
        send_ref[n * nstate : (n + 1) * nstate, :] = state.astype(bf16)


def own_kernel(me_ref, channels, maps, weight, keep_ref, spread2, scaled_sc, *, heads):
    half, nstate, width = keep_ref.shape
    mine = (me_ref[0] & 1) * half
    spread2[...] = spread_matrix(spread2.shape[0], heads, width)

    def scale(n):
        scaled_sc[n % 4] = (
            channels[mine + n].astype(f32) * spread(weight[...], mine + n, heads, spread2[...])
        ).astype(bf16)

    scale(0)
    scale(1)
    for n in range(half):
        if n + 2 < half:
            scale(n + 2)
        keep_ref[n] = dot(maps[mine + n], scaled_sc[n % 4], TN)[0:nstate]


def pair_blocks(x, size):
    lane = iota(x.shape, 1)
    zero = jnp.zeros_like(x)
    return jnp.concatenate([jnp.where(lane < size, x, zero), jnp.where(lane >= size, x, zero)], axis=0)


def within_kernel(channels, maps, step, cum, cum_t, consts, cot_hbm, w_out_hbm, *refs, heads, first, count, aliases):
    part_ref, scaled_ref, decay_ref, grad_ref, cot_ref, w_out_ref, fade_ref, _, spread2, fade_sc, sems = refs[aliases:]
    _, span, width = channels.shape
    nstate = maps.shape[2] // 2
    size = width // heads
    own = slice(first, first + count)
    cot_copy = pltpu.make_async_copy(cot_hbm.at[own], cot_ref.at[own], sems.at[0])
    if first == 0:
        w_out_copy = pltpu.make_async_copy(w_out_hbm, w_out_ref, sems.at[1])
        w_out_copy.start()
    cot_copy.start()
    spread2[...] = spread_matrix(spread2.shape[0], heads, width)
    fade_sc[...] = jnp.exp2(cum[...])

    def sensor(k, carry):
        s = first + k
        causal = iota((span, span), 0) >= iota((span, span), 1)
        chan = channels[s].astype(f32)
        scaled = (chan * spread(step[...], s, heads, spread2[...])).astype(bf16)
        scaled_ref[s] = scaled
        fade_ref[s] = spread(fade_sc[...], s, heads, spread2[...])
        both = maps[s]
        scores = dot(both[:, nstate:], both[:, 0:nstate], NT)
        row = cum_t[pl.ds(pl.multiple_of(s * heads, heads), heads), :]
        col = row.T
        for pair in range(heads // 2):
            weighted = []
            for h in (2 * pair, 2 * pair + 1):
                gap = jnp.broadcast_to(col[:, h : h + 1], (span, span)) - row[h : h + 1, :]
                decay = jnp.exp2(jnp.where(causal, gap, -jnp.inf))
                decay_ref[s, h] = decay.astype(bf16)
                weighted.append((scores * decay).astype(bf16))
            lanes = slice(2 * pair * size, 2 * (pair + 1) * size)
            out = dot(jnp.concatenate(weighted, axis=1), pair_blocks(scaled[:, lanes], size))
            part_ref[s, :, lanes] = out + consts[0:1, lanes] * chan[:, lanes]
        return carry

    lax.fori_loop(0, count, sensor, 0, unroll=2)
    if first == 0:
        w_out_copy.wait()
    cot_copy.wait()
    grad = dot(cot_ref[own].reshape(count * span, cot_ref.shape[2]), w_out_ref[...], NT)
    grad_ref[own] = grad.reshape(count, span, width)


def block_start(me, flips, sensors):
    return shard_start(me ^ flips, 2, sensors)


def back_kernel(me_ref, *refs, heads, blocks, aliases):
    states, refs = refs[0], refs[1:]
    maps, scaled, decay, part, grad, fades, consts = refs[:7]
    normed_ref, read_ref, gain_ref, _, carried_sc, back_sc, faded_sc = refs[7 + aliases :]
    sensors, span, width = part.shape
    nstate = maps.shape[2] // 2
    size = width // heads
    each = states.shape[0] // len(blocks)
    chunk = 32
    todo = [
        (block_start(me_ref[0], flips, sensors) + k, states, n * each + k)
        for n, flips in enumerate(blocks)
        for k in range(each)
    ]

    def carry_in(slot):
        s, state, k = todo[slot]
        carried_sc[slot] = dot(maps[s][:, nstate:], state[k])

    def normalize(slot, gain_sum):
        s = todo[slot][0]
        gain = consts[1:2, :]
        for c in range(0, span, chunk):
            rows = slice(c, c + chunk)
            fade = fades[s, rows, :]
            out = part[s, rows, :] + carried_sc[slot, rows, :] * fade
            inv = lax.rsqrt(jnp.mean(out * out, axis=-1, keepdims=True) + 1e-05)
            normed = out * inv
            normed_ref[s, rows, :] = (normed * gain).astype(bf16)
            g = grad[s, rows, :]
            gain_sum = gain_sum + jnp.sum((normed * g).reshape(chunk // 8, 8, width), axis=0)
            by_gain = g * gain
            mean = jnp.mean(by_gain * normed, axis=-1, keepdims=True)
            back = inv * (by_gain - normed * mean)
            back_sc[slot, rows, :] = back.astype(bf16)
            faded_sc[slot, rows, :] = (back * fade).astype(bf16)
        return gain_sum

    def read_out(slot):
        s, state, k = todo[slot]
        read = dot(faded_sc[slot], state[k], NT)
        pairs = jnp.zeros((span, span), f32)
        for pair in range(heads // 2):
            lanes = slice(2 * pair * size, 2 * (pair + 1) * size)
            both_heads = dot(back_sc[slot, :, lanes], pair_blocks(scaled[s, :, lanes], size), NT)
            pairs = pairs + both_heads[:, 0:span] * decay[s, 2 * pair].astype(f32)
            pairs = pairs + both_heads[:, span:] * decay[s, 2 * pair + 1].astype(f32)
        read_ref[s] = (read + dot(pairs.astype(bf16), maps[s][:, 0:nstate])).astype(bf16)

    gain_sum = jnp.zeros(gain_ref.shape, f32)
    for slot in range(len(todo)):
        carry_in(slot)
    for slot in range(len(todo)):
        gain_sum = normalize(slot, gain_sum)
    for slot in range(len(todo)):
        read_out(slot)
    gain_ref[...] = gain_sum


PIECE = 256


def grad_piece(normed, cot, read, mixed, blocks, piece):
    span, channels = normed.shape[1:]
    lanes = slice(piece * PIECE, (piece + 1) * PIECE)

    def product(left, right, start, size):
        here = pl.ds(start, size)
        rows = size * span
        return dot(left[here].reshape(rows, left.shape[2]), right[here, :, lanes].reshape(rows, PIECE), TN)

    return (
        sum(product(normed, cot, *block) for block in blocks),
        sum(product(read, mixed, *block) for block in blocks),
    )


def early_blocks(me, sensors):
    return [(block_start(me, flips, sensors), 2) for flips in (0, 1)]


def late_blocks(me, sensors):
    size = sensors // 4
    for other in (0, 1):
        yield block_start(me, 4 ^ other, sensors), 2
        yield shard_start(me ^ 2 ^ other, 1, sensors), size


def early_kernel(me_ref, normed, cot, read, mixed, _, total, __):
    channels, nstate = normed.shape[2], read.shape[2]
    for piece in range(total.shape[0]):
        out, into = grad_piece(normed, cot, read, mixed, early_blocks(me_ref[0], normed.shape[0]), piece)
        total[piece, 0:channels, :] = out
        total[piece, channels : channels + nstate, :] = into


def late_kernel(me_ref, normed, cot, read, mixed, before, *refs, part):
    *gains, keep_ref, send_ref, total = refs
    channels, nstate = normed.shape[2], read.shape[2]
    pieces = before.shape[0]
    own = channels // pieces
    bit = me_ref[0] & 1
    gain = sum(jnp.sum(ref[...], axis=0, keepdims=True) for ref in gains)
    for half in range(2):
        piece = half * (pieces // 2) + part
        out, into = grad_piece(normed, cot, read, mixed, list(late_blocks(me_ref[0], normed.shape[0])), piece)
        total[half, 0:channels, :] = out + before[piece, 0:channels, :]
        total[half, channels : channels + nstate, :] = into + before[piece, channels : channels + nstate, :]
        rest = total.shape[1] - channels - nstate
        total[half, channels + nstate :, :] = jnp.zeros((rest, PIECE), f32)
        total[half, channels + nstate : channels + nstate + 1, 0:own] = gain[:, piece * own : (piece + 1) * own]
    keep_ref[...] = total[bit]
    send_ref[...] = total[1 - bit].astype(bf16)


def finish_kernel(me_ref, mine, came, *refs, part, aliases):
    out_hbm, read_hbm, gain_hbm, out_sc, read_sc, gain_sc, sems = refs[aliases:]
    nstate = read_hbm.shape[0]
    channels, width = out_hbm.shape
    pieces = width // PIECE
    own = channels // pieces

    def write(halves):
        copies = []
        for half, rows in enumerate(halves):
            piece = half * (pieces // 2) + part
            out_sc[half] = rows[0:channels, :].astype(f32)
            read_sc[half] = rows[channels : channels + nstate, :].astype(f32)
            gain_sc[half] = rows[channels + nstate : channels + nstate + 1, 0:own].astype(f32)
            lanes = pl.ds(piece * PIECE, PIECE)
            copies += [
                pltpu.make_async_copy(out_sc.at[half], out_hbm.at[:, lanes], sems.at[half, 0]),
                pltpu.make_async_copy(read_sc.at[half], read_hbm.at[:, lanes], sems.at[half, 1]),
                pltpu.make_async_copy(gain_sc.at[half], gain_hbm.at[:, pl.ds(piece * own, own)], sems.at[half, 2]),
            ]
            for copy in copies[-3:]:
                copy.start()
        for copy in copies:
            copy.wait()

    pl.when(me_ref[0] & 1 == 0)(lambda: write((mine, came)))
    pl.when(me_ref[0] & 1 == 1)(lambda: write((came, mine)))


def whole(shape):
    return pl.BlockSpec(shape, lambda *_: (0,) * len(shape), pipeline_mode=pl.Buffered(1))


ANYWHERE = pl.BlockSpec(memory_space=pl.ANY)
HELD = pl.BlockSpec(memory_space=pltpu.VMEM)


def held(x):
    return pltpu.with_memory_space_constraint(x, pltpu.VMEM)


def call(body, name, scalars, grid, in_specs, out_specs, out_shape, scratch, vmem, flops, moved, aliases=None):
    return pl.pallas_call(
        body,
        name=name,
        grid_spec=pltpu.PrefetchScalarGridSpec(
            num_scalar_prefetch=scalars, grid=grid, in_specs=in_specs, out_specs=out_specs, scratch_shapes=scratch
        ),
        out_shape=out_shape,
        input_output_aliases=aliases or {},
        compiler_params=pltpu.CompilerParams(vmem_limit_bytes=vmem << 20),
        cost_estimate=pl.CostEstimate(flops=int(flops), bytes_accessed=int(moved), transcendentals=0),
    )


def front(me, readings, graph, cluster, mix, boundaries, w_channels, w_state, w_step, bias, fading_exponent, skip_gain, gain):
    sensors, span, width = readings.shape
    heads, channels, maps = w_step.shape[1], w_channels.shape[1], w_state.shape[1]
    nstate, lanes, chunk = maps // 2, sensors * heads, 16
    rows, half_rows = sensors * chunk, sensors // 2 * nstate
    small = [
        graph, cluster[None, :], mix, boundaries[None, :], w_step.T, bias[None, :], fading_exponent[None, :],
        skip_gain[None, :], gain[None, :], w_state, w_channels,
    ]
    outs = [
        ((sensors, span, width), bf16), ((sensors, span, channels), bf16), ((sensors, span, maps), bf16),
        ((span, lanes), f32), ((span, lanes), f32), ((lanes, span), f32),
        ((span, lanes), f32), ((half_rows + sensors, channels), bf16), ((sensors, channels), f32),
        ((8, 128), f32), ((8, channels), f32),
    ]
    return call(
        functools.partial(front_kernel, heads=heads, chunk=chunk, n_small=len(small)), "front", 1, (),
        [ANYWHERE] * (1 + len(small)),
        [HELD] * len(outs),
        [pltpu.VMEM(shape, dtype) for shape, dtype in outs],
        [pltpu.VMEM(x.shape, x.dtype) for x in small] + [
            pltpu.VMEM(readings.shape, bf16), pltpu.VMEM((rows, rows), bf16), pltpu.VMEM((width, maps + lanes), bf16),
            pltpu.VMEM((2 * lanes, channels), bf16),
            pltpu.VMEM((span, lanes), f32), pltpu.VMEM((4, span, channels), bf16),
            pltpu.SemaphoreType.DMA((len(small) + span // chunk,)),
        ],
        20, 5e9, 14e6,
    )(me, *[pltpu.with_memory_space_constraint(x, pltpu.HBM) for x in [readings] + small])


def own_states(me, channels, maps, weight, nstate):
    sensors, span, width = channels.shape
    lanes = weight.shape[1]
    return call(
        functools.partial(own_kernel, heads=lanes // sensors), "own", 1, (), [HELD] * 3, [HELD],
        [pltpu.VMEM((sensors // 2, nstate, width), f32)],
        [pltpu.VMEM((2 * lanes, width), bf16), pltpu.VMEM((4, span, width), bf16)], 8, 3e8, 2e6,
    )(me, *[held(x) for x in (channels, maps, weight)])[0]


def within(first, count, channels, maps, step, cum, cum_t, consts, cot, w_out, heads, done, token):
    sensors, span, width = channels.shape
    lanes = sensors * heads
    n_in = 8
    aliases = {n_in + k: k for k in range(len(done))}
    aliases[n_in + len(done)] = 7
    return call(
        functools.partial(within_kernel, heads=heads, first=first, count=count, aliases=len(done) + 1),
        "within", 0, (),
        [HELD] * 6 + [ANYWHERE] * 2 + [HELD] * len(done) + [ANYWHERE],
        [HELD] * 7 + [ANYWHERE],
        [
            pltpu.VMEM((sensors, span, width), f32), pltpu.VMEM((sensors, span, width), bf16),
            pltpu.VMEM((sensors, heads, span, span), bf16), pltpu.VMEM((sensors, span, width), f32),
            pltpu.VMEM(cot.shape, bf16), pltpu.VMEM(w_out.shape, bf16), pltpu.VMEM((sensors, span, width), f32),
            jax.ShapeDtypeStruct(token.shape, token.dtype),
        ],
        [pltpu.VMEM((2 * lanes, width), bf16), pltpu.VMEM((span, lanes), f32), pltpu.SemaphoreType.DMA((2,))],
        8, 3e8 * count, 1.5e6 * count, aliases,
    )(
        *[held(x) for x in (channels, maps, step, cum, cum_t, consts)],
        *[pltpu.with_memory_space_constraint(x, pltpu.HBM) for x in (cot, w_out)], *[held(x) for x in done], token,
    )


def back(me, blocks, states, maps, scaled, decay, part, grad, fades, consts, done, token):
    sensors, span, width = part.shape
    heads = decay.shape[1]
    at_once = sum(state.shape[0] for state in states)
    n_in = 8 + len(states)
    aliases = {n_in + k: k for k in range(len(done))}
    aliases[n_in + len(done)] = 3
    return call(
        functools.partial(back_kernel, heads=heads, blocks=blocks, aliases=len(done) + 1), "back", 1, (),
        [HELD] * (n_in - 1 + len(done)) + [ANYWHERE],
        [HELD] * 3 + [ANYWHERE],
        [
            pltpu.VMEM((sensors, span, width), bf16), pltpu.VMEM((sensors, span, maps.shape[2] // 2), bf16),
            pltpu.VMEM((8, width), f32), jax.ShapeDtypeStruct(token.shape, token.dtype),
        ],
        [
            pltpu.VMEM((at_once, span, width), f32),
            pltpu.VMEM((at_once, span, width), bf16), pltpu.VMEM((at_once, span, width), bf16),
        ],
        8, 3e8 * at_once, 1.5e6 * at_once, aliases,
    )(me, *[held(x) for x in (*states, maps, scaled, decay, part, grad, fades, consts) + done], token)


def grad_rows(channels, nstate):
    return -(-(channels + nstate + 1) // 32) * 32


def early_grads(me, normed, cot, read, mixed, token):
    rows = grad_rows(normed.shape[2], read.shape[2])
    return call(
        early_kernel, "early", 1, (), [HELD] * 4 + [ANYWHERE], [HELD, ANYWHERE],
        [pltpu.VMEM((cot.shape[2] // PIECE, rows, PIECE), f32), jax.ShapeDtypeStruct(token.shape, token.dtype)],
        [], 8, 6e8, 4e6, {5: 1},
    )(me, *[held(x) for x in (normed, cot, read, mixed)], token)


def late_grads(me, normed, cot, read, mixed, before, gains, part):
    rows = before.shape[1]
    return call(
        functools.partial(late_kernel, part=part), "late", 1, (), [HELD] * (5 + len(gains)), [HELD] * 2,
        [pltpu.VMEM((rows, PIECE), f32), pltpu.VMEM((rows, PIECE), bf16)],
        [pltpu.VMEM((2, rows, PIECE), f32)], 10, 8e8, 5e6,
    )(me, *[held(x) for x in (normed, cot, read, mixed, before, *gains)])


def finish(me, mine, came, part, channels, width, nstate, done):
    pieces = width // PIECE
    return call(
        functools.partial(finish_kernel, part=part, aliases=len(done)), "finish", 1, (),
        [HELD] * 2 + [ANYWHERE] * len(done), [ANYWHERE] * 3,
        [
            pltpu.HBM((channels, width), f32), pltpu.HBM((nstate, width), f32), pltpu.HBM((1, channels), f32),
        ],
        [
            pltpu.VMEM((2, channels, PIECE), f32), pltpu.VMEM((2, nstate, PIECE), f32),
            pltpu.VMEM((2, 1, channels // pieces), f32), pltpu.SemaphoreType.DMA((2, 3)),
        ],
        8, 1e6, 2e6, {3 + k: k for k in range(len(done))},
    )(me, held(mine), held(came), *[pltpu.with_memory_space_constraint(x, pltpu.HBM) for x in done])


def swap(x, distance, count):
    return lax.ppermute(x, "seq", [(i, i ^ distance) for i in range(count)])


def narrow(x):
    return lax.reduce_precision(x, 8, 7)


def pick(bit, when_one, when_zero):
    return jnp.where(bit == 1, when_one, when_zero)


def tied(x, token):
    return lax.optimization_barrier((x, token))


def bit_of(me, level):
    return (me >> level) & 1


def shard_start(me, level, sensors):
    return sum(bit_of(me, k) * (sensors >> (k + 1)) for k in range(level + 1))


def row(ref, k):
    return ref[pl.ds(k, 1), :]


EACH = 2


def widened(came, k, nstate):
    return came[k * nstate : (k + 1) * nstate, :].astype(f32)


def tails_of(came, nstate):
    return came[EACH * nstate :, :].astype(f32)


def core_kernel(me_ref, own, tail, came, low_ref, low_tail_ref, tail_ref, kept_ref, *refs):
    send_refs, other_tail = refs[:-1], refs[-1]
    me = me_ref[0]
    bit = bit_of(me, 0)
    size, nstate, width = own.shape
    sensors = tail.shape[0]
    start = shard_start(me, 0, sensors)
    other_tail[...] = came[size * nstate :, :].astype(f32)
    low_tail_ref[...] = pick(bit, other_tail[...], tail[...])
    total_tail = tail[...] + other_tail[...]
    tail_ref[...] = total_tail
    for n in range(1 + len(send_refs)):
        for k in range(EACH):
            sensor = block_start(me, 2 * n, sensors) + k
            j = sensor - start
            other = came[pl.ds(pl.multiple_of(j * nstate, nstate), nstate), :].astype(f32)
            low, high = pick(bit, other, own[j]), pick(bit, own[j], other)
            low_ref[j] = low
            total = low * jnp.exp2(pick(bit, row(tail, sensor), row(other_tail, sensor))) + high
            if n == 0:
                kept_ref[k] = total
            else:
                send_refs[n - 1][k * nstate : (k + 1) * nstate, :] = total.astype(bf16)
    for ref in send_refs:
        ref[EACH * nstate :, :] = total_tail.astype(bf16)


def join_cores(me, own, tail, came):
    size, nstate, width = own.shape
    sent = pltpu.VMEM((EACH * nstate + tail.shape[0], width), bf16)
    return call(
        core_kernel, "cores", 1, (), [HELD] * 3, [HELD] * 7,
        [
            pltpu.VMEM(own.shape, f32), pltpu.VMEM(tail.shape, f32), pltpu.VMEM(tail.shape, f32),
            pltpu.VMEM((EACH, nstate, width), f32), sent, sent, sent,
        ],
        [pltpu.VMEM(tail.shape, f32)], 6, 1e6, 1e6,
    )(me, *[held(x) for x in (own, tail, came)])


def chip_of(me):
    return (me >> 1) & 3


def group_kernel(me_ref, own, tail, *refs):
    cames, (first_ref, pair_ref, third_ref, first_tail, pair_tail, third_tail, send_ref, tail_sc) = refs[:3], refs[3:]
    me = me_ref[0]
    nstate = own.shape[1]
    sensors = tail.shape[0]
    chip = chip_of(me)

    def at(position, values):
        flip = chip ^ position
        return jnp.where(flip == 0, values[0], jnp.where(flip == 1, values[1], jnp.where(flip == 2, values[2], values[3])))

    tails = [tail[...]] + [tails_of(came, nstate) for came in cames]
    for position in range(4):
        tail_sc[position] = at(position, tails)
    first_tail[...] = tail_sc[0]
    pair_tail[...] = tail_sc[0] + tail_sc[1]
    third_tail[...] = tail_sc[2]
    if send_ref.shape[0] > EACH * nstate:
        send_ref[EACH * nstate :, :] = (tail_sc[0] + tail_sc[1] + tail_sc[2] + tail_sc[3]).astype(bf16)
    for k in range(EACH):
        sensor = pl.ds(block_start(me, 0, sensors) + k, 1)
        values = [own[k]] + [widened(came, k, nstate) for came in cames]
        first, second, third, fourth = [at(position, values) for position in range(4)]
        pair = first * jnp.exp2(tail_sc[1, sensor, :]) + second
        first_ref[k] = first
        pair_ref[k] = pair
        third_ref[k] = third
        both = tail_sc[2, sensor, :] + tail_sc[3, sensor, :]
        total = pair * jnp.exp2(both) + (third * jnp.exp2(tail_sc[3, sensor, :]) + fourth)
        send_ref[k * nstate : (k + 1) * nstate, :] = total.astype(bf16)


def join_group(me, own, tail, cames, with_tail):
    state, tails = pltpu.VMEM(own.shape, f32), pltpu.VMEM(tail.shape, f32)
    rows = cames[0].shape[0] - (0 if with_tail else tail.shape[0])
    return call(
        group_kernel, "group", 1, (), [HELD] * 5, [HELD] * 7,
        [state] * 3 + [tails] * 3 + [pltpu.VMEM((rows, own.shape[2]), bf16)],
        [pltpu.VMEM((4,) + tail.shape, f32)], 6, 1e6, 1e6,
    )(me, *[held(x) for x in (own, tail, *cames)])


def across_kernel(me_ref, own, before, came, next_ref, before_ref, *, level):
    me = me_ref[0]
    bit = bit_of(me, level)
    nstate = (own.shape[0] - own.shape[0] // 9) // EACH
    sensors = own.shape[0] - EACH * nstate
    rows = EACH * nstate
    for k in range(EACH):
        sensor = block_start(me, 0, sensors) + k
        here = slice(k * nstate, (k + 1) * nstate)
        other, mine, ahead = came[here, :].astype(f32), own[here, :], before[here, :]
        other_tail = came[rows:, :].astype(f32)
        mask = (iota(other_tail.shape, 0) == sensor).astype(f32)

        def of_sensor(tails):
            return jnp.sum(tails * mask, axis=0, keepdims=True)

        before_ref[here, :] = pick(bit, other * jnp.exp2(of_sensor(before[rows:, :])) + ahead, ahead)
        low, high = pick(bit, other, mine), pick(bit, mine, other)
        next_ref[here, :] = low * jnp.exp2(of_sensor(pick(bit, own[rows:, :], other_tail))) + high
    other_tail = came[rows:, :].astype(f32)
    next_ref[rows:, :] = own[rows:, :] + other_tail
    before_ref[rows:, :] = before[rows:, :] + pick(bit, other_tail, jnp.zeros_like(other_tail))


def across(me, own, before, came, level):
    out = pltpu.VMEM(own.shape, f32)
    return call(
        functools.partial(across_kernel, level=level), "across", 1, (), [HELD] * 3, [HELD] * 2, [out, out],
        [], 6, 1e6, 1e6,
    )(me, *[held(x) for x in (own, before, came)])


def landed(me, state, sensor, low, low_tail):
    start = shard_start(me, 0, low_tail.shape[0])
    after = state * jnp.exp2(row(low_tail, sensor)) + low[sensor - start]
    bit = bit_of(me, 0)
    return pick(bit, after, state).astype(bf16), pick(bit, state, after).astype(bf16)


def fall_kernel(
    me_ref, came, first, pair, third, first_tail, pair_tail, third_tail, low, low_tail,
    state_ref, core_ref, *send_refs, level,
):
    me = me_ref[0]
    nstate = first.shape[1]
    sensors = low_tail.shape[0]
    for k in range(EACH):
        sensor = block_start(me, 0, sensors) + k
        before = widened(came, k, nstate)
        if level is not None:
            before = pick(bit_of(me, level), before, jnp.zeros_like(before))
        third_start = before * jnp.exp2(row(pair_tail, sensor)) + pair[k]
        starts = [
            before,
            before * jnp.exp2(row(first_tail, sensor)) + first[k],
            third_start,
            third_start * jnp.exp2(row(third_tail, sensor)) + third[k],
        ]
        for n in range(4):
            chip = chip_of(me) ^ n
            state = jnp.where(
                chip == 0, starts[0], jnp.where(chip == 1, starts[1], jnp.where(chip == 2, starts[2], starts[3]))
            )
            if n == 0:
                state_ref[k], core_ref[k] = landed(me, state, sensor, low, low_tail)
            else:
                send_refs[n - 1][k] = state.astype(bf16)


def fall(me, came, level, group, low, low_tail):
    nstate, width = low.shape[1:]
    return call(
        functools.partial(fall_kernel, level=level), "fall", 1, (), [HELD] * 9, [HELD] * 5,
        [pltpu.VMEM((EACH, nstate, width), bf16)] * 5, [], 6, 1e6, 1e6,
    )(me, *[held(x) for x in (came, *group, low, low_tail)])


def land_kernel(me_ref, low, low_tail, *refs, blocks):
    cames, (state_ref, core_ref) = refs[: len(blocks)], refs[len(blocks) :]
    me = me_ref[0]
    for n, (flips, came) in enumerate(zip(blocks, cames)):
        for k in range(EACH):
            sensor = block_start(me, flips, low_tail.shape[0]) + k
            state_ref[n * EACH + k], core_ref[n * EACH + k] = landed(me, came[k].astype(f32), sensor, low, low_tail)


def land(me, low, low_tail, blocks, cames):
    out = pltpu.VMEM((EACH * len(blocks),) + low.shape[1:], bf16)
    return call(
        functools.partial(land_kernel, blocks=blocks), "land", 1, (), [HELD] * (2 + len(blocks)), [HELD] * 2,
        [out, out], [], 6, 1e6, 1e6,
    )(me, *[held(x) for x in (low, low_tail, *cames)])


SHARDED = 3


def halve_kernel(me_ref, part, came, kept_ref, gone_ref, *, level):
    size = kept_ref.shape[0]
    total = part[...] + came[...].astype(f32)
    bit = bit_of(me_ref[0], level)
    low, high = total[0:size], total[size:]
    kept_ref[...] = pick(bit, high, low)
    gone_ref[...] = pick(bit, low, high).astype(bf16)


def halve(me, part, came, level):
    shape = (part.shape[0] // 2, part.shape[1])
    return call(
        functools.partial(halve_kernel, level=level), "halve", 1, (), [HELD] * 2, [HELD] * 2,
        [pltpu.VMEM(shape, f32), pltpu.VMEM(shape, bf16)], [], 6, 1e6, 1e6,
    )(me, held(part), held(came))


def join_kernel(me_ref, part, came, out_ref, *, level):
    size = part.shape[0]
    bit = bit_of(me_ref[0], level)
    own, other = part[...].astype(f32), came[...].astype(f32)
    out_ref[0:size, :] = pick(bit, other, own).astype(bf16)
    out_ref[size:, :] = pick(bit, own, other).astype(bf16)


def join(me, part, came, level):
    return call(
        functools.partial(join_kernel, level=level), "join", 1, (), [HELD] * 2, [HELD],
        [pltpu.VMEM((2 * part.shape[0], part.shape[1]), bf16)], [], 6, 1e6, 1e6,
    )(me, held(part), held(came))[0]


def all_sum(keep, send, me, count, order):
    levels = count.bit_length() - 1
    part, came = keep, swap(send, 1, count)
    for level in order:
        part, gone = halve(me, part, came, level)
        came = swap(gone, 1 << level, count)
    part = part + came.astype(f32)
    for level in range(SHARDED, levels):
        part = narrow(part)
        part = part + swap(part.astype(bf16), 1 << level, count).astype(f32)
    part = part.astype(bf16)
    for level in reversed(order):
        part = join(me, part, swap(part, 1 << level, count), level)
    return part, swap(part, 1, count)


def per_device(
    count, readings, block_graph, cluster_of, mix_weight, boundaries, w_channels, w_state, w_step,
    step_bias, channel_fading_exponent, skip_gain, norm_gain, w_out, cotangent,
):
    sensors, span, width = readings.shape
    channels = w_channels.shape[1]
    nstate = w_state.shape[1] // 2
    me = lax.axis_index("seq").astype(jnp.int32)
    at = me[None]
    heads = skip_gain.shape[0]

    mixed, chans, maps, step, cum, cum_t, weight, send, tail, token, consts = front(
        at, readings, block_graph, cluster_of, mix_weight, boundaries, w_channels, w_state, w_step,
        step_bias, channel_fading_exponent, skip_gain, norm_gain,
    )
    work = {"token": token, "within": (), "back": (), "gains": []}

    def run_back(blocks, *states):
        part, scaled, decay, grad, _, _, fades = work["within"]
        normed, read, gain, work["token"] = back(
            at, blocks, states, maps, scaled, decay, part, grad, fades, consts, work["back"], work["token"]
        )
        work["back"] = (normed, read)
        work["gains"].append(gain)

    def tie(x):
        x, work["token"] = tied(x, work["token"])
        return x

    def run_within(first, size):
        *arrays, work["token"] = within(
            first, size, chans, maps, step, cum, cum_t, consts, cotangent, w_out, heads, work["within"], work["token"]
        )
        work["within"] = tuple(arrays)

    came = swap(send, 1, count)
    keep = own_states(at, chans, maps, weight, nstate)
    came, keep = tied(came, keep)
    low, low_tail, tail, kept, *sends = join_cores(at, keep, tail, came)
    sends = tie(sends)
    cames = [swap(x, 2 * (n + 1), count) for n, x in enumerate(sends)]
    run_within(0, 10)
    cames = tie(cames)
    levels = count.bit_length() - 1
    *group, send = join_group(at, kept, tail, cames, levels > SHARDED + 1)
    if levels == SHARDED + 1:
        came, level = swap(tie(send), 1 << SHARDED, count), SHARDED
        run_within(10, sensors - 10)
        came = tie(came)
    else:
        run_within(10, sensors - 10)
        own, before, level = send.astype(f32), jnp.zeros(send.shape, f32), None
        for k in range(SHARDED, levels):
            own, before = across(at, own, before, swap(own.astype(bf16), 1 << k, count), k)
        came = before
    states, to_core, *sends = fall(at, came, level, group, low, low_tail)
    to_core, sends = tie((to_core, sends))
    core = swap(to_core, 1, count)
    from_one, from_two, from_three = [swap(x, 2 * (n + 1), count) for n, x in enumerate(sends)]
    run_back((0,), states)
    run_back((1,), core)
    cot = work["within"][4]
    early, work["token"] = early_grads(at, work["back"][0], cot, work["back"][1], mixed, work["token"])
    arrived = tie((from_two, from_one, from_three))
    states, to_core = land(at, low, low_tail, (4, 2, 6), arrived)
    core = swap(tie(to_core), 1, count)
    run_back((4, 2, 6), states)
    run_back((5, 3, 7), core)
    results = ()
    sums = []
    for part, order in ((0, (1, 2)), (1, (2, 1))):
        keep_part, send_part = late_grads(
            at, work["back"][0], cot, work["back"][1], mixed, early, work["gains"], part
        )
        sums.append(all_sum(keep_part, send_part, at, count, order))
    for part in (0, 1):
        results = finish(at, *sums[part], part, channels, width, nstate, tuple(results))
    grad_out, grad_read, grad_gain = results
    return grad_out, grad_read.T, grad_gain[0]


def solution(mesh):
    in_specs = (
        P("groups", "seq", None), P("groups", None), P("groups"), P(), P(("groups", "seq")),
        P(), P(), P(), P(), P(), P(), P(), P(), P("groups", "seq", None),
    )
    out_specs = (P("groups", None), P("groups", None), P("groups"))
    return jax.shard_map(
        functools.partial(per_device, mesh.shape["seq"]),
        mesh=mesh, in_specs=in_specs, out_specs=out_specs, check_vma=False,
    )
```

```python
import functools
import math

import jax
import jax.numpy as jnp
from jax import lax
from jax.experimental import pallas as pl
from jax.experimental.pallas import tpu as pltpu
from jax.sharding import PartitionSpec as P

f32 = jnp.float32
bf16 = jnp.bfloat16
LOG2E = math.log2(math.e)
LOG_PULSE = math.log(0.7)
NT = (((1,), (1,)), ((), ()))
TN = (((0,), (0,)), ((), ()))


def dot(a, b, dims=(((1,), (0,)), ((), ()))):
    return lax.dot_general(a, b, dims, preferred_element_type=f32)


def split(x, terms):
    parts = []
    for _ in range(terms):
        part = x.astype(bf16)
        parts.append(part)
        x = x - part.astype(f32)
    return parts


def iota(shape, axis):
    return lax.broadcasted_iota(jnp.int32, shape, axis)


def spread_matrix(rows, heads, channels):
    size = channels // heads
    return (iota((rows, channels), 0) % heads == iota((rows, channels), 1) // size).astype(bf16)


def spread(values, sensor, heads, spread2):
    lane = iota(values.shape, 1)
    own = jnp.where(lane // heads == sensor, values, 0.0)
    return dot(jnp.concatenate(split(own, 2), axis=1), spread2)


def front_kernel(
    me_ref, readings_hbm, *refs, heads, chunk, n_small,
):
    hbm, refs = refs[:n_small], refs[n_small:]
    (mixed_ref, channels_ref, maps_ref, step_ref, cum_ref, cum_t_ref, weight_ref, send_ref, tail_ref, token_ref,
     consts_ref), refs = refs[:11], refs[11:]
    vmem, refs = refs[:n_small], refs[n_small:]
    readings, kmix, wms, spread2, log_sc, scaled_sc, sems = refs
    graph, cluster, mix, marks, w_step_t, bias, fading_exponent, skip_gain, norm_gain, w_state, w_channels = vmem
    sensors, span, width = readings.shape
    rows = sensors * chunk
    maps = w_state.shape[1]
    nstate = maps // 2
    channels = w_channels.shape[1]
    lanes = sensors * heads
    chunks = span // chunk

    def reading_copy(k):
        part = pl.ds(k * chunk, chunk)
        return pltpu.make_async_copy(readings_hbm.at[:, part], readings.at[:, part], sems.at[n_small + k])

    copies = [pltpu.make_async_copy(hbm[k], vmem[k], sems.at[k]) for k in range(n_small)]
    for copy in copies[:-2]:
        copy.start()
    reading_copy(0).start()
    copies[-2].start()
    reading_copy(1).start()
    copies[-1].start()
    for k in range(2, chunks):
        reading_copy(k).start()

    token_ref[...] = jnp.zeros_like(token_ref)
    wms[...] = jnp.zeros_like(wms)
    spread2[...] = spread_matrix(spread2.shape[0], heads, channels)
    for copy in copies[:-2]:
        copy.wait()
    wms[:, maps : maps + heads] = w_step_t[...].astype(f32).T.astype(bf16)
    picked = (iota((sensors, sensors), 0) == cluster[...]).astype(bf16)
    sensor_of = (iota((sensors, rows), 1) // chunk == iota((sensors, rows), 0)).astype(bf16)
    linked = dot(dot(picked, graph[...].astype(f32).astype(bf16), TN).astype(bf16), dot(picked, sensor_of).astype(bf16))
    coupling = (linked * sum(dot(part, sensor_of) for part in split(mix[...], 3))).astype(bf16).astype(f32)
    full = jnp.broadcast_to(coupling[:, None, :], (sensors, chunk, rows)).reshape(rows, rows)
    same = iota((rows, rows), 0) % chunk == iota((rows, rows), 1) % chunk
    kmix[...] = jnp.where(same, full, 0.0).astype(bf16)
    tiled = (iota((heads, lanes), 1) % heads == iota((heads, lanes), 0)).astype(bf16)
    both = jnp.concatenate([bias[...], -jnp.exp(fading_exponent[...]) * LOG2E], axis=0)
    wide = sum(dot(part, tiled) for part in split(both, 3))
    bias_row, rate_row = wide[0:1], wide[1:2]
    consts_ref[...] = jnp.zeros_like(consts_ref)
    consts_ref[0:1, :] = sum(dot(part, spread2[0:heads, :]) for part in split(skip_gain[...], 3))
    consts_ref[1:2, :] = norm_gain[...]

    def mix_chunk(i):
        here = slice(i * chunk, (i + 1) * chunk)
        reading_copy(i).wait()
        x = readings[:, here, :].reshape(rows, width)
        mixed_ref[:, here, :] = (x.astype(f32) + dot(kmix[...], x)).astype(bf16).reshape(sensors, chunk, width)

    mix_chunk(0)
    copies[-2].wait()
    wms[:, 0:maps] = w_state[...]
    for i in range(chunks):
        here = slice(i * chunk, (i + 1) * chunk)
        if i + 1 < chunks:
            mix_chunk(i + 1)
        mixed = mixed_ref[:, here, :].reshape(rows, width)
        small = dot(mixed, wms[...])
        if i == 0:
            copies[-1].wait()
        channels_ref[:, here, :] = dot(mixed, w_channels[...]).astype(bf16).reshape(sensors, chunk, channels)
        maps_ref[:, here, :] = small[:, 0:maps].astype(bf16).reshape(sensors, chunk, maps)
        steps = small[:, maps:].reshape(sensors, chunk, lanes)
        packed = steps[0]
        for s in range(1, sensors):
            packed = packed + pltpu.roll(steps[s], heads * s, 1)
        raw = (packed + bias_row).astype(bf16).astype(f32)
        step = jnp.maximum(raw, 0.0) + jnp.log1p(jnp.exp(-jnp.abs(raw)))
        step_ref[here, :] = step
        log_sc[here, :] = rate_row * step

    at, to = iota((span, span), 0), iota((span, span), 1)
    marked = jnp.sum(jnp.where(at == to, marks[...].astype(f32), 0.0), axis=1, keepdims=True)
    log_decay = log_sc[...] + (LOG_PULSE * LOG2E) * marked
    lower = (at >= to).astype(bf16)
    cum = sum(dot(lower, part) for part in split(log_decay, 3))
    cum_ref[...] = cum
    cum_t_ref[...] = cum.T
    last = cum[span - 1 : span, :]
    weight = jnp.exp2(last - cum) * step_ref[...]
    weight_ref[...] = weight

    half = sensors // 2
    mine = (me_ref[0] & 1) * half

    def scale(n):
        s = half - mine + n
        scaled_sc[n % 4] = (channels_ref[s].astype(f32) * spread(weight, s, heads, spread2[...])).astype(bf16)

    own = jnp.where(iota((sensors, lanes), 1) // heads == iota((sensors, lanes), 0), last, 0.0)
    tail = sum(dot(part, spread2[0:lanes, :]) for part in split(own, 3))
    tail_ref[...] = tail
    send_ref[half * nstate :, :] = tail.astype(bf16)
    scale(0)
    scale(1)
    for n in range(half):
        if n + 2 < half:
            scale(n + 2)
        state = dot(maps_ref[half - mine + n], scaled_sc[n % 4], TN)[0:nstate]
        send_ref[n * nstate : (n + 1) * nstate, :] = state.astype(bf16)


def own_kernel(me_ref, channels, maps, weight, keep_ref, spread2, scaled_sc, *, heads):
    half, nstate, width = keep_ref.shape
    mine = (me_ref[0] & 1) * half
    spread2[...] = spread_matrix(spread2.shape[0], heads, width)

    def scale(n):
        scaled_sc[n % 4] = (
            channels[mine + n].astype(f32) * spread(weight[...], mine + n, heads, spread2[...])
        ).astype(bf16)

    scale(0)
    scale(1)
    for n in range(half):
        if n + 2 < half:
            scale(n + 2)
        keep_ref[n] = dot(maps[mine + n], scaled_sc[n % 4], TN)[0:nstate]


def pair_blocks(x, size):
    lane = iota(x.shape, 1)
    zero = jnp.zeros_like(x)
    return jnp.concatenate([jnp.where(lane < size, x, zero), jnp.where(lane >= size, x, zero)], axis=0)


def within_kernel(channels, maps, step, cum, cum_t, consts, cot_hbm, w_out_hbm, *refs, heads, first, count, aliases):
    part_ref, scaled_ref, decay_ref, grad_ref, cot_ref, w_out_ref, fade_ref, _, spread2, fade_sc, sems = refs[aliases:]
    _, span, width = channels.shape
    nstate = maps.shape[2] // 2
    size = width // heads
    own = slice(first, first + count)
    cot_copy = pltpu.make_async_copy(cot_hbm.at[own], cot_ref.at[own], sems.at[0])
    if first == 0:
        w_out_copy = pltpu.make_async_copy(w_out_hbm, w_out_ref, sems.at[1])
        w_out_copy.start()
    cot_copy.start()
    spread2[...] = spread_matrix(spread2.shape[0], heads, width)
    fade_sc[...] = jnp.exp2(cum[...])

    def sensor(k, carry):
        s = first + k
        causal = iota((span, span), 0) >= iota((span, span), 1)
        chan = channels[s].astype(f32)
        scaled = (chan * spread(step[...], s, heads, spread2[...])).astype(bf16)
        scaled_ref[s] = scaled
        fade_ref[s] = spread(fade_sc[...], s, heads, spread2[...])
        both = maps[s]
        scores = dot(both[:, nstate:], both[:, 0:nstate], NT)
        row = cum_t[pl.ds(pl.multiple_of(s * heads, heads), heads), :]
        col = row.T
        for pair in range(heads // 2):
            weighted = []
            for h in (2 * pair, 2 * pair + 1):
                gap = jnp.broadcast_to(col[:, h : h + 1], (span, span)) - row[h : h + 1, :]
                decay = jnp.exp2(jnp.where(causal, gap, -jnp.inf))
                decay_ref[s, h] = decay.astype(bf16)
                weighted.append((scores * decay).astype(bf16))
            lanes = slice(2 * pair * size, 2 * (pair + 1) * size)
            out = dot(jnp.concatenate(weighted, axis=1), pair_blocks(scaled[:, lanes], size))
            part_ref[s, :, lanes] = out + consts[0:1, lanes] * chan[:, lanes]
        return carry

    lax.fori_loop(0, count, sensor, 0, unroll=2)
    if first == 0:
        w_out_copy.wait()
    cot_copy.wait()
    grad = dot(cot_ref[own].reshape(count * span, cot_ref.shape[2]), w_out_ref[...], NT)
    grad_ref[own] = grad.reshape(count, span, width)


def block_start(me, flips, sensors):
    return shard_start(me ^ flips, 2, sensors)


def back_kernel(me_ref, *refs, heads, blocks, aliases):
    states, refs = refs[0], refs[1:]
    maps, scaled, decay, part, grad, fades, consts = refs[:7]
    normed_ref, read_ref, gain_ref, _, carried_sc, back_sc, faded_sc = refs[7 + aliases :]
    sensors, span, width = part.shape
    nstate = maps.shape[2] // 2
    size = width // heads
    each = states.shape[0] // len(blocks)
    chunk = 32
    todo = [
        (block_start(me_ref[0], flips, sensors) + k, states, n * each + k)
        for n, flips in enumerate(blocks)
        for k in range(each)
    ]

    def carry_in(slot):
        s, state, k = todo[slot]
        carried_sc[slot] = dot(maps[s][:, nstate:], state[k])

    def normalize(slot, gain_sum):
        s = todo[slot][0]
        gain = consts[1:2, :]
        for c in range(0, span, chunk):
            rows = slice(c, c + chunk)
            fade = fades[s, rows, :]
            out = part[s, rows, :] + carried_sc[slot, rows, :] * fade
            inv = lax.rsqrt(jnp.mean(out * out, axis=-1, keepdims=True) + 1e-05)
            normed = out * inv
            normed_ref[s, rows, :] = (normed * gain).astype(bf16)
            g = grad[s, rows, :]
            gain_sum = gain_sum + jnp.sum((normed * g).reshape(chunk // 8, 8, width), axis=0)
            by_gain = g * gain
            mean = jnp.mean(by_gain * normed, axis=-1, keepdims=True)
            back = inv * (by_gain - normed * mean)
            back_sc[slot, rows, :] = back.astype(bf16)
            faded_sc[slot, rows, :] = (back * fade).astype(bf16)
        return gain_sum

    def read_out(slot):
        s, state, k = todo[slot]
        read = dot(faded_sc[slot], state[k], NT)
        pairs = jnp.zeros((span, span), f32)
        for pair in range(heads // 2):
            lanes = slice(2 * pair * size, 2 * (pair + 1) * size)
            both_heads = dot(back_sc[slot, :, lanes], pair_blocks(scaled[s, :, lanes], size), NT)
            pairs = pairs + both_heads[:, 0:span] * decay[s, 2 * pair].astype(f32)
            pairs = pairs + both_heads[:, span:] * decay[s, 2 * pair + 1].astype(f32)
        read_ref[s] = (read + dot(pairs.astype(bf16), maps[s][:, 0:nstate])).astype(bf16)

    gain_sum = jnp.zeros(gain_ref.shape, f32)
    for slot in range(len(todo)):
        carry_in(slot)
    for slot in range(len(todo)):
        gain_sum = normalize(slot, gain_sum)
    for slot in range(len(todo)):
        read_out(slot)
    gain_ref[...] = gain_sum


PIECE = 256


def grad_piece(normed, cot, read, mixed, blocks, piece):
    span, channels = normed.shape[1:]
    lanes = slice(piece * PIECE, (piece + 1) * PIECE)

    def product(left, right, start, size):
        here = pl.ds(start, size)
        rows = size * span
        return dot(left[here].reshape(rows, left.shape[2]), right[here, :, lanes].reshape(rows, PIECE), TN)

    return (
        sum(product(normed, cot, *block) for block in blocks),
        sum(product(read, mixed, *block) for block in blocks),
    )


def early_blocks(me, sensors):
    return [(block_start(me, flips, sensors), 2) for flips in (0, 1)]


def late_blocks(me, sensors):
    size = sensors // 4
    for other in (0, 1):
        yield block_start(me, 4 ^ other, sensors), 2
        yield shard_start(me ^ 2 ^ other, 1, sensors), size


def early_kernel(me_ref, normed, cot, read, mixed, _, total, __):
    channels, nstate = normed.shape[2], read.shape[2]
    for piece in range(total.shape[0]):
        out, into = grad_piece(normed, cot, read, mixed, early_blocks(me_ref[0], normed.shape[0]), piece)
        total[piece, 0:channels, :] = out
        total[piece, channels : channels + nstate, :] = into


def late_kernel(me_ref, normed, cot, read, mixed, before, *refs, part, kept):
    *gains, out_ref = refs
    channels, nstate = normed.shape[2], read.shape[2]
    pieces = before.shape[0]
    own = channels // pieces
    bit = me_ref[0] & 1
    blocks = list(late_blocks(me_ref[0], normed.shape[0]))
    gain = sum(jnp.sum(ref[...], axis=0, keepdims=True) for ref in gains)
    at = channels + nstate

    def write(half):
        piece = half * (pieces // 2) + part
        out, into = grad_piece(normed, cot, read, mixed, blocks, piece)
        out_ref[0:channels, :] = (out + before[piece, 0:channels, :]).astype(out_ref.dtype)
        out_ref[channels:at, :] = (into + before[piece, channels:at, :]).astype(out_ref.dtype)
        row_of = iota((out_ref.shape[0] - at, PIECE), 0)
        lane = iota((out_ref.shape[0] - at, PIECE), 1)
        values = jnp.concatenate([gain[:, piece * own : (piece + 1) * own]] * (PIECE // own), axis=1)
        rest = jnp.where((row_of == 0) & (lane < own), values, 0.0)
        out_ref[at:, :] = rest.astype(out_ref.dtype)

    for half in range(2):
        pl.when(bit == (half if kept else 1 - half))(functools.partial(write, half))


def finish_kernel(me_ref, mine, came, *refs, part, aliases):
    out_hbm, read_hbm, gain_hbm, out_sc, read_sc, gain_sc, sems = refs[aliases:]
    nstate = read_hbm.shape[0]
    channels, width = out_hbm.shape
    pieces = width // PIECE
    own = channels // pieces

    def write(halves):
        copies = []
        for half, rows in enumerate(halves):
            piece = half * (pieces // 2) + part
            out_sc[half] = rows[0:channels, :].astype(f32)
            read_sc[half] = rows[channels : channels + nstate, :].astype(f32)
            gain_sc[half] = rows[channels + nstate : channels + nstate + 1, 0:own].astype(f32)
            lanes = pl.ds(piece * PIECE, PIECE)
            copies += [
                pltpu.make_async_copy(out_sc.at[half], out_hbm.at[:, lanes], sems.at[half, 0]),
                pltpu.make_async_copy(read_sc.at[half], read_hbm.at[:, lanes], sems.at[half, 1]),
                pltpu.make_async_copy(gain_sc.at[half], gain_hbm.at[:, pl.ds(piece * own, own)], sems.at[half, 2]),
            ]
            for copy in copies[-3:]:
                copy.start()
        for copy in copies:
            copy.wait()

    pl.when(me_ref[0] & 1 == 0)(lambda: write((mine, came)))
    pl.when(me_ref[0] & 1 == 1)(lambda: write((came, mine)))


def whole(shape):
    return pl.BlockSpec(shape, lambda *_: (0,) * len(shape), pipeline_mode=pl.Buffered(1))


ANYWHERE = pl.BlockSpec(memory_space=pl.ANY)
HELD = pl.BlockSpec(memory_space=pltpu.VMEM)


def held(x):
    return pltpu.with_memory_space_constraint(x, pltpu.VMEM)


def call(body, name, scalars, grid, in_specs, out_specs, out_shape, scratch, vmem, flops, moved, aliases=None):
    return pl.pallas_call(
        body,
        name=name,
        grid_spec=pltpu.PrefetchScalarGridSpec(
            num_scalar_prefetch=scalars, grid=grid, in_specs=in_specs, out_specs=out_specs, scratch_shapes=scratch
        ),
        out_shape=out_shape,
        input_output_aliases=aliases or {},
        compiler_params=pltpu.CompilerParams(vmem_limit_bytes=vmem << 20),
        cost_estimate=pl.CostEstimate(flops=int(flops), bytes_accessed=int(moved), transcendentals=0),
    )


def front(me, readings, graph, cluster, mix, boundaries, w_channels, w_state, w_step, bias, fading_exponent, skip_gain, gain):
    sensors, span, width = readings.shape
    heads, channels, maps = w_step.shape[1], w_channels.shape[1], w_state.shape[1]
    nstate, lanes, chunk = maps // 2, sensors * heads, 16
    rows, half_rows = sensors * chunk, sensors // 2 * nstate
    small = [
        graph, cluster[None, :], mix, boundaries[None, :], w_step.T, bias[None, :], fading_exponent[None, :],
        skip_gain[None, :], gain[None, :], w_state, w_channels,
    ]
    outs = [
        ((sensors, span, width), bf16), ((sensors, span, channels), bf16), ((sensors, span, maps), bf16),
        ((span, lanes), f32), ((span, lanes), f32), ((lanes, span), f32),
        ((span, lanes), f32), ((half_rows + sensors, channels), bf16), ((sensors, channels), f32),
        ((8, 128), f32), ((8, channels), f32),
    ]
    return call(
        functools.partial(front_kernel, heads=heads, chunk=chunk, n_small=len(small)), "front", 1, (),
        [ANYWHERE] * (1 + len(small)),
        [HELD] * len(outs),
        [pltpu.VMEM(shape, dtype) for shape, dtype in outs],
        [pltpu.VMEM(x.shape, x.dtype) for x in small] + [
            pltpu.VMEM(readings.shape, bf16), pltpu.VMEM((rows, rows), bf16), pltpu.VMEM((width, maps + lanes), bf16),
            pltpu.VMEM((2 * lanes, channels), bf16),
            pltpu.VMEM((span, lanes), f32), pltpu.VMEM((4, span, channels), bf16),
            pltpu.SemaphoreType.DMA((len(small) + span // chunk,)),
        ],
        20, 5e9, 14e6,
    )(me, *[pltpu.with_memory_space_constraint(x, pltpu.HBM) for x in [readings] + small])


def own_states(me, channels, maps, weight, nstate):
    sensors, span, width = channels.shape
    lanes = weight.shape[1]
    return call(
        functools.partial(own_kernel, heads=lanes // sensors), "own", 1, (), [HELD] * 3, [HELD],
        [pltpu.VMEM((sensors // 2, nstate, width), f32)],
        [pltpu.VMEM((2 * lanes, width), bf16), pltpu.VMEM((4, span, width), bf16)], 8, 3e8, 2e6,
    )(me, *[held(x) for x in (channels, maps, weight)])[0]


def within(first, count, channels, maps, step, cum, cum_t, consts, cot, w_out, heads, done, token):
    sensors, span, width = channels.shape
    lanes = sensors * heads
    n_in = 8
    aliases = {n_in + k: k for k in range(len(done))}
    aliases[n_in + len(done)] = 7
    return call(
        functools.partial(within_kernel, heads=heads, first=first, count=count, aliases=len(done) + 1),
        "within", 0, (),
        [HELD] * 6 + [ANYWHERE] * 2 + [HELD] * len(done) + [ANYWHERE],
        [HELD] * 7 + [ANYWHERE],
        [
            pltpu.VMEM((sensors, span, width), f32), pltpu.VMEM((sensors, span, width), bf16),
            pltpu.VMEM((sensors, heads, span, span), bf16), pltpu.VMEM((sensors, span, width), f32),
            pltpu.VMEM(cot.shape, bf16), pltpu.VMEM(w_out.shape, bf16), pltpu.VMEM((sensors, span, width), f32),
            jax.ShapeDtypeStruct(token.shape, token.dtype),
        ],
        [pltpu.VMEM((2 * lanes, width), bf16), pltpu.VMEM((span, lanes), f32), pltpu.SemaphoreType.DMA((2,))],
        8, 3e8 * count, 1.5e6 * count, aliases,
    )(
        *[held(x) for x in (channels, maps, step, cum, cum_t, consts)],
        *[pltpu.with_memory_space_constraint(x, pltpu.HBM) for x in (cot, w_out)], *[held(x) for x in done], token,
    )


def back(me, blocks, states, maps, scaled, decay, part, grad, fades, consts, done, token):
    sensors, span, width = part.shape
    heads = decay.shape[1]
    at_once = sum(state.shape[0] for state in states)
    n_in = 8 + len(states)
    aliases = {n_in + k: k for k in range(len(done))}
    aliases[n_in + len(done)] = 3
    return call(
        functools.partial(back_kernel, heads=heads, blocks=blocks, aliases=len(done) + 1), "back", 1, (),
        [HELD] * (n_in - 1 + len(done)) + [ANYWHERE],
        [HELD] * 3 + [ANYWHERE],
        [
            pltpu.VMEM((sensors, span, width), bf16), pltpu.VMEM((sensors, span, maps.shape[2] // 2), bf16),
            pltpu.VMEM((8, width), f32), jax.ShapeDtypeStruct(token.shape, token.dtype),
        ],
        [
            pltpu.VMEM((at_once, span, width), f32),
            pltpu.VMEM((at_once, span, width), bf16), pltpu.VMEM((at_once, span, width), bf16),
        ],
        8, 3e8 * at_once, 1.5e6 * at_once, aliases,
    )(me, *[held(x) for x in (*states, maps, scaled, decay, part, grad, fades, consts) + done], token)


def grad_rows(channels, nstate):
    return -(-(channels + nstate + 1) // 32) * 32


def early_grads(me, normed, cot, read, mixed, token):
    rows = grad_rows(normed.shape[2], read.shape[2])
    return call(
        early_kernel, "early", 1, (), [HELD] * 4 + [ANYWHERE], [HELD, ANYWHERE],
        [pltpu.VMEM((cot.shape[2] // PIECE, rows, PIECE), f32), jax.ShapeDtypeStruct(token.shape, token.dtype)],
        [], 8, 6e8, 4e6, {5: 1},
    )(me, *[held(x) for x in (normed, cot, read, mixed)], token)


def late_grads(me, normed, cot, read, mixed, before, gains, part, kept):
    rows = before.shape[1]
    return call(
        functools.partial(late_kernel, part=part, kept=kept), "late", 1, (), [HELD] * (5 + len(gains)), [HELD],
        [pltpu.VMEM((rows, PIECE), f32 if kept else bf16)], [], 10, 4e8, 3e6,
    )(me, *[held(x) for x in (normed, cot, read, mixed, before, *gains)])[0]


def finish(me, mine, came, part, channels, width, nstate, done):
    pieces = width // PIECE
    return call(
        functools.partial(finish_kernel, part=part, aliases=len(done)), "finish", 1, (),
        [HELD] * 2 + [ANYWHERE] * len(done), [ANYWHERE] * 3,
        [
            pltpu.HBM((channels, width), f32), pltpu.HBM((nstate, width), f32), pltpu.HBM((1, channels), f32),
        ],
        [
            pltpu.VMEM((2, channels, PIECE), f32), pltpu.VMEM((2, nstate, PIECE), f32),
            pltpu.VMEM((2, 1, channels // pieces), f32), pltpu.SemaphoreType.DMA((2, 3)),
        ],
        8, 1e6, 2e6, {3 + k: k for k in range(len(done))},
    )(me, held(mine), held(came), *[pltpu.with_memory_space_constraint(x, pltpu.HBM) for x in done])


def swap(x, distance, count):
    return lax.ppermute(x, "seq", [(i, i ^ distance) for i in range(count)])


def narrow(x):
    return lax.reduce_precision(x, 8, 7)


def pick(bit, when_one, when_zero):
    return jnp.where(bit == 1, when_one, when_zero)


def tied(x, token):
    return lax.optimization_barrier((x, token))


def bit_of(me, level):
    return (me >> level) & 1


def shard_start(me, level, sensors):
    return sum(bit_of(me, k) * (sensors >> (k + 1)) for k in range(level + 1))


def row(ref, k):
    return ref[pl.ds(k, 1), :]


EACH = 2


def widened(came, k, nstate):
    return came[k * nstate : (k + 1) * nstate, :].astype(f32)


def tails_of(came, nstate):
    return came[EACH * nstate :, :].astype(f32)


def core_kernel(me_ref, own, tail, came, low_ref, low_tail_ref, tail_ref, kept_ref, *refs):
    send_refs, other_tail = refs[:-1], refs[-1]
    me = me_ref[0]
    bit = bit_of(me, 0)
    size, nstate, width = own.shape
    sensors = tail.shape[0]
    start = shard_start(me, 0, sensors)
    other_tail[...] = came[size * nstate :, :].astype(f32)
    low_tail_ref[...] = pick(bit, other_tail[...], tail[...])
    total_tail = tail[...] + other_tail[...]
    tail_ref[...] = total_tail
    for n in range(1 + len(send_refs)):
        for k in range(EACH):
            sensor = block_start(me, 2 * n, sensors) + k
            j = sensor - start
            other = came[pl.ds(pl.multiple_of(j * nstate, nstate), nstate), :].astype(f32)
            low, high = pick(bit, other, own[j]), pick(bit, own[j], other)
            low_ref[j] = low
            total = low * jnp.exp2(pick(bit, row(tail, sensor), row(other_tail, sensor))) + high
            if n == 0:
                kept_ref[k] = total
            else:
                send_refs[n - 1][k * nstate : (k + 1) * nstate, :] = total.astype(bf16)
    for ref in send_refs:
        ref[EACH * nstate :, :] = total_tail.astype(bf16)


def join_cores(me, own, tail, came):
    size, nstate, width = own.shape
    sent = pltpu.VMEM((EACH * nstate + tail.shape[0], width), bf16)
    return call(
        core_kernel, "cores", 1, (), [HELD] * 3, [HELD] * 7,
        [
            pltpu.VMEM(own.shape, f32), pltpu.VMEM(tail.shape, f32), pltpu.VMEM(tail.shape, f32),
            pltpu.VMEM((EACH, nstate, width), f32), sent, sent, sent,
        ],
        [pltpu.VMEM(tail.shape, f32)], 6, 1e6, 1e6,
    )(me, *[held(x) for x in (own, tail, came)])


def chip_of(me):
    return (me >> 1) & 3


def group_kernel(me_ref, own, tail, *refs):
    cames, (first_ref, pair_ref, third_ref, first_tail, pair_tail, third_tail, send_ref, tail_sc) = refs[:3], refs[3:]
    me = me_ref[0]
    nstate = own.shape[1]
    sensors = tail.shape[0]
    chip = chip_of(me)

    def at(position, values):
        flip = chip ^ position
        return jnp.where(flip == 0, values[0], jnp.where(flip == 1, values[1], jnp.where(flip == 2, values[2], values[3])))

    tails = [tail[...]] + [tails_of(came, nstate) for came in cames]
    for position in range(4):
        tail_sc[position] = at(position, tails)
    first_tail[...] = tail_sc[0]
    pair_tail[...] = tail_sc[0] + tail_sc[1]
    third_tail[...] = tail_sc[2]
    if send_ref.shape[0] > EACH * nstate:
        send_ref[EACH * nstate :, :] = (tail_sc[0] + tail_sc[1] + tail_sc[2] + tail_sc[3]).astype(bf16)
    for k in range(EACH):
        sensor = pl.ds(block_start(me, 0, sensors) + k, 1)
        values = [own[k]] + [widened(came, k, nstate) for came in cames]
        first, second, third, fourth = [at(position, values) for position in range(4)]
        pair = first * jnp.exp2(tail_sc[1, sensor, :]) + second
        first_ref[k] = first
        pair_ref[k] = pair
        third_ref[k] = third
        both = tail_sc[2, sensor, :] + tail_sc[3, sensor, :]
        total = pair * jnp.exp2(both) + (third * jnp.exp2(tail_sc[3, sensor, :]) + fourth)
        send_ref[k * nstate : (k + 1) * nstate, :] = total.astype(bf16)


def join_group(me, own, tail, cames, with_tail):
    state, tails = pltpu.VMEM(own.shape, f32), pltpu.VMEM(tail.shape, f32)
    rows = cames[0].shape[0] - (0 if with_tail else tail.shape[0])
    return call(
        group_kernel, "group", 1, (), [HELD] * 5, [HELD] * 7,
        [state] * 3 + [tails] * 3 + [pltpu.VMEM((rows, own.shape[2]), bf16)],
        [pltpu.VMEM((4,) + tail.shape, f32)], 6, 1e6, 1e6,
    )(me, *[held(x) for x in (own, tail, *cames)])


def across_kernel(me_ref, own, before, came, next_ref, before_ref, *, level):
    me = me_ref[0]
    bit = bit_of(me, level)
    nstate = (own.shape[0] - own.shape[0] // 9) // EACH
    sensors = own.shape[0] - EACH * nstate
    rows = EACH * nstate
    for k in range(EACH):
        sensor = block_start(me, 0, sensors) + k
        here = slice(k * nstate, (k + 1) * nstate)
        other, mine, ahead = came[here, :].astype(f32), own[here, :], before[here, :]
        other_tail = came[rows:, :].astype(f32)
        mask = (iota(other_tail.shape, 0) == sensor).astype(f32)

        def of_sensor(tails):
            return jnp.sum(tails * mask, axis=0, keepdims=True)

        before_ref[here, :] = pick(bit, other * jnp.exp2(of_sensor(before[rows:, :])) + ahead, ahead)
        low, high = pick(bit, other, mine), pick(bit, mine, other)
        next_ref[here, :] = low * jnp.exp2(of_sensor(pick(bit, own[rows:, :], other_tail))) + high
    other_tail = came[rows:, :].astype(f32)
    next_ref[rows:, :] = own[rows:, :] + other_tail
    before_ref[rows:, :] = before[rows:, :] + pick(bit, other_tail, jnp.zeros_like(other_tail))


def across(me, own, before, came, level):
    out = pltpu.VMEM(own.shape, f32)
    return call(
        functools.partial(across_kernel, level=level), "across", 1, (), [HELD] * 3, [HELD] * 2, [out, out],
        [], 6, 1e6, 1e6,
    )(me, *[held(x) for x in (own, before, came)])


def landed(me, state, sensor, low, low_tail):
    start = shard_start(me, 0, low_tail.shape[0])
    after = state * jnp.exp2(row(low_tail, sensor)) + low[sensor - start]
    bit = bit_of(me, 0)
    return pick(bit, after, state).astype(bf16), pick(bit, state, after).astype(bf16)


def fall_kernel(
    me_ref, came, first, pair, third, first_tail, pair_tail, third_tail, low, low_tail,
    state_ref, core_ref, *send_refs, level,
):
    me = me_ref[0]
    nstate = first.shape[1]
    sensors = low_tail.shape[0]
    for k in range(EACH):
        sensor = block_start(me, 0, sensors) + k
        before = widened(came, k, nstate)
        if level is not None:
            before = pick(bit_of(me, level), before, jnp.zeros_like(before))
        third_start = before * jnp.exp2(row(pair_tail, sensor)) + pair[k]
        starts = [
            before,
            before * jnp.exp2(row(first_tail, sensor)) + first[k],
            third_start,
            third_start * jnp.exp2(row(third_tail, sensor)) + third[k],
        ]
        for n in range(4):
            chip = chip_of(me) ^ n
            state = jnp.where(
                chip == 0, starts[0], jnp.where(chip == 1, starts[1], jnp.where(chip == 2, starts[2], starts[3]))
            )
            if n == 0:
                state_ref[k], core_ref[k] = landed(me, state, sensor, low, low_tail)
            else:
                send_refs[n - 1][k] = state.astype(bf16)


def fall(me, came, level, group, low, low_tail):
    nstate, width = low.shape[1:]
    return call(
        functools.partial(fall_kernel, level=level), "fall", 1, (), [HELD] * 9, [HELD] * 5,
        [pltpu.VMEM((EACH, nstate, width), bf16)] * 5, [], 6, 1e6, 1e6,
    )(me, *[held(x) for x in (came, *group, low, low_tail)])


def land_kernel(me_ref, low, low_tail, *refs, blocks):
    cames, (state_ref, core_ref) = refs[: len(blocks)], refs[len(blocks) :]
    me = me_ref[0]
    for n, (flips, came) in enumerate(zip(blocks, cames)):
        for k in range(EACH):
            sensor = block_start(me, flips, low_tail.shape[0]) + k
            state_ref[n * EACH + k], core_ref[n * EACH + k] = landed(me, came[k].astype(f32), sensor, low, low_tail)


def land(me, low, low_tail, blocks, cames):
    out = pltpu.VMEM((EACH * len(blocks),) + low.shape[1:], bf16)
    return call(
        functools.partial(land_kernel, blocks=blocks), "land", 1, (), [HELD] * (2 + len(blocks)), [HELD] * 2,
        [out, out], [], 6, 1e6, 1e6,
    )(me, *[held(x) for x in (low, low_tail, *cames)])


SHARDED = 3


def halve_kernel(me_ref, part, came, kept_ref, gone_ref, *, level):
    size = kept_ref.shape[0]
    total = part[...] + came[...].astype(f32)
    bit = bit_of(me_ref[0], level)
    low, high = total[0:size], total[size:]
    kept_ref[...] = pick(bit, high, low)
    gone_ref[...] = pick(bit, low, high).astype(bf16)


def halve(me, part, came, level):
    shape = (part.shape[0] // 2, part.shape[1])
    return call(
        functools.partial(halve_kernel, level=level), "halve", 1, (), [HELD] * 2, [HELD] * 2,
        [pltpu.VMEM(shape, f32), pltpu.VMEM(shape, bf16)], [], 6, 1e6, 1e6,
    )(me, held(part), held(came))


def join_kernel(me_ref, part, came, out_ref, *, level):
    size = part.shape[0]
    bit = bit_of(me_ref[0], level)
    own, other = part[...].astype(f32), came[...].astype(f32)
    out_ref[0:size, :] = pick(bit, other, own).astype(bf16)
    out_ref[size:, :] = pick(bit, own, other).astype(bf16)


def join(me, part, came, level):
    return call(
        functools.partial(join_kernel, level=level), "join", 1, (), [HELD] * 2, [HELD],
        [pltpu.VMEM((2 * part.shape[0], part.shape[1]), bf16)], [], 6, 1e6, 1e6,
    )(me, held(part), held(came))[0]


def all_sum(part, came, me, count, order):
    levels = count.bit_length() - 1
    for level in order:
        part, gone = halve(me, part, came, level)
        came = swap(gone, 1 << level, count)
    part = part + came.astype(f32)
    for level in range(SHARDED, levels):
        part = narrow(part)
        part = part + swap(part.astype(bf16), 1 << level, count).astype(f32)
    part = part.astype(bf16)
    for level in reversed(order):
        part = join(me, part, swap(part, 1 << level, count), level)
    return part, swap(part, 1, count)


def per_device(
    count, readings, block_graph, cluster_of, mix_weight, boundaries, w_channels, w_state, w_step,
    step_bias, channel_fading_exponent, skip_gain, norm_gain, w_out, cotangent,
):
    sensors, span, width = readings.shape
    channels = w_channels.shape[1]
    nstate = w_state.shape[1] // 2
    me = lax.axis_index("seq").astype(jnp.int32)
    at = me[None]
    heads = skip_gain.shape[0]

    mixed, chans, maps, step, cum, cum_t, weight, send, tail, token, consts = front(
        at, readings, block_graph, cluster_of, mix_weight, boundaries, w_channels, w_state, w_step,
        step_bias, channel_fading_exponent, skip_gain, norm_gain,
    )
    work = {"token": token, "within": (), "back": (), "gains": []}

    def run_back(blocks, *states):
        part, scaled, decay, grad, _, _, fades = work["within"]
        normed, read, gain, work["token"] = back(
            at, blocks, states, maps, scaled, decay, part, grad, fades, consts, work["back"], work["token"]
        )
        work["back"] = (normed, read)
        work["gains"].append(gain)

    def tie(x):
        x, work["token"] = tied(x, work["token"])
        return x

    def run_within(first, size):
        *arrays, work["token"] = within(
            first, size, chans, maps, step, cum, cum_t, consts, cotangent, w_out, heads, work["within"], work["token"]
        )
        work["within"] = tuple(arrays)

    came = swap(send, 1, count)
    keep = own_states(at, chans, maps, weight, nstate)
    came, keep = tied(came, keep)
    low, low_tail, tail, kept, *sends = join_cores(at, keep, tail, came)
    sends = tie(sends)
    cames = [swap(x, 2 * (n + 1), count) for n, x in enumerate(sends)]
    run_within(0, 10)
    cames = tie(cames)
    levels = count.bit_length() - 1
    *group, send = join_group(at, kept, tail, cames, levels > SHARDED + 1)
    if levels == SHARDED + 1:
        came, level = swap(tie(send), 1 << SHARDED, count), SHARDED
        run_within(10, sensors - 10)
        came = tie(came)
    else:
        run_within(10, sensors - 10)
        own, before, level = send.astype(f32), jnp.zeros(send.shape, f32), None
        for k in range(SHARDED, levels):
            own, before = across(at, own, before, swap(own.astype(bf16), 1 << k, count), k)
        came = before
    states, to_core, *sends = fall(at, came, level, group, low, low_tail)
    to_core, sends = tie((to_core, sends))
    core = swap(to_core, 1, count)
    from_one, from_two, from_three = [swap(x, 2 * (n + 1), count) for n, x in enumerate(sends)]
    run_back((0,), states)
    run_back((1,), core)
    cot = work["within"][4]
    early, work["token"] = early_grads(at, work["back"][0], cot, work["back"][1], mixed, work["token"])
    arrived = tie((from_two, from_one, from_three))
    states, to_core = land(at, low, low_tail, (4, 2, 6), arrived)
    core = swap(tie(to_core), 1, count)
    run_back((4, 2, 6), states)
    run_back((5, 3, 7), core)
    results = ()
    late = functools.partial(late_grads, at, work["back"][0], cot, work["back"][1], mixed, early, work["gains"])
    came = [swap(late(part, False), 1, count) for part in (0, 1)]
    sums = [all_sum(late(part, True), came[part], at, count, order) for part, order in ((0, (1, 2)), (1, (2, 1)))]
    for part in (0, 1):
        results = finish(at, *sums[part], part, channels, width, nstate, tuple(results))
    grad_out, grad_read, grad_gain = results
    return grad_out, grad_read.T, grad_gain[0]


def solution(mesh):
    in_specs = (
        P("groups", "seq", None), P("groups", None), P("groups"), P(), P(("groups", "seq")),
        P(), P(), P(), P(), P(), P(), P(), P(), P("groups", "seq", None),
    )
    out_specs = (P("groups", None), P("groups", None), P("groups"))
    return jax.shard_map(
        functools.partial(per_device, mesh.shape["seq"]),
        mesh=mesh, in_specs=in_specs, out_specs=out_specs, check_vma=False,
    )
```

```python
import functools
import math

import jax
import jax.numpy as jnp
from jax import lax
from jax.experimental import pallas as pl
from jax.experimental.pallas import tpu as pltpu
from jax.sharding import PartitionSpec as P

f32 = jnp.float32
bf16 = jnp.bfloat16
LOG2E = math.log2(math.e)
LOG_PULSE = math.log(0.7)
NT = (((1,), (1,)), ((), ()))
TN = (((0,), (0,)), ((), ()))


def dot(a, b, dims=(((1,), (0,)), ((), ()))):
    return lax.dot_general(a, b, dims, preferred_element_type=f32)


def split(x, terms):
    parts = []
    for _ in range(terms):
        part = x.astype(bf16)
        parts.append(part)
        x = x - part.astype(f32)
    return parts


def iota(shape, axis):
    return lax.broadcasted_iota(jnp.int32, shape, axis)


def spread_matrix(rows, heads, channels):
    size = channels // heads
    return (iota((rows, channels), 0) % heads == iota((rows, channels), 1) // size).astype(bf16)


def spread(values, sensor, heads, spread2):
    lane = iota(values.shape, 1)
    own = jnp.where(lane // heads == sensor, values, 0.0)
    return dot(jnp.concatenate(split(own, 2), axis=1), spread2)


def front_kernel(
    me_ref, readings_hbm, *refs, heads, chunk, n_small,
):
    hbm, refs = refs[:n_small], refs[n_small:]
    (mixed_ref, channels_ref, maps_ref, step_ref, cum_ref, cum_t_ref, weight_ref, send_ref, tail_ref, token_ref,
     consts_ref), refs = refs[:11], refs[11:]
    vmem, refs = refs[:n_small], refs[n_small:]
    readings, kmix, wms, spread2, log_sc, scaled_sc, sems = refs
    graph, cluster, mix, marks, w_step_t, bias, fading_exponent, skip_gain, norm_gain, w_state, w_channels = vmem
    sensors, span, width = readings.shape
    rows = sensors * chunk
    maps = w_state.shape[1]
    nstate = maps // 2
    channels = w_channels.shape[1]
    lanes = sensors * heads
    chunks = span // chunk

    def reading_copy(k):
        part = pl.ds(k * chunk, chunk)
        return pltpu.make_async_copy(readings_hbm.at[:, part], readings.at[:, part], sems.at[n_small + k])

    copies = [pltpu.make_async_copy(hbm[k], vmem[k], sems.at[k]) for k in range(n_small)]
    for copy in copies[:-2]:
        copy.start()
    reading_copy(0).start()
    copies[-2].start()
    reading_copy(1).start()
    copies[-1].start()
    for k in range(2, chunks):
        reading_copy(k).start()

    token_ref[...] = jnp.zeros_like(token_ref)
    wms[...] = jnp.zeros_like(wms)
    spread2[...] = spread_matrix(spread2.shape[0], heads, channels)
    for copy in copies[:-2]:
        copy.wait()
    wms[:, maps : maps + heads] = w_step_t[...].astype(f32).T.astype(bf16)
    picked = (iota((sensors, sensors), 0) == cluster[...]).astype(bf16)
    sensor_of = (iota((sensors, rows), 1) // chunk == iota((sensors, rows), 0)).astype(bf16)
    linked = dot(dot(picked, graph[...].astype(f32).astype(bf16), TN).astype(bf16), dot(picked, sensor_of).astype(bf16))
    coupling = (linked * sum(dot(part, sensor_of) for part in split(mix[...], 3))).astype(bf16).astype(f32)
    full = jnp.broadcast_to(coupling[:, None, :], (sensors, chunk, rows)).reshape(rows, rows)
    same = iota((rows, rows), 0) % chunk == iota((rows, rows), 1) % chunk
    kmix[...] = jnp.where(same, full, 0.0).astype(bf16)
    tiled = (iota((heads, lanes), 1) % heads == iota((heads, lanes), 0)).astype(bf16)
    both = jnp.concatenate([bias[...], -jnp.exp(fading_exponent[...]) * LOG2E], axis=0)
    wide = sum(dot(part, tiled) for part in split(both, 3))
    bias_row, rate_row = wide[0:1], wide[1:2]
    consts_ref[...] = jnp.zeros_like(consts_ref)
    consts_ref[0:1, :] = sum(dot(part, spread2[0:heads, :]) for part in split(skip_gain[...], 3))
    consts_ref[1:2, :] = norm_gain[...]

    def mix_chunk(i):
        here = slice(i * chunk, (i + 1) * chunk)
        reading_copy(i).wait()
        x = readings[:, here, :].reshape(rows, width)
        mixed_ref[:, here, :] = (x.astype(f32) + dot(kmix[...], x)).astype(bf16).reshape(sensors, chunk, width)

    mix_chunk(0)
    copies[-2].wait()
    wms[:, 0:maps] = w_state[...]
    for i in range(chunks):
        here = slice(i * chunk, (i + 1) * chunk)
        if i + 1 < chunks:
            mix_chunk(i + 1)
        mixed = mixed_ref[:, here, :].reshape(rows, width)
        small = dot(mixed, wms[...])
        if i == 0:
            copies[-1].wait()
        channels_ref[:, here, :] = dot(mixed, w_channels[...]).astype(bf16).reshape(sensors, chunk, channels)
        maps_ref[:, here, :] = small[:, 0:maps].astype(bf16).reshape(sensors, chunk, maps)
        steps = small[:, maps:].reshape(sensors, chunk, lanes)
        packed = steps[0]
        for s in range(1, sensors):
            packed = packed + pltpu.roll(steps[s], heads * s, 1)
        raw = (packed + bias_row).astype(bf16).astype(f32)
        step = jnp.maximum(raw, 0.0) + jnp.log1p(jnp.exp(-jnp.abs(raw)))
        step_ref[here, :] = step
        log_sc[here, :] = rate_row * step

    at, to = iota((span, span), 0), iota((span, span), 1)
    marked = jnp.sum(jnp.where(at == to, marks[...].astype(f32), 0.0), axis=1, keepdims=True)
    log_decay = log_sc[...] + (LOG_PULSE * LOG2E) * marked
    lower = (at >= to).astype(bf16)
    cum = sum(dot(lower, part) for part in split(log_decay, 3))
    cum_ref[...] = cum
    cum_t_ref[...] = cum.T
    last = cum[span - 1 : span, :]
    weight = jnp.exp2(last - cum) * step_ref[...]
    weight_ref[...] = weight

    half = sensors // 2
    mine = (me_ref[0] & 1) * half

    def scale(n):
        s = half - mine + n
        scaled_sc[n % 4] = (channels_ref[s].astype(f32) * spread(weight, s, heads, spread2[...])).astype(bf16)

    own = jnp.where(iota((sensors, lanes), 1) // heads == iota((sensors, lanes), 0), last, 0.0)
    tail = sum(dot(part, spread2[0:lanes, :]) for part in split(own, 3))
    tail_ref[...] = tail
    send_ref[half * nstate :, :] = tail.astype(bf16)
    scale(0)
    scale(1)
    for n in range(half):
        if n + 2 < half:
            scale(n + 2)
        state = dot(maps_ref[half - mine + n], scaled_sc[n % 4], TN)[0:nstate]
        send_ref[n * nstate : (n + 1) * nstate, :] = state.astype(bf16)


def own_kernel(me_ref, channels, maps, weight, keep_ref, spread2, scaled_sc, *, heads):
    half, nstate, width = keep_ref.shape
    mine = (me_ref[0] & 1) * half
    spread2[...] = spread_matrix(spread2.shape[0], heads, width)

    def scale(n):
        scaled_sc[n % 4] = (
            channels[mine + n].astype(f32) * spread(weight[...], mine + n, heads, spread2[...])
        ).astype(bf16)

    scale(0)
    scale(1)
    for n in range(half):
        if n + 2 < half:
            scale(n + 2)
        keep_ref[n] = dot(maps[mine + n], scaled_sc[n % 4], TN)[0:nstate]


def pair_blocks(x, size):
    lane = iota(x.shape, 1)
    zero = jnp.zeros_like(x)
    return jnp.concatenate([jnp.where(lane < size, x, zero), jnp.where(lane >= size, x, zero)], axis=0)


def within_kernel(channels, maps, step, cum, cum_t, consts, cot_hbm, w_out_hbm, *refs, heads, first, count, aliases):
    part_ref, scaled_ref, decay_ref, grad_ref, cot_ref, w_out_ref, fade_ref, _, spread2, fade_sc, sems = refs[aliases:]
    _, span, width = channels.shape
    nstate = maps.shape[2] // 2
    size = width // heads
    own = slice(first, first + count)
    cot_copy = pltpu.make_async_copy(cot_hbm.at[own], cot_ref.at[own], sems.at[0])
    if first == 0:
        w_out_copy = pltpu.make_async_copy(w_out_hbm, w_out_ref, sems.at[1])
        w_out_copy.start()
    cot_copy.start()
    spread2[...] = spread_matrix(spread2.shape[0], heads, width)
    fade_sc[...] = jnp.exp2(cum[...])

    def sensor(k, carry):
        s = first + k
        causal = iota((span, span), 0) >= iota((span, span), 1)
        chan = channels[s].astype(f32)
        scaled = (chan * spread(step[...], s, heads, spread2[...])).astype(bf16)
        scaled_ref[s] = scaled
        fade_ref[s] = spread(fade_sc[...], s, heads, spread2[...])
        both = maps[s]
        scores = dot(both[:, nstate:], both[:, 0:nstate], NT)
        row = cum_t[pl.ds(pl.multiple_of(s * heads, heads), heads), :]
        col = row.T
        for pair in range(heads // 2):
            weighted = []
            for h in (2 * pair, 2 * pair + 1):
                gap = jnp.broadcast_to(col[:, h : h + 1], (span, span)) - row[h : h + 1, :]
                decay = jnp.exp2(jnp.where(causal, gap, -jnp.inf))
                decay_ref[s, h] = decay.astype(bf16)
                weighted.append((scores * decay).astype(bf16))
            lanes = slice(2 * pair * size, 2 * (pair + 1) * size)
            out = dot(jnp.concatenate(weighted, axis=1), pair_blocks(scaled[:, lanes], size))
            part_ref[s, :, lanes] = out + consts[0:1, lanes] * chan[:, lanes]
        return carry

    lax.fori_loop(0, count, sensor, 0, unroll=2)
    if first == 0:
        w_out_copy.wait()
    cot_copy.wait()
    grad = dot(cot_ref[own].reshape(count * span, cot_ref.shape[2]), w_out_ref[...], NT)
    grad_ref[own] = grad.reshape(count, span, width)


def block_start(me, flips, sensors):
    return shard_start(me ^ flips, 2, sensors)


def back_kernel(me_ref, *refs, heads, blocks, aliases):
    states, refs = refs[0], refs[1:]
    maps, scaled, decay, part, grad, fades, consts = refs[:7]
    normed_ref, read_ref, gain_ref, _, carried_sc, back_sc, faded_sc = refs[7 + aliases :]
    sensors, span, width = part.shape
    nstate = maps.shape[2] // 2
    size = width // heads
    each = states.shape[0] // len(blocks)
    chunk = 32
    todo = [
        (block_start(me_ref[0], flips, sensors) + k, states, n * each + k)
        for n, flips in enumerate(blocks)
        for k in range(each)
    ]

    def carry_in(slot):
        s, state, k = todo[slot]
        carried_sc[slot] = dot(maps[s][:, nstate:], state[k])

    def normalize(slot, gain_sum):
        s = todo[slot][0]
        gain = consts[1:2, :]
        for c in range(0, span, chunk):
            rows = slice(c, c + chunk)
            fade = fades[s, rows, :]
            out = part[s, rows, :] + carried_sc[slot, rows, :] * fade
            inv = lax.rsqrt(jnp.mean(out * out, axis=-1, keepdims=True) + 1e-05)
            normed = out * inv
            normed_ref[s, rows, :] = (normed * gain).astype(bf16)
            g = grad[s, rows, :]
            gain_sum = gain_sum + jnp.sum((normed * g).reshape(chunk // 8, 8, width), axis=0)
            by_gain = g * gain
            mean = jnp.mean(by_gain * normed, axis=-1, keepdims=True)
            back = inv * (by_gain - normed * mean)
            back_sc[slot, rows, :] = back.astype(bf16)
            faded_sc[slot, rows, :] = (back * fade).astype(bf16)
        return gain_sum

    def read_out(slot):
        s, state, k = todo[slot]
        read = dot(faded_sc[slot], state[k], NT)
        pairs = jnp.zeros((span, span), f32)
        for pair in range(heads // 2):
            lanes = slice(2 * pair * size, 2 * (pair + 1) * size)
            both_heads = dot(back_sc[slot, :, lanes], pair_blocks(scaled[s, :, lanes], size), NT)
            pairs = pairs + both_heads[:, 0:span] * decay[s, 2 * pair].astype(f32)
            pairs = pairs + both_heads[:, span:] * decay[s, 2 * pair + 1].astype(f32)
        read_ref[s] = (read + dot(pairs.astype(bf16), maps[s][:, 0:nstate])).astype(bf16)

    gain_sum = jnp.zeros(gain_ref.shape, f32)
    for slot in range(len(todo)):
        carry_in(slot)
    gain_sum = normalize(0, gain_sum)
    for slot in range(len(todo)):
        if slot + 1 < len(todo):
            gain_sum = normalize(slot + 1, gain_sum)
        read_out(slot)
    gain_ref[...] = gain_sum


PIECE = 256


def grad_piece(normed, cot, read, mixed, blocks, piece):
    span, channels = normed.shape[1:]
    lanes = slice(piece * PIECE, (piece + 1) * PIECE)

    def product(left, right, start, size):
        here = pl.ds(start, size)
        rows = size * span
        return dot(left[here].reshape(rows, left.shape[2]), right[here, :, lanes].reshape(rows, PIECE), TN)

    return (
        sum(product(normed, cot, *block) for block in blocks),
        sum(product(read, mixed, *block) for block in blocks),
    )


def early_blocks(me, sensors):
    return [(block_start(me, flips, sensors), 2) for flips in (0, 1)]


def late_blocks(me, sensors):
    size = sensors // 4
    for other in (0, 1):
        yield block_start(me, 4 ^ other, sensors), 2
        yield shard_start(me ^ 2 ^ other, 1, sensors), size


def early_kernel(me_ref, normed, cot, read, mixed, _, total, __):
    channels, nstate = normed.shape[2], read.shape[2]
    for piece in range(total.shape[0]):
        out, into = grad_piece(normed, cot, read, mixed, early_blocks(me_ref[0], normed.shape[0]), piece)
        total[piece, 0:channels, :] = out
        total[piece, channels : channels + nstate, :] = into


def late_kernel(me_ref, normed, cot, read, mixed, before, *refs, part, kept):
    *gains, out_ref = refs
    channels, nstate = normed.shape[2], read.shape[2]
    pieces = before.shape[0]
    own = channels // pieces
    bit = me_ref[0] & 1
    blocks = list(late_blocks(me_ref[0], normed.shape[0]))
    gain = sum(jnp.sum(ref[...], axis=0, keepdims=True) for ref in gains)
    at = channels + nstate

    def write(half):
        piece = half * (pieces // 2) + part
        out, into = grad_piece(normed, cot, read, mixed, blocks, piece)
        out_ref[0:channels, :] = (out + before[piece, 0:channels, :]).astype(out_ref.dtype)
        out_ref[channels:at, :] = (into + before[piece, channels:at, :]).astype(out_ref.dtype)
        row_of = iota((out_ref.shape[0] - at, PIECE), 0)
        lane = iota((out_ref.shape[0] - at, PIECE), 1)
        values = jnp.concatenate([gain[:, piece * own : (piece + 1) * own]] * (PIECE // own), axis=1)
        rest = jnp.where((row_of == 0) & (lane < own), values, 0.0)
        out_ref[at:, :] = rest.astype(out_ref.dtype)

    for half in range(2):
        pl.when(bit == (half if kept else 1 - half))(functools.partial(write, half))


def finish_kernel(me_ref, mine, came, *refs, part, aliases):
    out_hbm, read_hbm, gain_hbm, out_sc, read_sc, gain_sc, sems = refs[aliases:]
    nstate = read_hbm.shape[0]
    channels, width = out_hbm.shape
    pieces = width // PIECE
    own = channels // pieces

    def write(halves):
        copies = []
        for half, rows in enumerate(halves):
            piece = half * (pieces // 2) + part
            out_sc[half] = rows[0:channels, :].astype(f32)
            read_sc[half] = rows[channels : channels + nstate, :].astype(f32)
            gain_sc[half] = rows[channels + nstate : channels + nstate + 1, 0:own].astype(f32)
            lanes = pl.ds(piece * PIECE, PIECE)
            copies += [
                pltpu.make_async_copy(out_sc.at[half], out_hbm.at[:, lanes], sems.at[half, 0]),
                pltpu.make_async_copy(read_sc.at[half], read_hbm.at[:, lanes], sems.at[half, 1]),
                pltpu.make_async_copy(gain_sc.at[half], gain_hbm.at[:, pl.ds(piece * own, own)], sems.at[half, 2]),
            ]
            for copy in copies[-3:]:
                copy.start()
        for copy in copies:
            copy.wait()

    pl.when(me_ref[0] & 1 == 0)(lambda: write((mine, came)))
    pl.when(me_ref[0] & 1 == 1)(lambda: write((came, mine)))


def whole(shape):
    return pl.BlockSpec(shape, lambda *_: (0,) * len(shape), pipeline_mode=pl.Buffered(1))


ANYWHERE = pl.BlockSpec(memory_space=pl.ANY)
HELD = pl.BlockSpec(memory_space=pltpu.VMEM)


def held(x):
    return pltpu.with_memory_space_constraint(x, pltpu.VMEM)


def call(body, name, scalars, grid, in_specs, out_specs, out_shape, scratch, vmem, flops, moved, aliases=None):
    return pl.pallas_call(
        body,
        name=name,
        grid_spec=pltpu.PrefetchScalarGridSpec(
            num_scalar_prefetch=scalars, grid=grid, in_specs=in_specs, out_specs=out_specs, scratch_shapes=scratch
        ),
        out_shape=out_shape,
        input_output_aliases=aliases or {},
        compiler_params=pltpu.CompilerParams(vmem_limit_bytes=vmem << 20),
        cost_estimate=pl.CostEstimate(flops=int(flops), bytes_accessed=int(moved), transcendentals=0),
    )


def front(me, readings, graph, cluster, mix, boundaries, w_channels, w_state, w_step, bias, fading_exponent, skip_gain, gain):
    sensors, span, width = readings.shape
    heads, channels, maps = w_step.shape[1], w_channels.shape[1], w_state.shape[1]
    nstate, lanes, chunk = maps // 2, sensors * heads, 16
    rows, half_rows = sensors * chunk, sensors // 2 * nstate
    small = [
        graph, cluster[None, :], mix, boundaries[None, :], w_step.T, bias[None, :], fading_exponent[None, :],
        skip_gain[None, :], gain[None, :], w_state, w_channels,
    ]
    outs = [
        ((sensors, span, width), bf16), ((sensors, span, channels), bf16), ((sensors, span, maps), bf16),
        ((span, lanes), f32), ((span, lanes), f32), ((lanes, span), f32),
        ((span, lanes), f32), ((half_rows + sensors, channels), bf16), ((sensors, channels), f32),
        ((8, 128), f32), ((8, channels), f32),
    ]
    return call(
        functools.partial(front_kernel, heads=heads, chunk=chunk, n_small=len(small)), "front", 1, (),
        [ANYWHERE] * (1 + len(small)),
        [HELD] * len(outs),
        [pltpu.VMEM(shape, dtype) for shape, dtype in outs],
        [pltpu.VMEM(x.shape, x.dtype) for x in small] + [
            pltpu.VMEM(readings.shape, bf16), pltpu.VMEM((rows, rows), bf16), pltpu.VMEM((width, maps + lanes), bf16),
            pltpu.VMEM((2 * lanes, channels), bf16),
            pltpu.VMEM((span, lanes), f32), pltpu.VMEM((4, span, channels), bf16),
            pltpu.SemaphoreType.DMA((len(small) + span // chunk,)),
        ],
        20, 5e9, 14e6,
    )(me, *[pltpu.with_memory_space_constraint(x, pltpu.HBM) for x in [readings] + small])


def own_states(me, channels, maps, weight, nstate):
    sensors, span, width = channels.shape
    lanes = weight.shape[1]
    return call(
        functools.partial(own_kernel, heads=lanes // sensors), "own", 1, (), [HELD] * 3, [HELD],
        [pltpu.VMEM((sensors // 2, nstate, width), f32)],
        [pltpu.VMEM((2 * lanes, width), bf16), pltpu.VMEM((4, span, width), bf16)], 8, 3e8, 2e6,
    )(me, *[held(x) for x in (channels, maps, weight)])[0]


def within(first, count, channels, maps, step, cum, cum_t, consts, cot, w_out, heads, done, token):
    sensors, span, width = channels.shape
    lanes = sensors * heads
    n_in = 8
    aliases = {n_in + k: k for k in range(len(done))}
    aliases[n_in + len(done)] = 7
    return call(
        functools.partial(within_kernel, heads=heads, first=first, count=count, aliases=len(done) + 1),
        "within", 0, (),
        [HELD] * 6 + [ANYWHERE] * 2 + [HELD] * len(done) + [ANYWHERE],
        [HELD] * 7 + [ANYWHERE],
        [
            pltpu.VMEM((sensors, span, width), f32), pltpu.VMEM((sensors, span, width), bf16),
            pltpu.VMEM((sensors, heads, span, span), bf16), pltpu.VMEM((sensors, span, width), f32),
            pltpu.VMEM(cot.shape, bf16), pltpu.VMEM(w_out.shape, bf16), pltpu.VMEM((sensors, span, width), f32),
            jax.ShapeDtypeStruct(token.shape, token.dtype),
        ],
        [pltpu.VMEM((2 * lanes, width), bf16), pltpu.VMEM((span, lanes), f32), pltpu.SemaphoreType.DMA((2,))],
        8, 3e8 * count, 1.5e6 * count, aliases,
    )(
        *[held(x) for x in (channels, maps, step, cum, cum_t, consts)],
        *[pltpu.with_memory_space_constraint(x, pltpu.HBM) for x in (cot, w_out)], *[held(x) for x in done], token,
    )


def back(me, blocks, states, maps, scaled, decay, part, grad, fades, consts, done, token):
    sensors, span, width = part.shape
    heads = decay.shape[1]
    at_once = sum(state.shape[0] for state in states)
    n_in = 8 + len(states)
    aliases = {n_in + k: k for k in range(len(done))}
    aliases[n_in + len(done)] = 3
    return call(
        functools.partial(back_kernel, heads=heads, blocks=blocks, aliases=len(done) + 1), "back", 1, (),
        [HELD] * (n_in - 1 + len(done)) + [ANYWHERE],
        [HELD] * 3 + [ANYWHERE],
        [
            pltpu.VMEM((sensors, span, width), bf16), pltpu.VMEM((sensors, span, maps.shape[2] // 2), bf16),
            pltpu.VMEM((8, width), f32), jax.ShapeDtypeStruct(token.shape, token.dtype),
        ],
        [
            pltpu.VMEM((at_once, span, width), f32),
            pltpu.VMEM((at_once, span, width), bf16), pltpu.VMEM((at_once, span, width), bf16),
        ],
        8, 3e8 * at_once, 1.5e6 * at_once, aliases,
    )(me, *[held(x) for x in (*states, maps, scaled, decay, part, grad, fades, consts) + done], token)


def grad_rows(channels, nstate):
    return -(-(channels + nstate + 1) // 32) * 32


def early_grads(me, normed, cot, read, mixed, token):
    rows = grad_rows(normed.shape[2], read.shape[2])
    return call(
        early_kernel, "early", 1, (), [HELD] * 4 + [ANYWHERE], [HELD, ANYWHERE],
        [pltpu.VMEM((cot.shape[2] // PIECE, rows, PIECE), f32), jax.ShapeDtypeStruct(token.shape, token.dtype)],
        [], 8, 6e8, 4e6, {5: 1},
    )(me, *[held(x) for x in (normed, cot, read, mixed)], token)


def late_grads(me, normed, cot, read, mixed, before, gains, part, kept):
    rows = before.shape[1]
    return call(
        functools.partial(late_kernel, part=part, kept=kept), "late", 1, (), [HELD] * (5 + len(gains)), [HELD],
        [pltpu.VMEM((rows, PIECE), f32 if kept else bf16)], [], 10, 4e8, 3e6,
    )(me, *[held(x) for x in (normed, cot, read, mixed, before, *gains)])[0]


def finish(me, mine, came, part, channels, width, nstate, done):
    pieces = width // PIECE
    return call(
        functools.partial(finish_kernel, part=part, aliases=len(done)), "finish", 1, (),
        [HELD] * 2 + [ANYWHERE] * len(done), [ANYWHERE] * 3,
        [
            pltpu.HBM((channels, width), f32), pltpu.HBM((nstate, width), f32), pltpu.HBM((1, channels), f32),
        ],
        [
            pltpu.VMEM((2, channels, PIECE), f32), pltpu.VMEM((2, nstate, PIECE), f32),
            pltpu.VMEM((2, 1, channels // pieces), f32), pltpu.SemaphoreType.DMA((2, 3)),
        ],
        8, 1e6, 2e6, {3 + k: k for k in range(len(done))},
    )(me, held(mine), held(came), *[pltpu.with_memory_space_constraint(x, pltpu.HBM) for x in done])


def swap(x, distance, count):
    return lax.ppermute(x, "seq", [(i, i ^ distance) for i in range(count)])


def narrow(x):
    return lax.reduce_precision(x, 8, 7)


def pick(bit, when_one, when_zero):
    return jnp.where(bit == 1, when_one, when_zero)


def tied(x, token):
    return lax.optimization_barrier((x, token))


def bit_of(me, level):
    return (me >> level) & 1


def shard_start(me, level, sensors):
    return sum(bit_of(me, k) * (sensors >> (k + 1)) for k in range(level + 1))


def row(ref, k):
    return ref[pl.ds(k, 1), :]


EACH = 2


def widened(came, k, nstate):
    return came[k * nstate : (k + 1) * nstate, :].astype(f32)


def tails_of(came, nstate):
    return came[EACH * nstate :, :].astype(f32)


def core_kernel(me_ref, own, tail, came, low_ref, low_tail_ref, tail_ref, kept_ref, *refs):
    send_refs, other_tail = refs[:-1], refs[-1]
    me = me_ref[0]
    bit = bit_of(me, 0)
    size, nstate, width = own.shape
    sensors = tail.shape[0]
    start = shard_start(me, 0, sensors)
    other_tail[...] = came[size * nstate :, :].astype(f32)
    low_tail_ref[...] = pick(bit, other_tail[...], tail[...])
    total_tail = tail[...] + other_tail[...]
    tail_ref[...] = total_tail
    for n in range(1 + len(send_refs)):
        for k in range(EACH):
            sensor = block_start(me, 2 * n, sensors) + k
            j = sensor - start
            other = came[pl.ds(pl.multiple_of(j * nstate, nstate), nstate), :].astype(f32)
            low, high = pick(bit, other, own[j]), pick(bit, own[j], other)
            low_ref[j] = low
            total = low * jnp.exp2(pick(bit, row(tail, sensor), row(other_tail, sensor))) + high
            if n == 0:
                kept_ref[k] = total
            else:
                send_refs[n - 1][k * nstate : (k + 1) * nstate, :] = total.astype(bf16)
    for ref in send_refs:
        ref[EACH * nstate :, :] = total_tail.astype(bf16)


def join_cores(me, own, tail, came):
    size, nstate, width = own.shape
    sent = pltpu.VMEM((EACH * nstate + tail.shape[0], width), bf16)
    return call(
        core_kernel, "cores", 1, (), [HELD] * 3, [HELD] * 7,
        [
            pltpu.VMEM(own.shape, f32), pltpu.VMEM(tail.shape, f32), pltpu.VMEM(tail.shape, f32),
            pltpu.VMEM((EACH, nstate, width), f32), sent, sent, sent,
        ],
        [pltpu.VMEM(tail.shape, f32)], 6, 1e6, 1e6,
    )(me, *[held(x) for x in (own, tail, came)])


def chip_of(me):
    return (me >> 1) & 3


def group_kernel(me_ref, own, tail, *refs):
    cames, (first_ref, pair_ref, third_ref, first_tail, pair_tail, third_tail, send_ref, tail_sc) = refs[:3], refs[3:]
    me = me_ref[0]
    nstate = own.shape[1]
    sensors = tail.shape[0]
    chip = chip_of(me)

    def at(position, values):
        flip = chip ^ position
        return jnp.where(flip == 0, values[0], jnp.where(flip == 1, values[1], jnp.where(flip == 2, values[2], values[3])))

    tails = [tail[...]] + [tails_of(came, nstate) for came in cames]
    for position in range(4):
        tail_sc[position] = at(position, tails)
    first_tail[...] = tail_sc[0]
    pair_tail[...] = tail_sc[0] + tail_sc[1]
    third_tail[...] = tail_sc[2]
    if send_ref.shape[0] > EACH * nstate:
        send_ref[EACH * nstate :, :] = (tail_sc[0] + tail_sc[1] + tail_sc[2] + tail_sc[3]).astype(bf16)
    for k in range(EACH):
        sensor = pl.ds(block_start(me, 0, sensors) + k, 1)
        values = [own[k]] + [widened(came, k, nstate) for came in cames]
        first, second, third, fourth = [at(position, values) for position in range(4)]
        pair = first * jnp.exp2(tail_sc[1, sensor, :]) + second
        first_ref[k] = first
        pair_ref[k] = pair
        third_ref[k] = third
        both = tail_sc[2, sensor, :] + tail_sc[3, sensor, :]
        total = pair * jnp.exp2(both) + (third * jnp.exp2(tail_sc[3, sensor, :]) + fourth)
        send_ref[k * nstate : (k + 1) * nstate, :] = total.astype(bf16)


def join_group(me, own, tail, cames, with_tail):
    state, tails = pltpu.VMEM(own.shape, f32), pltpu.VMEM(tail.shape, f32)
    rows = cames[0].shape[0] - (0 if with_tail else tail.shape[0])
    return call(
        group_kernel, "group", 1, (), [HELD] * 5, [HELD] * 7,
        [state] * 3 + [tails] * 3 + [pltpu.VMEM((rows, own.shape[2]), bf16)],
        [pltpu.VMEM((4,) + tail.shape, f32)], 6, 1e6, 1e6,
    )(me, *[held(x) for x in (own, tail, *cames)])


def across_kernel(me_ref, own, before, came, next_ref, before_ref, *, level):
    me = me_ref[0]
    bit = bit_of(me, level)
    nstate = (own.shape[0] - own.shape[0] // 9) // EACH
    sensors = own.shape[0] - EACH * nstate
    rows = EACH * nstate
    for k in range(EACH):
        sensor = block_start(me, 0, sensors) + k
        here = slice(k * nstate, (k + 1) * nstate)
        other, mine, ahead = came[here, :].astype(f32), own[here, :], before[here, :]
        other_tail = came[rows:, :].astype(f32)
        mask = (iota(other_tail.shape, 0) == sensor).astype(f32)

        def of_sensor(tails):
            return jnp.sum(tails * mask, axis=0, keepdims=True)

        before_ref[here, :] = pick(bit, other * jnp.exp2(of_sensor(before[rows:, :])) + ahead, ahead)
        low, high = pick(bit, other, mine), pick(bit, mine, other)
        next_ref[here, :] = low * jnp.exp2(of_sensor(pick(bit, own[rows:, :], other_tail))) + high
    other_tail = came[rows:, :].astype(f32)
    next_ref[rows:, :] = own[rows:, :] + other_tail
    before_ref[rows:, :] = before[rows:, :] + pick(bit, other_tail, jnp.zeros_like(other_tail))


def across(me, own, before, came, level):
    out = pltpu.VMEM(own.shape, f32)
    return call(
        functools.partial(across_kernel, level=level), "across", 1, (), [HELD] * 3, [HELD] * 2, [out, out],
        [], 6, 1e6, 1e6,
    )(me, *[held(x) for x in (own, before, came)])


def landed(me, state, sensor, low, low_tail):
    start = shard_start(me, 0, low_tail.shape[0])
    after = state * jnp.exp2(row(low_tail, sensor)) + low[sensor - start]
    bit = bit_of(me, 0)
    return pick(bit, after, state).astype(bf16), pick(bit, state, after).astype(bf16)


def fall_kernel(
    me_ref, came, first, pair, third, first_tail, pair_tail, third_tail, low, low_tail,
    state_ref, core_ref, *send_refs, level,
):
    me = me_ref[0]
    nstate = first.shape[1]
    sensors = low_tail.shape[0]
    for k in range(EACH):
        sensor = block_start(me, 0, sensors) + k
        before = widened(came, k, nstate)
        if level is not None:
            before = pick(bit_of(me, level), before, jnp.zeros_like(before))
        third_start = before * jnp.exp2(row(pair_tail, sensor)) + pair[k]
        starts = [
            before,
            before * jnp.exp2(row(first_tail, sensor)) + first[k],
            third_start,
            third_start * jnp.exp2(row(third_tail, sensor)) + third[k],
        ]
        for n in range(4):
            chip = chip_of(me) ^ n
            state = jnp.where(
                chip == 0, starts[0], jnp.where(chip == 1, starts[1], jnp.where(chip == 2, starts[2], starts[3]))
            )
            if n == 0:
                state_ref[k], core_ref[k] = landed(me, state, sensor, low, low_tail)
            else:
                send_refs[n - 1][k] = state.astype(bf16)


def fall(me, came, level, group, low, low_tail):
    nstate, width = low.shape[1:]
    return call(
        functools.partial(fall_kernel, level=level), "fall", 1, (), [HELD] * 9, [HELD] * 5,
        [pltpu.VMEM((EACH, nstate, width), bf16)] * 5, [], 6, 1e6, 1e6,
    )(me, *[held(x) for x in (came, *group, low, low_tail)])


def land_kernel(me_ref, low, low_tail, *refs, blocks):
    cames, (state_ref, core_ref) = refs[: len(blocks)], refs[len(blocks) :]
    me = me_ref[0]
    for n, (flips, came) in enumerate(zip(blocks, cames)):
        for k in range(EACH):
            sensor = block_start(me, flips, low_tail.shape[0]) + k
            state_ref[n * EACH + k], core_ref[n * EACH + k] = landed(me, came[k].astype(f32), sensor, low, low_tail)


def land(me, low, low_tail, blocks, cames):
    out = pltpu.VMEM((EACH * len(blocks),) + low.shape[1:], bf16)
    return call(
        functools.partial(land_kernel, blocks=blocks), "land", 1, (), [HELD] * (2 + len(blocks)), [HELD] * 2,
        [out, out], [], 6, 1e6, 1e6,
    )(me, *[held(x) for x in (low, low_tail, *cames)])


SHARDED = 3


def halve_kernel(me_ref, part, came, kept_ref, gone_ref, *, level):
    size = kept_ref.shape[0]
    total = part[...] + came[...].astype(f32)
    bit = bit_of(me_ref[0], level)
    low, high = total[0:size], total[size:]
    kept_ref[...] = pick(bit, high, low)
    gone_ref[...] = pick(bit, low, high).astype(bf16)


def halve(me, part, came, level):
    shape = (part.shape[0] // 2, part.shape[1])
    return call(
        functools.partial(halve_kernel, level=level), "halve", 1, (), [HELD] * 2, [HELD] * 2,
        [pltpu.VMEM(shape, f32), pltpu.VMEM(shape, bf16)], [], 6, 1e6, 1e6,
    )(me, held(part), held(came))


def join_kernel(me_ref, part, came, out_ref, *, level):
    size = part.shape[0]
    bit = bit_of(me_ref[0], level)
    own, other = part[...].astype(f32), came[...].astype(f32)
    out_ref[0:size, :] = pick(bit, other, own).astype(bf16)
    out_ref[size:, :] = pick(bit, own, other).astype(bf16)


def join(me, part, came, level):
    return call(
        functools.partial(join_kernel, level=level), "join", 1, (), [HELD] * 2, [HELD],
        [pltpu.VMEM((2 * part.shape[0], part.shape[1]), bf16)], [], 6, 1e6, 1e6,
    )(me, held(part), held(came))[0]


def all_sum(part, came, me, count, order):
    levels = count.bit_length() - 1
    for level in order:
        part, gone = halve(me, part, came, level)
        came = swap(gone, 1 << level, count)
    part = part + came.astype(f32)
    for level in range(SHARDED, levels):
        part = narrow(part)
        part = part + swap(part.astype(bf16), 1 << level, count).astype(f32)
    part = part.astype(bf16)
    for level in reversed(order):
        part = join(me, part, swap(part, 1 << level, count), level)
    return part, swap(part, 1, count)


def per_device(
    count, readings, block_graph, cluster_of, mix_weight, boundaries, w_channels, w_state, w_step,
    step_bias, channel_fading_exponent, skip_gain, norm_gain, w_out, cotangent,
):
    sensors, span, width = readings.shape
    channels = w_channels.shape[1]
    nstate = w_state.shape[1] // 2
    me = lax.axis_index("seq").astype(jnp.int32)
    at = me[None]
    heads = skip_gain.shape[0]

    mixed, chans, maps, step, cum, cum_t, weight, send, tail, token, consts = front(
        at, readings, block_graph, cluster_of, mix_weight, boundaries, w_channels, w_state, w_step,
        step_bias, channel_fading_exponent, skip_gain, norm_gain,
    )
    work = {"token": token, "within": (), "back": (), "gains": []}

    def run_back(blocks, *states):
        part, scaled, decay, grad, _, _, fades = work["within"]
        normed, read, gain, work["token"] = back(
            at, blocks, states, maps, scaled, decay, part, grad, fades, consts, work["back"], work["token"]
        )
        work["back"] = (normed, read)
        work["gains"].append(gain)

    def tie(x):
        x, work["token"] = tied(x, work["token"])
        return x

    def run_within(first, size):
        *arrays, work["token"] = within(
            first, size, chans, maps, step, cum, cum_t, consts, cotangent, w_out, heads, work["within"], work["token"]
        )
        work["within"] = tuple(arrays)

    came = swap(send, 1, count)
    keep = own_states(at, chans, maps, weight, nstate)
    came, keep = tied(came, keep)
    low, low_tail, tail, kept, *sends = join_cores(at, keep, tail, came)
    sends = tie(sends)
    cames = [swap(x, 2 * (n + 1), count) for n, x in enumerate(sends)]
    run_within(0, 10)
    cames = tie(cames)
    levels = count.bit_length() - 1
    *group, send = join_group(at, kept, tail, cames, levels > SHARDED + 1)
    if levels == SHARDED + 1:
        came, level = swap(tie(send), 1 << SHARDED, count), SHARDED
        run_within(10, sensors - 10)
        came = tie(came)
    else:
        run_within(10, sensors - 10)
        own, before, level = send.astype(f32), jnp.zeros(send.shape, f32), None
        for k in range(SHARDED, levels):
            own, before = across(at, own, before, swap(own.astype(bf16), 1 << k, count), k)
        came = before
    states, to_core, *sends = fall(at, came, level, group, low, low_tail)
    to_core, sends = tie((to_core, sends))
    core = swap(to_core, 1, count)
    from_one, from_two, from_three = [swap(x, 2 * (n + 1), count) for n, x in enumerate(sends)]
    run_back((0,), states)
    run_back((1,), core)
    cot = work["within"][4]
    early, work["token"] = early_grads(at, work["back"][0], cot, work["back"][1], mixed, work["token"])
    arrived = tie((from_two, from_one, from_three))
    states, to_core = land(at, low, low_tail, (4, 2, 6), arrived)
    core = swap(tie(to_core), 1, count)
    run_back((4, 2, 6), states)
    run_back((5, 3, 7), core)
    results = ()
    late = functools.partial(late_grads, at, work["back"][0], cot, work["back"][1], mixed, early, work["gains"])
    came = [swap(late(part, False), 1, count) for part in (0, 1)]
    sums = [all_sum(late(part, True), came[part], at, count, order) for part, order in ((0, (1, 2)), (1, (2, 1)))]
    for part in (0, 1):
        results = finish(at, *sums[part], part, channels, width, nstate, tuple(results))
    grad_out, grad_read, grad_gain = results
    return grad_out, grad_read.T, grad_gain[0]


def solution(mesh):
    in_specs = (
        P("groups", "seq", None), P("groups", None), P("groups"), P(), P(("groups", "seq")),
        P(), P(), P(), P(), P(), P(), P(), P(), P("groups", "seq", None),
    )
    out_specs = (P("groups", None), P("groups", None), P("groups"))
    return jax.shard_map(
        functools.partial(per_device, mesh.shape["seq"]),
        mesh=mesh, in_specs=in_specs, out_specs=out_specs, check_vma=False,
    )
```
